32 devices in a mesh: dp: 8 (over y, x, core), frame: 4 (over z).
Axes of the slice: x: 2, y: 2, z: 4, core: 2. Of those that a mesh axis runs over, the one named last changes fastest.
Arguments:
- queries: bfloat16 [8, 4, 128, 2048], P('dp', 'frame'), may hold values from -12 to 12
- key_states: bfloat16 [8, 4, 128, 2048], P('dp', 'frame'), may hold values from -6 to 6
- value_states: bfloat16 [8, 4, 128, 2048], P('dp', 'frame'), may hold values from -6 to 6
- head_scale: float32 [16], replicated, may hold values from 0.5 to 4
- out_weight: bfloat16 [2048, 3072], P('dp'), may hold values from -0.125 to 0.125
- frame_pattern: int32 [4, 2], replicated, may hold values from 0 to 3, as said below
- out_grad: bfloat16 [8, 4, 128, 3072], P('dp', 'frame'), may hold values from -6 to 6
Outputs:
- attended: bfloat16 [8, 4, 128, 3072], P('dp', 'frame')
- query_grad: bfloat16 [8, 4, 128, 2048], P('dp', 'frame')
- key_grad: bfloat16 [8, 4, 128, 2048], P('dp', 'frame')
- value_grad: bfloat16 [8, 4, 128, 2048], P('dp', 'frame')
- scale_grad: float32 [16], replicated
The draws below stay inside these ranges and needn't reach their ends.
Inputs may be any that keep to these rules, and one draw needn't show every extreme that they name: `frame_pattern`: row f names 2 different frames, the first of them f itself.
All inputs are finite; a program needn't handle non-finite values.
Results may differ from the reference program's by a relative error of at most 0.0058.
Values may be sent and summed in bfloat16 or wider, within the bound.
No kernel may reach another device: no remote copies, remote signals or barrier semaphores. Data moves between devices by JAX's collectives and lax.ppermute only.
A program may use at most 128 MiB of HBM per device.

```python
import math
import jax
import jax.numpy as jnp
from jax import lax

D = 3072
H = 16
HDH = 128
TOK = 128
HD = 2048
FRAMES = 4
SLOTS = 2
CLIPS = 8


def key_field(key):
    shape = (CLIPS, FRAMES, TOK, H * HDH)
    field = jnp.clip(jax.random.normal(jax.random.fold_in(key, 11), shape, jnp.float32), -6.0, 6.0)
    return field


def draw_key_states(key, part):
    return key_field(key).astype(jnp.bfloat16)


def draw_queries(key, part):
    shape = (CLIPS, FRAMES, TOK, H * HDH)
    base = jnp.clip(jax.random.normal(jax.random.fold_in(key, 12), shape, jnp.float32), -6.0, 6.0)
    return base.astype(jnp.bfloat16)


def draw_frame_pattern(key, part):
    frames = jnp.arange(FRAMES, dtype=jnp.int32)
    subkeys = jax.random.split(jax.random.fold_in(key, 21), FRAMES)
    orders = jax.vmap(lambda single: jax.random.permutation(single, FRAMES - 1))(subkeys).astype(jnp.int32)
    others = orders + (orders >= frames[:, None]).astype(jnp.int32)
    return jnp.concatenate([frames[:, None], others[:, :SLOTS - 1]], axis=1).astype(jnp.int32)


def levels(rng, dims, cuts, low, largest):
    def one(dim, shards_of):
        steps = jax.random.uniform(jax.random.fold_in(jax.random.fold_in(rng, 6), dim), (shards_of,), jnp.float32, low / len(cuts), largest / len(cuts))
        return jnp.repeat(jnp.exp(steps), dims[dim] // shards_of).reshape((-1,) + (1,) * (len(dims) - dim - 1))

    factor_of = one(*cuts[0])
    for cut in cuts[1:]:
        factor_of = factor_of * one(*cut)
    return factor_of


def centred(own_key, shape, scale, most, pieces=(), kind=jnp.bfloat16):
    result = scale * jax.random.normal(own_key, shape, jnp.float32)
    if pieces:
        result = result * levels(own_key, shape, pieces, -0.22, 0.18)
    return jnp.clip(result, -most, most).astype(kind)


def setup_inputs(seed: int = 0) -> dict:
    arg_keys = jax.random.split(jax.random.key(seed), 8)
    return {
        "queries": draw_queries(jax.random.fold_in(arg_keys[7], 71), 0),
        "key_states": draw_key_states(jax.random.fold_in(arg_keys[7], 71), 0),
        "value_states": centred(arg_keys[2], (CLIPS, FRAMES, TOK, HD), 1.0, 6.0, ((0, 8), (1, 4))),
        "head_scale": jnp.clip(jnp.exp(jax.random.uniform(arg_keys[3], (H,), jnp.float32, math.log(0.5), math.log(4.0))), 0.5, 4.0),
        "out_weight": centred(arg_keys[4], (HD, D), HD ** -0.5, 0.125, ((0, 8),)),
        "frame_pattern": draw_frame_pattern(jax.random.fold_in(arg_keys[7], 71), 0),
        "out_grad": centred(arg_keys[6], (CLIPS, FRAMES, TOK, D), 1.0, 6.0, ((0, 8), (1, 4))),
    }


def head_pass(queries, key_states, value_states, out_grad, head_scale, out_weight, frame_pattern):
    frames = queries.shape[0]
    tokens = queries.shape[1]
    inv_root = 1.0 / math.sqrt(HDH)
    factor = head_scale * inv_root
    query_heads = queries.reshape(frames, tokens, H, HDH).astype(jnp.float32)
    key_sel = key_states[frame_pattern].reshape(frames, SLOTS * tokens, H, HDH).astype(jnp.float32)
    value_sel = value_states[frame_pattern].reshape(frames, SLOTS * tokens, H, HDH).astype(jnp.float32)
    plain_scores = jnp.einsum('fthd,fkhd->fhtk', query_heads, key_sel, precision=lax.Precision.HIGHEST)
    probs = jax.nn.softmax(plain_scores * factor[None, :, None, None], axis=-1)
    probs_low = lax.optimization_barrier(probs.astype(jnp.bfloat16)).astype(jnp.float32)
    context = jnp.einsum('fhtk,fkhd->fthd', probs_low, value_sel, precision=lax.Precision.HIGHEST).astype(jnp.bfloat16)
    context_rows = context.reshape(frames * tokens, H * HDH)
    attended = jnp.dot(context_rows, out_weight, preferred_element_type=jnp.float32).astype(jnp.bfloat16)
    grad_rows = out_grad.reshape(frames * tokens, out_grad.shape[2])
    context_grad = lax.dot_general(grad_rows, out_weight, (((1,), (1,)), ((), ())), preferred_element_type=jnp.float32).astype(jnp.bfloat16)
    grad_heads = context_grad.reshape(frames, tokens, H, HDH).astype(jnp.float32)
    prob_grad = jnp.einsum('fthd,fkhd->fhtk', grad_heads, value_sel, precision=lax.Precision.HIGHEST)
    score_grad = probs * (prob_grad - lax.optimization_barrier(jnp.sum(prob_grad * probs, axis=-1, keepdims=True)))
    scale_part = lax.optimization_barrier(jnp.sum(score_grad * plain_scores, axis=(0, 2, 3))) * inv_root
    score_low = lax.optimization_barrier(score_grad.astype(jnp.bfloat16)).astype(jnp.float32)
    query_grad = jnp.einsum('fhtk,fkhd->fthd', score_low, key_sel, precision=lax.Precision.HIGHEST) * factor[None, None, :, None]
    query_grad = query_grad.astype(jnp.bfloat16).reshape(frames, tokens, H * HDH)
    key_part = jnp.einsum('fhtk,fthd->fkhd', score_low, query_heads, precision=lax.Precision.HIGHEST) * factor[None, None, :, None]
    key_part = key_part.reshape(frames, SLOTS, tokens, H * HDH)
    key_grad = jnp.zeros((frames, tokens, H * HDH), jnp.float32).at[frame_pattern].add(key_part).astype(jnp.bfloat16)
    value_part = jnp.einsum('fhtk,fthd->fkhd', probs_low, grad_heads, precision=lax.Precision.HIGHEST)
    value_part = value_part.reshape(frames, SLOTS, tokens, H * HDH)
    value_grad = jnp.zeros((frames, tokens, H * HDH), jnp.float32).at[frame_pattern].add(value_part).astype(jnp.bfloat16)
    return (attended.reshape(frames, tokens, out_weight.shape[1]), query_grad, key_grad, value_grad, scale_part)

def reference(queries, key_states, value_states, head_scale, out_weight, frame_pattern, out_grad):

    def one_clip(items):
        return head_pass(items[0], items[1], items[2], items[3], head_scale, out_weight, frame_pattern)
    results = lax.map(one_clip, (queries, key_states, value_states, out_grad))
    scale_grad = lax.optimization_barrier(jnp.sum(results[4], axis=0))
    return (results[0], results[1], results[2], results[3], scale_grad)
```

```python
import functools
import math

import jax
import jax.numpy as jnp
from jax import lax
from jax.experimental import pallas as pl
from jax.experimental.pallas import tpu as pltpu
from jax.sharding import PartitionSpec as P

HDH = 128
LANES = 128


F32 = jnp.float32
BF16 = jnp.bfloat16
NT = (((1,), (1,)), ((), ()))
NN = (((1,), (0,)), ((), ()))
TN = (((0,), (0,)), ((), ()))
SMEM = pl.BlockSpec(memory_space=pltpu.SMEM)
VMEM = pl.BlockSpec(memory_space=pltpu.VMEM)


def dot(a, b, dims):
    return lax.dot_general(a, b, dims, preferred_element_type=F32)


def lane_block(index, width):
    return pl.ds(pl.multiple_of(index * width, LANES), width)


def call(body, outs, operands, smem=0, scratch=(), name=None):
    return pl.pallas_call(
        body,
        out_shape=outs,
        in_specs=[SMEM] * smem + [VMEM] * (len(operands) - smem),
        out_specs=[VMEM] * len(outs),
        scratch_shapes=list(scratch),
        name=name,
    )(*operands)


def pack_body(frames, width, count, *refs):
    place = refs[0][0]
    sources = refs[1 : 1 + count]
    outs = refs[1 + count :]
    for s in range(frames):
        target = lax.rem(place + s, frames)
        for i in range(count):
            outs[s][i] = sources[i][:, lane_block(target, width)]


def pack(place, sources, frames):
    tokens, full = sources[0].shape
    width = full // frames
    shape = jax.ShapeDtypeStruct((len(sources), tokens, width), BF16)
    return call(
        functools.partial(pack_body, frames, width, len(sources)),
        [shape] * frames,
        [place, *sources],
        smem=1,
        name="pack",
    )


def unpack_body(frames, width, count, *refs):
    place = refs[0][0]
    blocks = refs[1 : 1 + frames]
    outs = refs[1 + frames :]
    for s in range(frames):
        source = lax.rem(place + s, frames)
        for i in range(count):
            outs[i][:, lane_block(source, width)] = blocks[s][i]


def unpack(place, blocks, frames):
    count, tokens, width = blocks[0].shape
    shape = jax.ShapeDtypeStruct((tokens, width * frames), BF16)
    return call(
        functools.partial(unpack_body, frames, width, count),
        [shape] * count,
        [place, *blocks],
        smem=1,
        name="unpack",
    )


def softmax_parts(query, keys, factor):
    plain = [dot(query, key, NT) for key in keys]
    logits = [p * factor for p in plain]
    top = functools.reduce(jnp.maximum, [jnp.max(l, axis=1, keepdims=True) for l in logits])
    raised = [jnp.exp(l - top) for l in logits]
    total = functools.reduce(jnp.add, [jnp.sum(e, axis=1, keepdims=True) for e in raised])
    inverse = 1.0 / total
    return plain, [e * inverse for e in raised]


def forward_body(frames, heads, slots, place_ref, scale_ref, pattern_ref, *refs):
    blocks = refs[:frames]
    outs = refs[frames : 2 * frames]
    held = refs[2 * frames]
    place = place_ref[0]
    inv_root = 1.0 / math.sqrt(HDH)
    for s in range(frames):
        frame = lax.rem(place + frames - s, frames)
        held[frame] = blocks[s][1:3]
    for s in range(frames):
        frame = lax.rem(place + frames - s, frames)
        chosen = [pattern_ref[frame, j] for j in range(slots)]
        for h in range(heads):
            at = slice(h * HDH, (h + 1) * HDH)
            factor = scale_ref[place * heads + h] * inv_root
            keys = [held[g, 0, :, at] for g in chosen]
            _, probs = softmax_parts(blocks[s][0, :, at], keys, factor)
            context = functools.reduce(
                jnp.add,
                [dot(p.astype(BF16), held[g, 1, :, at], NN) for p, g in zip(probs, chosen)],
            )
            outs[s][0, :, at] = context.astype(BF16)


def forward(place, scale, pattern, blocks):
    frames = len(blocks)
    _, tokens, width = blocks[0].shape
    shape = jax.ShapeDtypeStruct((1, tokens, width), BF16)
    return call(
        functools.partial(forward_body, frames, width // HDH, pattern.shape[1]),
        [shape] * frames,
        [place, scale, pattern, *blocks],
        smem=3,
        scratch=[pltpu.VMEM((frames, 2, tokens, width), BF16)],
        name="forward",
    )


def backward_body(frames, heads, slots, place_ref, scale_ref, pattern_ref, *refs):
    blocks = refs[:frames]
    grads = refs[frames : 2 * frames]
    outs = refs[2 * frames : 3 * frames]
    scale_out = refs[3 * frames]
    held, key_sum, value_sum = refs[3 * frames + 1 :]
    place = place_ref[0]
    inv_root = 1.0 / math.sqrt(HDH)
    key_sum[...] = jnp.zeros_like(key_sum)
    value_sum[...] = jnp.zeros_like(value_sum)
    for s in range(frames):
        frame = lax.rem(place + frames - s, frames)
        held[frame] = blocks[s][1:3]
    terms = [jnp.zeros((1, tokens_of(blocks)), F32) for _ in range(heads)]
    for s in range(frames):
        frame = lax.rem(place + frames - s, frames)
        chosen = [pattern_ref[frame, j] for j in range(slots)]
        for h in range(heads):
            at = slice(h * HDH, (h + 1) * HDH)
            factor = scale_ref[place * heads + h] * inv_root
            query = blocks[s][0, :, at]
            grad = grads[s][0, :, at]
            keys = [held[g, 0, :, at] for g in chosen]
            plain, probs = softmax_parts(query, keys, factor)
            prob_grads = [dot(grad, held[g, 1, :, at], NT) for g in chosen]
            weighted = functools.reduce(
                jnp.add,
                [jnp.sum(d * p, axis=1, keepdims=True) for d, p in zip(prob_grads, probs)],
            )
            score_grads = [p * (d - weighted) for d, p in zip(prob_grads, probs)]
            for sg, p in zip(score_grads, plain):
                terms[h] = terms[h] + jnp.sum(sg * p, axis=0, keepdims=True)
            low = [sg.astype(BF16) for sg in score_grads]
            query_grad = functools.reduce(
                jnp.add, [dot(sg, key, NN) for sg, key in zip(low, keys)]
            )
            outs[s][0, :, at] = (query_grad * factor).astype(BF16)
            for g, sg, p in zip(chosen, low, probs):
                key_sum[g, :, at] += dot(sg, query, TN) * factor
                value_sum[g, :, at] += dot(p.astype(BF16), grad, TN)
    for s in range(frames):
        frame = lax.rem(place + frames - s, frames)
        outs[s][1] = key_sum[frame].astype(BF16)
        outs[s][2] = value_sum[frame].astype(BF16)
    lanes = lax.broadcasted_iota(jnp.int32, scale_out.shape, 1)
    result = jnp.zeros(scale_out.shape, F32)
    for h in range(heads):
        part = jnp.sum(terms[h], axis=1, keepdims=True) * inv_root
        result = result + jnp.where(lanes == place * heads + h, part, 0.0)
    scale_out[...] = result


def tokens_of(blocks):
    return blocks[0].shape[1]


def backward(place, scale, pattern, blocks, grads):
    frames = len(blocks)
    _, tokens, width = blocks[0].shape
    shape = jax.ShapeDtypeStruct((3, tokens, width), BF16)
    result = call(
        functools.partial(backward_body, frames, width // HDH, pattern.shape[1]),
        [shape] * frames + [jax.ShapeDtypeStruct((1, LANES), F32)],
        [place, scale, pattern, *blocks, *grads],
        smem=3,
        scratch=[
            pltpu.VMEM((frames, 2, tokens, width), BF16),
            pltpu.VMEM((frames, tokens, width), F32),
            pltpu.VMEM((frames, tokens, width), F32),
        ],
        name="backward",
    )
    return result[:frames], result[frames]


def context_grad_body(count, *refs):
    mine, other = refs[:2]
    weights = refs[2 : 2 + count]
    mine_out, other_out = refs[2 + count :]
    start = 0
    for w in weights:
        at = slice(start, start + w.shape[0])
        other_out[:, at] = dot(other[...], w[...], NT).astype(BF16)
        mine_out[:, at] = dot(mine[...], w[...], NT).astype(BF16)
        start += w.shape[0]


def context_grads(mine, other, weights):
    tokens = mine.shape[0]
    features = sum(w.shape[0] for w in weights)
    shape = jax.ShapeDtypeStruct((tokens, features), BF16)
    return call(
        functools.partial(context_grad_body, len(weights)),
        [shape, shape],
        [mine, other, *weights],
        name="context_grads",
    )


def project_body(count, rows, *refs):
    weights = refs[1 : 1 + count]
    out = refs[1 + count]
    start = 0
    total = None
    for w in weights:
        part = dot(rows_of(refs[0], start, w.shape[0]), w[...], NN)
        total = part if total is None else total + part
        start += w.shape[0]
    out[...] = total.astype(out.dtype)


def rows_of(ref, start, size):
    return ref[:, start : start + size]


def project(context, weights, dtype):
    tokens, features = context.shape
    width = weights[0].shape[1]
    tile = math.gcd(width, 1024)
    return pl.pallas_call(
        functools.partial(project_body, len(weights), tokens),
        grid=(width // tile,),
        out_shape=jax.ShapeDtypeStruct((tokens, width), dtype),
        in_specs=[pl.BlockSpec((tokens, features), lambda i: (0, 0))]
        + [pl.BlockSpec((w.shape[0], tile), lambda i: (0, i)) for w in weights],
        out_specs=pl.BlockSpec((tokens, tile), lambda i: (0, i)),
        name="project",
    )(context, *weights)


def join_body(frames, pieces, size, *refs):
    place = refs[0][0]
    half = refs[1][0]
    inner = refs[1][1]
    count = len(pieces)
    mine = refs[2 : 2 + count]
    other = refs[2 + count : 2 + 2 * count]
    outs = refs[2 + 2 * count : 2 + 2 * count + frames]
    whole = refs[-1]
    group = sum(len(p) for p in pieces)
    width = whole.shape[1] // frames
    for h, sources in ((half, mine), (1 - half, other)):
        for source, names in zip(sources, pieces):
            for k, j in enumerate(names):
                spot = h * group + jnp.bitwise_xor(inner, j)
                whole[:, lane_block(spot, size)] = source[:, k * size : (k + 1) * size]
    for s in range(frames):
        outs[s][0] = whole[:, lane_block(lax.rem(place + s, frames), width)]


def join(place, where, mine, other, pieces, size, frames, full):
    tokens = mine[0].shape[0]
    if size % LANES == 0:
        shape = jax.ShapeDtypeStruct((1, tokens, full // frames), BF16)
        return call(
            functools.partial(join_body, frames, pieces, size),
            [shape] * frames,
            [place, where, *mine, *other],
            smem=2,
            scratch=[pltpu.VMEM((tokens, full), BF16)],
            name="join",
        )
    group = sum(len(p) for p in pieces)
    whole = jnp.zeros((tokens, full), BF16)
    for h, sources in ((where[0], mine), (1 - where[0], other)):
        for source, names in zip(sources, pieces):
            for k, j in enumerate(names):
                spot = h * group + jnp.bitwise_xor(where[1], j)
                piece = source[:, k * size : (k + 1) * size]
                whole = lax.dynamic_update_slice(whole, piece, (0, spot * size))
    return pack(place, [whole], frames)


def part_body(frames, count, size, *refs):
    place = refs[0][0]
    half = refs[1][0]
    inner = refs[1][1]
    blocks = refs[2 : 2 + frames]
    keep, send, whole = refs[2 + frames :]
    width = whole.shape[1] // frames
    for s in range(frames):
        whole[:, lane_block(lax.rem(place + s, frames), width)] = blocks[s][0]
    for j in range(count):
        spot = jnp.bitwise_xor(inner, j)
        at = slice(j * size, (j + 1) * size)
        keep[:, at] = whole[:, lane_block(half * count + spot, size)]
        send[:, at] = whole[:, lane_block((1 - half) * count + spot, size)]


def part(place, where, blocks, count, size):
    frames = len(blocks)
    _, tokens, width = blocks[0].shape
    if size % LANES == 0:
        shape = jax.ShapeDtypeStruct((tokens, count * size), BF16)
        return call(
            functools.partial(part_body, frames, count, size),
            [shape, shape],
            [place, where, *blocks],
            smem=2,
            scratch=[pltpu.VMEM((tokens, width * frames), BF16)],
            name="part",
        )
    whole = unpack(place, blocks, frames)[0]

    def half_of(h):
        spots = [h * count + jnp.bitwise_xor(where[1], j) for j in range(count)]
        return jnp.concatenate(
            [lax.dynamic_slice_in_dim(whole, spot * size, size, axis=1) for spot in spots], axis=1
        )

    return half_of(where[0]), half_of(1 - where[0])


def local(queries, key_states, value_states, head_scale, out_weight, frame_pattern, out_grad):
    frames = lax.axis_size("frame")
    group = lax.axis_size("dp")
    tokens, full = queries.shape[2:]
    model = out_grad.shape[3]
    heads = full // HDH
    count = group // 2
    size = out_weight.shape[0]
    place = lax.axis_index("frame").astype(jnp.int32).reshape(1)
    row = lax.axis_index("dp").astype(jnp.int32)
    where = jnp.stack([row // count, lax.rem(row, count)])

    def shift(x, s):
        return lax.ppermute(x, "frame", [(i, (i + s) % frames) for i in range(frames)])

    def swap(x, bit, axis="dp"):
        n = lax.axis_size(axis)
        return lax.ppermute(x, axis, [(i, i ^ bit) for i in range(n)])

    grad_rows = out_grad[0, 0]
    other_rows = swap(grad_rows, count)
    chunks = 2 if size % 256 == 0 else 1
    step = size // chunks
    weights = {0: [out_weight[i * step : (i + 1) * step] for i in range(chunks)]}
    bit = count // 2
    while bit:
        for j in list(weights):
            weights[j ^ bit] = [swap(c, bit) for c in weights[j]]
        bit //= 2

    sent = pack(place, [queries[0, 0], key_states[0, 0], value_states[0, 0]], frames)
    blocks = [sent[0]] + [shift(sent[s], s) for s in range(1, frames)]
    context = forward(place, head_scale, frame_pattern, blocks)
    context = [context[0]] + [shift(context[s], -s) for s in range(1, frames)]

    early = list(range(count // 2))
    late = list(range(count // 2, count))
    mine, other = [], []
    for names in (early, late):
        flat = [c for j in names for c in weights[j]]
        own, theirs = context_grads(grad_rows, other_rows, flat)
        mine.append(own)
        other.append(swap(theirs, count))
    sent = join(place, where, mine, other, (early, late), size, frames, full)
    grads = [sent[0]] + [shift(sent[s], s) for s in range(1, frames)]

    sent, scale_part = backward(place, head_scale, frame_pattern, blocks, grads)
    bit = group // 2
    while bit:
        scale_part = scale_part + swap(scale_part, bit)
        bit //= 2
    bit = frames // 2
    while bit:
        scale_part = scale_part + swap(scale_part, bit, "frame")
        bit //= 2
    blocks = [sent[0]] + [shift(sent[s], -s) for s in range(1, frames)]

    keep, send = part(place, where, context, count, size)
    flat = [c for j in range(count) for c in weights[j]]
    theirs = project(swap(send, count), flat, F32)
    own = project(keep, flat, F32)
    attended = (own + swap(theirs, count)).astype(BF16)

    query_grad, key_grad, value_grad = unpack(place, blocks, frames)
    shape = (1, 1, tokens, full)
    return (
        attended.reshape(1, 1, tokens, model),
        query_grad.reshape(shape),
        key_grad.reshape(shape),
        value_grad.reshape(shape),
        scale_part[0, :heads],
    )


def solution(mesh):
    spec = P("dp", "frame", None, None)
    return jax.shard_map(
        local,
        mesh=mesh,
        in_specs=(spec, spec, spec, P(), P("dp", None), P(), spec),
        out_specs=(spec, spec, spec, spec, P()),
        check_vma=False,
    )
```

```python
import functools
import math

import jax
import jax.numpy as jnp
from jax import lax
from jax.experimental import pallas as pl
from jax.experimental.pallas import tpu as pltpu
from jax.sharding import PartitionSpec as P


HDH = 128
LANES = 128


F32 = jnp.float32
BF16 = jnp.bfloat16
NT = (((1,), (1,)), ((), ()))
NN = (((1,), (0,)), ((), ()))
TN = (((0,), (0,)), ((), ()))
SMEM = pl.BlockSpec(memory_space=pltpu.SMEM)
VMEM = pl.BlockSpec(memory_space=pltpu.VMEM)


def dot(a, b, dims):
    return lax.dot_general(a, b, dims, preferred_element_type=F32)


def lane_block(index, width):
    return pl.ds(pl.multiple_of(index * width, LANES), width)


def call(body, outs, operands, smem=0, scratch=()):
    return pl.pallas_call(
        body,
        out_shape=outs,
        in_specs=[SMEM] * smem + [VMEM] * (len(operands) - smem),
        out_specs=[VMEM] * len(outs),
        scratch_shapes=list(scratch),
    )(*operands)


def pack_body(frames, width, count, *refs):
    place = refs[0][0]
    sources = refs[1 : 1 + count]
    outs = refs[1 + count :]
    for s in range(frames):
        target = lax.rem(place + s, frames)
        for i in range(count):
            outs[s][i] = sources[i][:, lane_block(target, width)]


def pack(place, sources, frames):
    tokens, full = sources[0].shape
    width = full // frames
    shape = jax.ShapeDtypeStruct((len(sources), tokens, width), BF16)
    return call(
        functools.partial(pack_body, frames, width, len(sources)),
        [shape] * frames,
        [place, *sources],
        smem=1,
    )


def unpack_body(frames, width, count, *refs):
    place = refs[0][0]
    blocks = refs[1 : 1 + frames]
    outs = refs[1 + frames :]
    for s in range(frames):
        source = lax.rem(place + s, frames)
        for i in range(count):
            outs[i][:, lane_block(source, width)] = blocks[s][i]


def unpack(place, blocks, frames):
    count, tokens, width = blocks[0].shape
    shape = jax.ShapeDtypeStruct((tokens, width * frames), BF16)
    return call(
        functools.partial(unpack_body, frames, width, count),
        [shape] * count,
        [place, *blocks],
        smem=1,
    )


def softmax_parts(query, keys, factor):
    plain = [dot(query, key, NT) for key in keys]
    logits = [p * factor for p in plain]
    top = functools.reduce(jnp.maximum, [jnp.max(l, axis=1, keepdims=True) for l in logits])
    raised = [jnp.exp(l - top) for l in logits]
    total = functools.reduce(jnp.add, [jnp.sum(e, axis=1, keepdims=True) for e in raised])
    inverse = 1.0 / total
    return plain, [e * inverse for e in raised]


def forward_body(frames, heads, slots, place_ref, scale_ref, pattern_ref, *refs):
    blocks = refs[:frames]
    outs = refs[frames : 2 * frames]
    held = refs[2 * frames]
    place = place_ref[0]
    inv_root = 1.0 / math.sqrt(HDH)
    for s in range(frames):
        frame = lax.rem(place + frames - s, frames)
        held[frame] = blocks[s][1:3]
    for s in range(frames):
        frame = lax.rem(place + frames - s, frames)
        chosen = [pattern_ref[frame, j] for j in range(slots)]
        for h in range(heads):
            at = slice(h * HDH, (h + 1) * HDH)
            factor = scale_ref[place * heads + h] * inv_root
            keys = [held[g, 0, :, at] for g in chosen]
            _, probs = softmax_parts(blocks[s][0, :, at], keys, factor)
            context = functools.reduce(
                jnp.add,
                [dot(p.astype(BF16), held[g, 1, :, at], NN) for p, g in zip(probs, chosen)],
            )
            outs[s][0, :, at] = context.astype(BF16)


def forward(place, scale, pattern, blocks):
    frames = len(blocks)
    _, tokens, width = blocks[0].shape
    shape = jax.ShapeDtypeStruct((1, tokens, width), BF16)
    return call(
        functools.partial(forward_body, frames, width // HDH, pattern.shape[1]),
        [shape] * frames,
        [place, scale, pattern, *blocks],
        smem=3,
        scratch=[pltpu.VMEM((frames, 2, tokens, width), BF16)],
    )


def backward_body(frames, heads, slots, place_ref, scale_ref, pattern_ref, *refs):
    blocks = refs[:frames]
    grads = refs[frames : 2 * frames]
    outs = refs[2 * frames : 3 * frames]
    scale_out = refs[3 * frames]
    held, key_sum, value_sum = refs[3 * frames + 1 :]
    place = place_ref[0]
    inv_root = 1.0 / math.sqrt(HDH)
    key_sum[...] = jnp.zeros_like(key_sum)
    value_sum[...] = jnp.zeros_like(value_sum)
    for s in range(frames):
        frame = lax.rem(place + frames - s, frames)
        held[frame] = blocks[s][1:3]
    terms = [jnp.zeros((1, tokens_of(blocks)), F32) for _ in range(heads)]
    for s in range(frames):
        frame = lax.rem(place + frames - s, frames)
        chosen = [pattern_ref[frame, j] for j in range(slots)]
        for h in range(heads):
            at = slice(h * HDH, (h + 1) * HDH)
            factor = scale_ref[place * heads + h] * inv_root
            query = blocks[s][0, :, at]
            grad = grads[s][0, :, at]
            keys = [held[g, 0, :, at] for g in chosen]
            plain, probs = softmax_parts(query, keys, factor)
            prob_grads = [dot(grad, held[g, 1, :, at], NT) for g in chosen]
            weighted = functools.reduce(
                jnp.add,
                [jnp.sum(d * p, axis=1, keepdims=True) for d, p in zip(prob_grads, probs)],
            )
            score_grads = [p * (d - weighted) for d, p in zip(prob_grads, probs)]
            for sg, p in zip(score_grads, plain):
                terms[h] = terms[h] + jnp.sum(sg * p, axis=0, keepdims=True)
            low = [sg.astype(BF16) for sg in score_grads]
            query_grad = functools.reduce(
                jnp.add, [dot(sg, key, NN) for sg, key in zip(low, keys)]
            )
            outs[s][0, :, at] = (query_grad * factor).astype(BF16)
            for g, sg, p in zip(chosen, low, probs):
                key_sum[g, :, at] += dot(sg, query, TN) * factor
                value_sum[g, :, at] += dot(p.astype(BF16), grad, TN)
    for s in range(frames):
        frame = lax.rem(place + frames - s, frames)
        outs[s][1] = key_sum[frame].astype(BF16)
        outs[s][2] = value_sum[frame].astype(BF16)
    lanes = lax.broadcasted_iota(jnp.int32, scale_out.shape, 1)
    result = jnp.zeros(scale_out.shape, F32)
    for h in range(heads):
        part = jnp.sum(terms[h], axis=1, keepdims=True) * inv_root
        result = result + jnp.where(lanes == place * heads + h, part, 0.0)
    scale_out[...] = result


def tokens_of(blocks):
    return blocks[0].shape[1]


def backward(place, scale, pattern, blocks, grads):
    frames = len(blocks)
    _, tokens, width = blocks[0].shape
    shape = jax.ShapeDtypeStruct((3, tokens, width), BF16)
    result = call(
        functools.partial(backward_body, frames, width // HDH, pattern.shape[1]),
        [shape] * frames + [jax.ShapeDtypeStruct((1, LANES), F32)],
        [place, scale, pattern, *blocks, *grads],
        smem=3,
        scratch=[
            pltpu.VMEM((frames, 2, tokens, width), BF16),
            pltpu.VMEM((frames, tokens, width), F32),
            pltpu.VMEM((frames, tokens, width), F32),
        ],
    )
    return result[:frames], result[frames]


def context_grad_body(count, *refs):
    mine, other = refs[:2]
    weights = refs[2 : 2 + count]
    mine_out, other_out = refs[2 + count :]
    start = 0
    for w in weights:
        at = slice(start, start + w.shape[0])
        other_out[:, at] = dot(other[...], w[...], NT).astype(BF16)
        mine_out[:, at] = dot(mine[...], w[...], NT).astype(BF16)
        start += w.shape[0]


def context_grads(mine, other, weights):
    tokens = mine.shape[0]
    features = sum(w.shape[0] for w in weights)
    shape = jax.ShapeDtypeStruct((tokens, features), BF16)
    return call(
        functools.partial(context_grad_body, len(weights)), [shape, shape], [mine, other, *weights]
    )


def project_body(count, *refs):
    weights = refs[1 : 1 + count]
    out = refs[-1]
    start = 0
    total = None
    for w in weights:
        part = dot(rows_of(refs[0], start, w.shape[0]), w[...], NN)
        total = part if total is None else total + part
        start += w.shape[0]
    out[...] = total.astype(out.dtype)


def rows_of(ref, start, size):
    return ref[:, start : start + size]


def project(context, weights, dtype):
    tokens, features = context.shape
    width = weights[0].shape[1]
    tile = math.gcd(width, 1024)
    return pl.pallas_call(
        functools.partial(project_body, len(weights)),
        grid=(width // tile,),
        out_shape=jax.ShapeDtypeStruct((tokens, width), dtype),
        in_specs=[pl.BlockSpec((tokens, features), lambda i: (0, 0))]
        + [pl.BlockSpec((w.shape[0], tile), lambda i: (0, i)) for w in weights],
        out_specs=pl.BlockSpec((tokens, tile), lambda i: (0, i)),
        name="project",
    )(context, *weights)


def join_body(frames, pieces, size, *refs):
    place = refs[0][0]
    half = refs[1][0]
    inner = refs[1][1]
    count = len(pieces)
    mine = refs[2 : 2 + count]
    other = refs[2 + count : 2 + 2 * count]
    outs = refs[2 + 2 * count : 2 + 2 * count + frames]
    whole = refs[-1]
    group = sum(len(p) for p in pieces)
    width = whole.shape[1] // frames
    for h, sources in ((half, mine), (1 - half, other)):
        for source, names in zip(sources, pieces):
            for k, j in enumerate(names):
                spot = h * group + jnp.bitwise_xor(inner, j)
                whole[:, lane_block(spot, size)] = source[:, k * size : (k + 1) * size]
    for s in range(frames):
        outs[s][0] = whole[:, lane_block(lax.rem(place + s, frames), width)]


def join(place, where, mine, other, pieces, size, frames, full):
    tokens = mine[0].shape[0]
    if size % LANES == 0:
        shape = jax.ShapeDtypeStruct((1, tokens, full // frames), BF16)
        return call(
            functools.partial(join_body, frames, pieces, size),
            [shape] * frames,
            [place, where, *mine, *other],
            smem=2,
            scratch=[pltpu.VMEM((tokens, full), BF16)],
        )
    group = sum(len(p) for p in pieces)
    whole = jnp.zeros((tokens, full), BF16)
    for h, sources in ((where[0], mine), (1 - where[0], other)):
        for source, names in zip(sources, pieces):
            for k, j in enumerate(names):
                spot = h * group + jnp.bitwise_xor(where[1], j)
                piece = source[:, k * size : (k + 1) * size]
                whole = lax.dynamic_update_slice(whole, piece, (0, spot * size))
    return pack(place, [whole], frames)


def part_body(frames, count, size, *refs):
    place = refs[0][0]
    half = refs[1][0]
    inner = refs[1][1]
    blocks = refs[2 : 2 + frames]
    keep, send, whole = refs[2 + frames :]
    width = whole.shape[1] // frames
    for s in range(frames):
        whole[:, lane_block(lax.rem(place + s, frames), width)] = blocks[s][0]
    for j in range(count):
        spot = jnp.bitwise_xor(inner, j)
        at = slice(j * size, (j + 1) * size)
        keep[:, at] = whole[:, lane_block(half * count + spot, size)]
        send[:, at] = whole[:, lane_block((1 - half) * count + spot, size)]


def part(place, where, blocks, count, size):
    frames = len(blocks)
    _, tokens, width = blocks[0].shape
    if size % LANES == 0:
        shape = jax.ShapeDtypeStruct((tokens, count * size), BF16)
        return call(
            functools.partial(part_body, frames, count, size),
            [shape, shape],
            [place, where, *blocks],
            smem=2,
            scratch=[pltpu.VMEM((tokens, width * frames), BF16)],
        )
    whole = unpack(place, blocks, frames)[0]

    def half_of(h):
        spots = [h * count + jnp.bitwise_xor(where[1], j) for j in range(count)]
        return jnp.concatenate(
            [lax.dynamic_slice_in_dim(whole, spot * size, size, axis=1) for spot in spots], axis=1
        )

    return half_of(where[0]), half_of(1 - where[0])


def local(queries, key_states, value_states, head_scale, out_weight, frame_pattern, out_grad):
    frames = lax.axis_size("frame")
    group = lax.axis_size("dp")
    tokens, full = queries.shape[2:]
    model = out_grad.shape[3]
    heads = full // HDH
    count = group // 2
    size = out_weight.shape[0]
    place = lax.axis_index("frame").astype(jnp.int32).reshape(1)
    row = lax.axis_index("dp").astype(jnp.int32)
    where = jnp.stack([row // count, lax.rem(row, count)])

    def exchange(blocks, sign):
        def shift(s):
            return [(i, (i + sign * s) % frames) for i in range(frames)]

        return [blocks[0]] + [lax.ppermute(blocks[s], "frame", shift(s)) for s in range(1, frames)]

    def swap(x, bit):
        return lax.ppermute(x, "dp", [(i, i ^ bit) for i in range(group)])

    grad_rows = out_grad[0, 0]
    other_rows = swap(grad_rows, count)
    chunks = 2 if size % 256 == 0 else 1
    step = size // chunks
    weights = {0: [out_weight[i * step : (i + 1) * step] for i in range(chunks)]}
    bit = count // 2
    while bit:
        for j in list(weights):
            weights[j ^ bit] = [swap(c, bit) for c in weights[j]]
        bit //= 2
    early = [c for j in range(count // 2) for c in weights[j]]
    late = [c for j in range(count // 2, count) for c in weights[j]]
    names = (list(range(count // 2)), list(range(count // 2, count)))

    sent = pack(place, [queries[0, 0], key_states[0, 0], value_states[0, 0]], frames)
    blocks = exchange(sent, 1)
    mine_early, theirs = context_grads(grad_rows, other_rows, early)
    other_early = swap(theirs, count)
    context = forward(place, head_scale, frame_pattern, blocks)
    context = exchange(context, -1)
    mine_late, theirs = context_grads(grad_rows, other_rows, late)
    other_late = swap(theirs, count)
    mine = [mine_early, mine_late]
    other = [other_early, other_late]
    sent = join(place, where, mine, other, names, size, frames, full)
    grads = exchange(sent, 1)

    keep, send = part(place, where, context, count, size)
    taken = swap(send, count)
    own = project(keep, early + late, F32)
    theirs = project(taken, early + late, F32)
    returned = swap(theirs, count)
    attended = (own + returned).astype(BF16)

    sent, scale_part = backward(place, head_scale, frame_pattern, blocks, grads)
    blocks = exchange(sent, -1)
    bit = group // 2
    while bit:
        scale_part = scale_part + swap(scale_part, bit)
        bit //= 2
    scale_sum = functools.reduce(jnp.add, exchange([scale_part] * frames, 1))

    query_grad, key_grad, value_grad = unpack(place, blocks, frames)
    shape = (1, 1, tokens, full)
    return (
        attended.reshape(1, 1, tokens, model),
        query_grad.reshape(shape),
        key_grad.reshape(shape),
        value_grad.reshape(shape),
        scale_sum[0, :heads],
    )


def solution(mesh):
    spec = P("dp", "frame", None, None)
    return jax.shard_map(
        local,
        mesh=mesh,
        in_specs=(spec, spec, spec, P(), P("dp", None), P(), spec),
        out_specs=(spec, spec, spec, spec, P()),
        check_vma=False,
    )
```

```python
import functools
import math

import jax
import jax.numpy as jnp
from jax import lax
from jax.experimental import pallas as pl
from jax.experimental.pallas import tpu as pltpu
from jax.sharding import PartitionSpec as P


HDH = 128
LANES = 128
LOG2E = 1.0 / math.log(2.0)


F32 = jnp.float32
BF16 = jnp.bfloat16
NT = (((1,), (1,)), ((), ()))
NN = (((1,), (0,)), ((), ()))
TN = (((0,), (0,)), ((), ()))
SMEM = pl.BlockSpec(memory_space=pltpu.SMEM)
VMEM = pl.BlockSpec(memory_space=pltpu.VMEM)


def dot(a, b, dims):
    return lax.dot_general(a, b, dims, preferred_element_type=F32)


def lane_block(index, width):
    return pl.ds(pl.multiple_of(index * width, LANES), width)


def call(body, outs, operands, smem=0, scratch=()):
    return pl.pallas_call(
        body,
        out_shape=outs,
        in_specs=[SMEM] * smem + [VMEM] * (len(operands) - smem),
        out_specs=[VMEM] * len(outs),
        scratch_shapes=list(scratch),
    )(*operands)


def pack_body(frames, width, count, *refs):
    place = refs[0][0]
    sources = refs[1 : 1 + count]
    outs = refs[1 + count :]
    for s in range(frames):
        target = lax.rem(place + s, frames)
        for i in range(count):
            outs[s][i] = sources[i][:, lane_block(target, width)]


def pack(place, sources, frames):
    tokens, full = sources[0].shape
    width = full // frames
    shape = jax.ShapeDtypeStruct((len(sources), tokens, width), BF16)
    return call(
        functools.partial(pack_body, frames, width, len(sources)),
        [shape] * frames,
        [place, *sources],
        smem=1,
    )


def unpack_body(frames, width, count, *refs):
    place = refs[0][0]
    blocks = refs[1 : 1 + frames]
    outs = refs[1 + frames :]
    for s in range(frames):
        source = lax.rem(place + s, frames)
        for i in range(count):
            outs[i][:, lane_block(source, width)] = blocks[s][i]


def unpack(place, blocks, frames):
    count, tokens, width = blocks[0].shape
    shape = jax.ShapeDtypeStruct((tokens, width * frames), BF16)
    return call(
        functools.partial(unpack_body, frames, width, count),
        [shape] * count,
        [place, *blocks],
        smem=1,
    )


def both(parts):
    return jnp.concatenate(parts, axis=0)


def softmax_rows(query, keys, factor):
    plain = dot(keys, query, NT)
    top = jnp.max(plain, axis=0, keepdims=True)
    raised = jnp.exp2((plain - top) * (factor * LOG2E))
    total = jnp.sum(raised, axis=0, keepdims=True)
    return plain, raised * (1.0 / total)


def forward_body(frames, heads, slots, place_ref, scale_ref, pattern_ref, *refs):
    blocks = refs[:frames]
    outs = refs[frames : 2 * frames]
    held = refs[2 * frames]
    place = place_ref[0]
    inv_root = 1.0 / math.sqrt(HDH)
    for s in range(frames):
        frame = lax.rem(place + frames - s, frames)
        held[frame] = blocks[s][1:3]
    for s in range(frames):
        frame = lax.rem(place + frames - s, frames)
        chosen = [pattern_ref[frame, j] for j in range(slots)]
        for h in range(heads):
            at = slice(h * HDH, (h + 1) * HDH)
            factor = scale_ref[place * heads + h] * inv_root
            keys = both([held[g, 0, :, at] for g in chosen])
            values = both([held[g, 1, :, at] for g in chosen])
            _, probs = softmax_rows(blocks[s][0, :, at], keys, factor)
            outs[s][0, :, at] = dot(probs.astype(BF16), values, TN).astype(BF16)


def forward(place, scale, pattern, blocks):
    frames = len(blocks)
    _, tokens, width = blocks[0].shape
    shape = jax.ShapeDtypeStruct((1, tokens, width), BF16)
    return call(
        functools.partial(forward_body, frames, width // HDH, pattern.shape[1]),
        [shape] * frames,
        [place, scale, pattern, *blocks],
        smem=3,
        scratch=[pltpu.VMEM((frames, 2, tokens, width), BF16)],
    )


def backward_body(frames, heads, slots, place_ref, scale_ref, pattern_ref, *refs):
    blocks = refs[:frames]
    grads = refs[frames : 2 * frames]
    outs = refs[2 * frames : 3 * frames]
    scale_out = refs[3 * frames]
    held, key_sum, value_sum = refs[3 * frames + 1 :]
    place = place_ref[0]
    tokens = tokens_of(blocks)
    inv_root = 1.0 / math.sqrt(HDH)
    factors = [scale_ref[place * heads + h] * inv_root for h in range(heads)]
    key_sum[...] = jnp.zeros_like(key_sum)
    value_sum[...] = jnp.zeros_like(value_sum)
    for s in range(frames):
        frame = lax.rem(place + frames - s, frames)
        held[frame] = blocks[s][1:3]
    terms = [jnp.zeros((1, tokens), F32) for _ in range(heads)]
    for s in range(frames):
        frame = lax.rem(place + frames - s, frames)
        chosen = [pattern_ref[frame, j] for j in range(slots)]
        for h in range(heads):
            at = slice(h * HDH, (h + 1) * HDH)
            query = blocks[s][0, :, at]
            grad = grads[s][0, :, at]
            keys = both([held[g, 0, :, at] for g in chosen])
            values = both([held[g, 1, :, at] for g in chosen])
            plain, probs = softmax_rows(query, keys, factors[h])
            prob_grads = dot(values, grad, NT)
            weighted = jnp.sum(prob_grads * probs, axis=0, keepdims=True)
            score_grads = probs * (prob_grads - weighted)
            terms[h] = terms[h] + jnp.sum(score_grads * plain, axis=0, keepdims=True)
            low = score_grads.astype(BF16)
            outs[s][0, :, at] = (dot(low, keys, TN) * factors[h]).astype(BF16)
            key_part = dot(low, query, NN)
            value_part = dot(probs.astype(BF16), grad, NN)
            for j, g in enumerate(chosen):
                rows = slice(j * tokens, (j + 1) * tokens)
                key_sum[g, :, at] += key_part[rows]
                value_sum[g, :, at] += value_part[rows]
    for s in range(frames):
        frame = lax.rem(place + frames - s, frames)
        for h in range(heads):
            at = slice(h * HDH, (h + 1) * HDH)
            outs[s][1, :, at] = (key_sum[frame, :, at] * factors[h]).astype(BF16)
        outs[s][2] = value_sum[frame].astype(BF16)
    lanes = lax.broadcasted_iota(jnp.int32, scale_out.shape, 1)
    result = jnp.zeros(scale_out.shape, F32)
    for h in range(heads):
        part = jnp.sum(terms[h], axis=1, keepdims=True) * inv_root
        result = result + jnp.where(lanes == place * heads + h, part, 0.0)
    scale_out[...] = result


def tokens_of(blocks):
    return blocks[0].shape[1]


def backward(place, scale, pattern, blocks, grads):
    frames = len(blocks)
    _, tokens, width = blocks[0].shape
    shape = jax.ShapeDtypeStruct((3, tokens, width), BF16)
    result = call(
        functools.partial(backward_body, frames, width // HDH, pattern.shape[1]),
        [shape] * frames + [jax.ShapeDtypeStruct((1, LANES), F32)],
        [place, scale, pattern, *blocks, *grads],
        smem=3,
        scratch=[
            pltpu.VMEM((frames, 2, tokens, width), BF16),
            pltpu.VMEM((frames, tokens, width), F32),
            pltpu.VMEM((frames, tokens, width), F32),
        ],
    )
    return result[:frames], result[frames]


def context_grad_body(skip, count, *refs):
    refs = refs[skip:]
    mine, other = refs[:2]
    weights = refs[2 : 2 + count]
    mine_out, other_out = refs[2 + count :]
    tokens = mine.shape[0]
    rows = both([other[...], mine[...]])
    start = 0
    for w in weights:
        at = slice(start, start + w.shape[0])
        result = dot(rows, w[...], NT).astype(BF16)
        other_out[:, at] = result[:tokens]
        mine_out[:, at] = result[tokens:]
        start += w.shape[0]


def context_grads(mine, other, weights, scalars=()):
    tokens = mine.shape[0]
    features = sum(w.shape[0] for w in weights)
    shape = jax.ShapeDtypeStruct((tokens, features), BF16)
    return call(
        functools.partial(context_grad_body, len(scalars), len(weights)),
        [shape, shape],
        [*scalars, mine, other, *weights],
        smem=len(scalars),
    )


def project_body(count, *refs):
    mine, other = refs[:2]
    weights = refs[2 : 2 + count]
    mine_out, other_out = refs[2 + count :]
    tokens = mine.shape[0]
    rows = both([other[...], mine[...]])
    start = 0
    total = None
    for w in weights:
        part = dot(rows[:, start : start + w.shape[0]], w[...], NN)
        total = part if total is None else total + part
        start += w.shape[0]
    other_out[...] = total[:tokens]
    mine_out[...] = total[tokens:]


def project_pair(mine, other, weights):
    tokens, features = mine.shape
    width = weights[0].shape[1]
    tile = math.gcd(width, 1024)
    rows = pl.BlockSpec((tokens, features), lambda i: (0, 0))
    columns = pl.BlockSpec((tokens, tile), lambda i: (0, i))
    shape = jax.ShapeDtypeStruct((tokens, width), F32)
    return pl.pallas_call(
        functools.partial(project_body, len(weights)),
        grid=(width // tile,),
        out_shape=[shape, shape],
        in_specs=[rows, rows]
        + [pl.BlockSpec((w.shape[0], tile), lambda i: (0, i)) for w in weights],
        out_specs=[columns, columns],
        name="project",
    )(mine, other, *weights)


def place_in_half(row, group):
    half = lax.div(row, group)
    return half, row - half * group


def join_body(frames, pieces, size, *refs):
    place = refs[0][0]
    half, inner = place_in_half(refs[1][0], sum(len(p) for p in pieces))
    count = len(pieces)
    mine = refs[2 : 2 + count]
    other = refs[2 + count : 2 + 2 * count]
    outs = refs[2 + 2 * count : 2 + 2 * count + frames]
    whole = refs[-1]
    group = sum(len(p) for p in pieces)
    width = whole.shape[1] // frames
    for h, sources in ((half, mine), (1 - half, other)):
        for source, names in zip(sources, pieces):
            for k, j in enumerate(names):
                spot = h * group + jnp.bitwise_xor(inner, j)
                whole[:, lane_block(spot, size)] = source[:, k * size : (k + 1) * size]
    for s in range(frames):
        outs[s][0] = whole[:, lane_block(lax.rem(place + s, frames), width)]


def join(place, row, mine, other, pieces, size, frames, full):
    tokens = mine[0].shape[0]
    if size % LANES == 0:
        shape = jax.ShapeDtypeStruct((1, tokens, full // frames), BF16)
        return call(
            functools.partial(join_body, frames, pieces, size),
            [shape] * frames,
            [place, row, *mine, *other],
            smem=2,
            scratch=[pltpu.VMEM((tokens, full), BF16)],
        )
    group = sum(len(p) for p in pieces)
    whole = jnp.zeros((tokens, full), BF16)
    half, inner = place_in_half(row[0], group)
    for h, sources in ((half, mine), (1 - half, other)):
        for source, names in zip(sources, pieces):
            for k, j in enumerate(names):
                spot = h * group + jnp.bitwise_xor(inner, j)
                piece = source[:, k * size : (k + 1) * size]
                whole = lax.dynamic_update_slice(whole, piece, (0, spot * size))
    return pack(place, [whole], frames)


def part_body(frames, count, size, *refs):
    place = refs[0][0]
    half, inner = place_in_half(refs[1][0], count)
    blocks = refs[2 : 2 + frames]
    keep, send, whole = refs[2 + frames :]
    width = whole.shape[1] // frames
    for s in range(frames):
        whole[:, lane_block(lax.rem(place + s, frames), width)] = blocks[s][0]
    for j in range(count):
        spot = jnp.bitwise_xor(inner, j)
        at = slice(j * size, (j + 1) * size)
        keep[:, at] = whole[:, lane_block(half * count + spot, size)]
        send[:, at] = whole[:, lane_block((1 - half) * count + spot, size)]


def part(place, row, blocks, count, size):
    frames = len(blocks)
    _, tokens, width = blocks[0].shape
    if size % LANES == 0:
        shape = jax.ShapeDtypeStruct((tokens, count * size), BF16)
        return call(
            functools.partial(part_body, frames, count, size),
            [shape, shape],
            [place, row, *blocks],
            smem=2,
            scratch=[pltpu.VMEM((tokens, width * frames), BF16)],
        )
    whole = unpack(place, blocks, frames)[0]
    half, inner = place_in_half(row[0], count)

    def half_of(h):
        spots = [h * count + jnp.bitwise_xor(inner, j) for j in range(count)]
        return jnp.concatenate(
            [lax.dynamic_slice_in_dim(whole, spot * size, size, axis=1) for spot in spots], axis=1
        )

    return half_of(half), half_of(1 - half)


def local(queries, key_states, value_states, head_scale, out_weight, frame_pattern, out_grad):
    frames = lax.axis_size("frame")
    group = lax.axis_size("dp")
    tokens, full = queries.shape[2:]
    model = out_grad.shape[3]
    heads = full // HDH
    count = group // 2
    size = out_weight.shape[0]
    place = lax.axis_index("frame").astype(jnp.int32).reshape(1)
    row = lax.axis_index("dp").astype(jnp.int32).reshape(1)

    def exchange(blocks, sign):
        def shift(s):
            return [(i, (i + sign * s) % frames) for i in range(frames)]

        return [blocks[0]] + [lax.ppermute(blocks[s], "frame", shift(s)) for s in range(1, frames)]

    def swap(x, bit):
        return lax.ppermute(x, "dp", [(i, i ^ bit) for i in range(group)])

    grad_rows = out_grad[0, 0]
    other_rows = swap(grad_rows, count)
    weights = {0: [out_weight]}
    bit = count // 2
    while bit:
        for j in list(weights):
            weights[j ^ bit] = [swap(c, bit) for c in weights[j]]
        bit //= 2
    early = [c for j in range(count // 2) for c in weights[j]]
    late = [c for j in range(count // 2, count) for c in weights[j]]
    names = (list(range(count // 2)), list(range(count // 2, count)))

    sent = pack(place, [queries[0, 0], key_states[0, 0], value_states[0, 0]], frames)
    blocks = exchange(sent, 1)
    mine_early, theirs = context_grads(grad_rows, other_rows, early, [frame_pattern])
    other_early = swap(theirs, count)
    context = forward(place, head_scale, frame_pattern, blocks)
    context = exchange(context, -1)
    mine_late, theirs = context_grads(grad_rows, other_rows, late)
    other_late = swap(theirs, count)
    mine = [mine_early, mine_late]
    other = [other_early, other_late]
    sent = join(place, row, mine, other, names, size, frames, full)
    grads = exchange(sent, 1)

    keep, send = part(place, row, context, count, size)
    taken = swap(send, count)
    own, theirs = project_pair(keep, taken, early + late)
    returned = swap(theirs, count)
    attended = (own + returned).astype(BF16)

    sent, scale_part = backward(place, head_scale, frame_pattern, blocks, grads)
    blocks = exchange(sent, -1)
    bit = 1
    while bit < group:
        scale_part = scale_part + swap(scale_part, bit)
        bit *= 2
    scale_sum = functools.reduce(jnp.add, exchange([scale_part] * frames, 1))

    query_grad, key_grad, value_grad = unpack(place, blocks, frames)
    shape = (1, 1, tokens, full)
    return (
        attended.reshape(1, 1, tokens, model),
        query_grad.reshape(shape),
        key_grad.reshape(shape),
        value_grad.reshape(shape),
        scale_sum[0, :heads],
    )


def solution(mesh):
    spec = P("dp", "frame", None, None)
    return jax.shard_map(
        local,
        mesh=mesh,
        in_specs=(spec, spec, spec, P(), P("dp", None), P(), spec),
        out_specs=(spec, spec, spec, spec, P()),
        check_vma=False,
    )
```

```python
import functools
import math

import jax
import jax.numpy as jnp
from jax import lax
from jax.experimental import pallas as pl
from jax.experimental.pallas import tpu as pltpu
from jax.sharding import PartitionSpec as P


HDH = 128
LANES = 128
LOG2E = 1.0 / math.log(2.0)


F32 = jnp.float32
BF16 = jnp.bfloat16
NT = (((1,), (1,)), ((), ()))
NN = (((1,), (0,)), ((), ()))
TN = (((0,), (0,)), ((), ()))
SMEM = pl.BlockSpec(memory_space=pltpu.SMEM)
VMEM = pl.BlockSpec(memory_space=pltpu.VMEM)


def dot(a, b, dims):
    return lax.dot_general(a, b, dims, preferred_element_type=F32)


def lane_block(index, width):
    return pl.ds(pl.multiple_of(index * width, LANES), width)


def call(body, outs, operands, smem=0, scratch=()):
    return pl.pallas_call(
        body,
        out_shape=outs,
        in_specs=[SMEM] * smem + [VMEM] * (len(operands) - smem),
        out_specs=[VMEM] * len(outs),
        scratch_shapes=list(scratch),
    )(*operands)


def pack_body(frames, width, count, *refs):
    place = refs[0][0]
    sources = refs[1 : 1 + count]
    outs = refs[1 + count :]
    for s in range(frames):
        target = lax.rem(place + s, frames)
        for i in range(count):
            outs[s][i] = sources[i][:, lane_block(target, width)]


def pack(place, sources, frames):
    tokens, full = sources[0].shape
    width = full // frames
    shape = jax.ShapeDtypeStruct((len(sources), tokens, width), BF16)
    return call(
        functools.partial(pack_body, frames, width, len(sources)),
        [shape] * frames,
        [place, *sources],
        smem=1,
    )


def unpack_body(frames, width, count, *refs):
    place = refs[0][0]
    blocks = refs[1 : 1 + frames]
    outs = refs[1 + frames :]
    for s in range(frames):
        source = lax.rem(place + s, frames)
        for i in range(count):
            outs[i][:, lane_block(source, width)] = blocks[s][i]


def unpack(place, blocks, frames):
    count, tokens, width = blocks[0].shape
    shape = jax.ShapeDtypeStruct((tokens, width * frames), BF16)
    return call(
        functools.partial(unpack_body, frames, width, count),
        [shape] * count,
        [place, *blocks],
        smem=1,
    )


def piece_of(target, late, row, frames):
    quarter = frames // 2
    inner = lax.rem(row, frames)
    far = jnp.bitwise_xor(lax.div(inner, quarter), late)
    return lax.div(target, quarter) * frames + far * quarter + lax.rem(target, quarter)


def both(parts):
    return jnp.concatenate(parts, axis=0)


def softmax_rows(query, keys, factor):
    plain = dot(keys, query, NT)
    top = jnp.max(plain, axis=0, keepdims=True)
    raised = jnp.exp2((plain - top) * (factor * LOG2E))
    total = jnp.sum(raised, axis=0, keepdims=True)
    return plain, raised * (1.0 / total)


def head_numbers(place, row, heads, split, frames):
    if not split:
        return [place * heads + h for h in range(heads)]
    each = heads // 2
    pieces = [piece_of(place, late, row, frames) for late in range(2)]
    return [pieces[h // each] * each + h % each for h in range(heads)]


def factors_of(place, row, scale_ref, heads, split, frames):
    inv_root = 1.0 / math.sqrt(HDH)
    return [scale_ref[n] * inv_root for n in head_numbers(place, row, heads, split, frames)]


def forward_body(frames, heads, slots, split, *refs):
    place_ref, row_ref, scale_ref, pattern_ref = refs[:4]
    blocks = refs[4 : 4 + frames]
    outs = refs[4 + frames : 4 + 2 * frames]
    held = refs[-1]
    place = place_ref[0]
    factors = factors_of(place, row_ref[0], scale_ref, heads, split, frames)
    for s in range(frames):
        frame = lax.rem(place + frames - s, frames)
        held[frame] = blocks[s][1:3]
    for s in range(frames):
        frame = lax.rem(place + frames - s, frames)
        chosen = [pattern_ref[frame, j] for j in range(slots)]
        for h in range(heads):
            at = slice(h * HDH, (h + 1) * HDH)
            keys = both([held[g, 0, :, at] for g in chosen])
            values = both([held[g, 1, :, at] for g in chosen])
            _, probs = softmax_rows(blocks[s][0, :, at], keys, factors[h])
            outs[s][0, :, at] = dot(probs.astype(BF16), values, TN).astype(BF16)


def forward(place, row, scale, pattern, blocks, split=False):
    frames = len(blocks)
    _, tokens, width = blocks[0].shape
    shape = jax.ShapeDtypeStruct((1, tokens, width), BF16)
    return call(
        functools.partial(forward_body, frames, width // HDH, pattern.shape[1], split),
        [shape] * frames,
        [place, row, scale, pattern, *blocks],
        smem=4,
        scratch=[pltpu.VMEM((frames, 2, tokens, width), BF16)],
    )


def backward_body(frames, heads, slots, half, before, *refs):
    place_ref, row_ref, scale_ref, pattern_ref = refs[:4]
    earlier = refs[4 : 4 + before]
    refs = refs[4 + before :]
    blocks = refs[:frames]
    grads = refs[frames : 2 * frames]
    outs = refs[2 * frames : 3 * frames]
    scale_out = refs[3 * frames]
    held, key_sum, value_sum = refs[3 * frames + 1 :]
    place = place_ref[0]
    tokens = tokens_of(blocks)
    inv_root = 1.0 / math.sqrt(HDH)
    if half is None:
        base = 0
        numbers = head_numbers(place, row_ref[0], heads, False, frames)
    else:
        base = half * heads * HDH
        numbers = head_numbers(place, row_ref[0], 2 * heads, True, frames)
        numbers = numbers[half * heads : (half + 1) * heads]
    factors = [scale_ref[n] * inv_root for n in numbers]
    part = slice(base, base + heads * HDH)
    key_sum[...] = jnp.zeros_like(key_sum)
    value_sum[...] = jnp.zeros_like(value_sum)
    for s in range(frames):
        frame = lax.rem(place + frames - s, frames)
        held[frame] = blocks[s][1:3, :, part]
    terms = [jnp.zeros((1, tokens), F32) for _ in range(heads)]
    for s in range(frames):
        frame = lax.rem(place + frames - s, frames)
        chosen = [pattern_ref[frame, j] for j in range(slots)]
        for h in range(heads):
            at = slice(h * HDH, (h + 1) * HDH)
            query = blocks[s][0, :, base + h * HDH : base + (h + 1) * HDH]
            grad = grads[s][0, :, at]
            keys = both([held[g, 0, :, at] for g in chosen])
            values = both([held[g, 1, :, at] for g in chosen])
            plain, probs = softmax_rows(query, keys, factors[h])
            prob_grads = dot(values, grad, NT)
            weighted = jnp.sum(prob_grads * probs, axis=0, keepdims=True)
            score_grads = probs * (prob_grads - weighted)
            terms[h] = terms[h] + jnp.sum(score_grads * plain, axis=0, keepdims=True)
            low = score_grads.astype(BF16)
            outs[s][0, :, at] = (dot(low, keys, TN) * factors[h]).astype(BF16)
            key_part = dot(low, query, NN)
            value_part = dot(probs.astype(BF16), grad, NN)
            for j, g in enumerate(chosen):
                rows = slice(j * tokens, (j + 1) * tokens)
                key_sum[g, :, at] += key_part[rows]
                value_sum[g, :, at] += value_part[rows]
    for s in range(frames):
        frame = lax.rem(place + frames - s, frames)
        for h in range(heads):
            at = slice(h * HDH, (h + 1) * HDH)
            outs[s][1, :, at] = (key_sum[frame, :, at] * factors[h]).astype(BF16)
        outs[s][2] = value_sum[frame].astype(BF16)
    lanes = lax.broadcasted_iota(jnp.int32, scale_out.shape, 1)
    result = earlier[0][...] if before else jnp.zeros(scale_out.shape, F32)
    for h in range(heads):
        term = jnp.sum(terms[h], axis=1, keepdims=True) * inv_root
        result = result + jnp.where(lanes == numbers[h], term, 0.0)
    scale_out[...] = result


def tokens_of(blocks):
    return blocks[0].shape[1]


def backward(place, row, scale, pattern, blocks, grads, half=None, before=()):
    frames = len(blocks)
    _, tokens, width = grads[0].shape
    shape = jax.ShapeDtypeStruct((3, tokens, width), BF16)
    result = call(
        functools.partial(
            backward_body, frames, width // HDH, pattern.shape[1], half, len(before)
        ),
        [shape] * frames + [jax.ShapeDtypeStruct((1, LANES), F32)],
        [place, row, scale, pattern, *before, *blocks, *grads],
        smem=4,
        scratch=[
            pltpu.VMEM((frames, 2, tokens, width), BF16),
            pltpu.VMEM((frames, tokens, width), F32),
            pltpu.VMEM((frames, tokens, width), F32),
        ],
    )
    return result[:frames], result[frames]


def context_grad_body(skip, count, *refs):
    refs = refs[skip:]
    mine, other = refs[:2]
    weights = refs[2 : 2 + count]
    mine_out, other_out = refs[2 + count :]
    tokens = mine.shape[0]
    rows = both([other[...], mine[...]])
    start = 0
    for w in weights:
        at = slice(start, start + w.shape[0])
        result = dot(rows, w[...], NT).astype(BF16)
        other_out[:, at] = result[:tokens]
        mine_out[:, at] = result[tokens:]
        start += w.shape[0]


def context_grads(mine, other, weights, scalars=()):
    tokens = mine.shape[0]
    features = sum(w.shape[0] for w in weights)
    shape = jax.ShapeDtypeStruct((tokens, features), BF16)
    return call(
        functools.partial(context_grad_body, len(scalars), len(weights)),
        [shape, shape],
        [*scalars, mine, other, *weights],
        smem=len(scalars),
    )


def project_body(count, columns, *refs):
    mine, other = refs[:2]
    weights = refs[2 : 2 + count]
    mine_out, other_out = refs[2 + count :]
    tokens = mine.shape[0]
    rows = both([other[...], mine[...]])
    start = 0
    total = None
    for w in weights:
        part = dot(rows[:, start : start + w.shape[0]], w[:, columns], NN)
        total = part if total is None else total + part
        start += w.shape[0]
    other_out[...] = total[:tokens].astype(other_out.dtype)
    mine_out[...] = total[tokens:]


def project_pair(mine, other, weights, first=0, last=None):
    tokens, _ = mine.shape
    columns = slice(first, weights[0].shape[1] if last is None else last)
    width = columns.stop - columns.start
    return call(
        functools.partial(project_body, len(weights), columns),
        [jax.ShapeDtypeStruct((tokens, width), kind) for kind in (F32, BF16)],
        [mine, other, *weights],
    )


def place_in_half(row, group):
    half = lax.div(row, group)
    return half, row - half * group


def join_body(frames, pieces, size, *refs):
    place = refs[0][0]
    half, inner = place_in_half(refs[1][0], sum(len(p) for p in pieces))
    count = len(pieces)
    mine = refs[2 : 2 + count]
    other = refs[2 + count : 2 + 2 * count]
    outs = refs[2 + 2 * count : 2 + 2 * count + frames]
    whole = refs[-1]
    group = sum(len(p) for p in pieces)
    width = whole.shape[1] // frames
    for h, sources in ((half, mine), (1 - half, other)):
        for source, names in zip(sources, pieces):
            for k, j in enumerate(names):
                spot = h * group + jnp.bitwise_xor(inner, j)
                whole[:, lane_block(spot, size)] = source[:, k * size : (k + 1) * size]
    for s in range(frames):
        outs[s][0] = whole[:, lane_block(lax.rem(place + s, frames), width)]


def join(place, row, mine, other, pieces, size, frames, full):
    tokens = mine[0].shape[0]
    if size % LANES == 0:
        shape = jax.ShapeDtypeStruct((1, tokens, full // frames), BF16)
        return call(
            functools.partial(join_body, frames, pieces, size),
            [shape] * frames,
            [place, row, *mine, *other],
            smem=2,
            scratch=[pltpu.VMEM((tokens, full), BF16)],
        )
    group = sum(len(p) for p in pieces)
    whole = jnp.zeros((tokens, full), BF16)
    half, inner = place_in_half(row[0], group)
    for h, sources in ((half, mine), (1 - half, other)):
        for source, names in zip(sources, pieces):
            for k, j in enumerate(names):
                spot = h * group + jnp.bitwise_xor(inner, j)
                piece = source[:, k * size : (k + 1) * size]
                whole = lax.dynamic_update_slice(whole, piece, (0, spot * size))
    return pack(place, [whole], frames)


def part_body(frames, count, size, *refs):
    place = refs[0][0]
    half, inner = place_in_half(refs[1][0], count)
    blocks = refs[2 : 2 + frames]
    keep, send, whole = refs[2 + frames :]
    width = whole.shape[1] // frames
    for s in range(frames):
        whole[:, lane_block(lax.rem(place + s, frames), width)] = blocks[s][0]
    for j in range(count):
        spot = jnp.bitwise_xor(inner, j)
        at = slice(j * size, (j + 1) * size)
        keep[:, at] = whole[:, lane_block(half * count + spot, size)]
        send[:, at] = whole[:, lane_block((1 - half) * count + spot, size)]


def part(place, row, blocks, count, size):
    frames = len(blocks)
    _, tokens, width = blocks[0].shape
    if size % LANES == 0:
        shape = jax.ShapeDtypeStruct((tokens, count * size), BF16)
        return call(
            functools.partial(part_body, frames, count, size),
            [shape, shape],
            [place, row, *blocks],
            smem=2,
            scratch=[pltpu.VMEM((tokens, width * frames), BF16)],
        )
    whole = unpack(place, blocks, frames)[0]
    half, inner = place_in_half(row[0], count)

    def half_of(h):
        spots = [h * count + jnp.bitwise_xor(inner, j) for j in range(count)]
        return jnp.concatenate(
            [lax.dynamic_slice_in_dim(whole, spot * size, size, axis=1) for spot in spots], axis=1
        )

    return half_of(half), half_of(1 - half)


def split_pack_body(frames, count, *refs):
    place, row = refs[0][0], refs[1][0]
    sources = refs[2 : 2 + count]
    outs = refs[2 + count :]
    size = outs[0].shape[2] // 2
    for s in range(frames):
        target = lax.rem(place + s, frames)
        for late in range(2):
            piece = piece_of(target, late, row, frames)
            for i in range(count):
                at = slice(late * size, (late + 1) * size)
                outs[s][i, :, at] = sources[i][:, lane_block(piece, size)]


def split_pack(place, row, sources, frames):
    tokens, full = sources[0].shape
    shape = jax.ShapeDtypeStruct((len(sources), tokens, full // frames), BF16)
    return call(
        functools.partial(split_pack_body, frames, len(sources)),
        [shape] * frames,
        [place, row, *sources],
        smem=2,
    )


def scatter_body(frames, count, late, *refs):
    place, row = refs[0][0], refs[1][0]
    blocks = refs[2 : 2 + frames]
    outs = refs[-1 - count : -1]
    arrived = refs[-1]
    size = blocks[0].shape[2]
    copies = []
    for s in range(frames):
        piece = piece_of(lax.rem(place + s, frames), late, row, frames)
        for i in range(count):
            target = outs[i].at[:, lane_block(piece, size)]
            copies.append(
                pltpu.make_async_copy(blocks[s].at[i], target, arrived.at[s * count + i])
            )
    for copy in copies:
        copy.start()
    for copy in copies:
        copy.wait()


def scatter(place, row, blocks, late, full, partly):
    frames = len(blocks)
    count, tokens, _ = blocks[0].shape
    whole = pl.BlockSpec(memory_space=pltpu.HBM)
    return pl.pallas_call(
        functools.partial(scatter_body, frames, count, late),
        out_shape=[jax.ShapeDtypeStruct((tokens, full), BF16)] * count,
        in_specs=[SMEM] * 2 + [whole] * (frames + len(partly)),
        out_specs=[whole] * count,
        scratch_shapes=[pltpu.SemaphoreType.DMA((frames * count,))],
        input_output_aliases={2 + frames + i: i for i in range(len(partly))},
        name="scatter",
    )(place, row, *blocks, *partly)


def split_join_body(frames, count, *refs):
    place, row = refs[0][0], refs[1][0]
    mine = refs[2 : 2 + count]
    other = refs[2 + count : 2 + 2 * count]
    outs = refs[2 + 2 * count : 2 + 2 * count + frames]
    own, theirs = refs[2 + 2 * count + frames :]
    quarter = frames // 2
    size = own.shape[1] // quarter
    half, inner = place_in_half(row, frames)
    for sources, whole in ((mine, own), (other, theirs)):
        start = 0
        for source in sources:
            whole[:, start : start + source.shape[1]] = source[...]
            start += source.shape[1]
    for s in range(frames):
        target = lax.rem(place + s, frames)
        near = jnp.bitwise_xor(lax.rem(target, quarter), lax.rem(inner, quarter))
        at = lane_block(near, size)
        outs[s][0] = jnp.where(lax.div(target, quarter) == half, own[:, at], theirs[:, at])


def split_join(place, row, mine, other, frames):
    tokens = mine[0].shape[0]
    width = sum(m.shape[1] for m in mine)
    shape = jax.ShapeDtypeStruct((1, tokens, 2 * width // frames), BF16)
    return call(
        functools.partial(split_join_body, frames, len(mine)),
        [shape] * frames,
        [place, row, *mine, *other],
        smem=2,
        scratch=[pltpu.VMEM((tokens, width), BF16)] * 2,
    )


def split_part_body(frames, *refs):
    place, row = refs[0][0], refs[1][0]
    blocks = refs[2 : 2 + frames]
    keep, send, whole = refs[2 + frames :]
    size = keep.shape[1] // frames
    half, inner = place_in_half(row, frames)
    for s in range(frames):
        for late in range(2):
            piece = piece_of(lax.rem(place + s, frames), late, row, frames)
            whole[:, lane_block(piece, size)] = blocks[s][0, :, late * size : (late + 1) * size]
    for j in range(frames):
        spot = jnp.bitwise_xor(inner, j)
        at = slice(j * size, (j + 1) * size)
        keep[:, at] = whole[:, lane_block(half * frames + spot, size)]
        send[:, at] = whole[:, lane_block((1 - half) * frames + spot, size)]


def split_part(place, row, blocks):
    frames = len(blocks)
    _, tokens, width = blocks[0].shape
    shape = jax.ShapeDtypeStruct((tokens, frames * width // 2), BF16)
    return call(
        functools.partial(split_part_body, frames),
        [shape, shape],
        [place, row, *blocks],
        smem=2,
        scratch=[pltpu.VMEM((tokens, width * frames), BF16)],
    )


def exchange(blocks, sign):
    frames = len(blocks)

    def shift(s):
        return [(i, (i + sign * s) % frames) for i in range(frames)]

    return [blocks[0]] + [lax.ppermute(blocks[s], "frame", shift(s)) for s in range(1, frames)]


def swap(x, bit):
    group = lax.axis_size("dp")
    return lax.ppermute(x, "dp", [(i, i ^ bit) for i in range(group)])


def gather_half(out_weight, count):
    weights = {0: out_weight}
    bit = count // 2
    while bit:
        for j in list(weights):
            weights[j ^ bit] = swap(weights[j], bit)
        bit //= 2
    return [weights[j] for j in range(count)]


def finish_body(pieces, *refs):
    own = refs[:pieces]
    other = refs[pieces : 2 * pieces]
    scales = refs[2 * pieces : -2]
    out, scale_out = refs[-2:]
    start = 0
    for mine, theirs in zip(own, other):
        at = slice(start, start + mine.shape[1])
        out[:, at] = (mine[...] + theirs[...].astype(F32)).astype(BF16)
        start = at.stop
    total = functools.reduce(jnp.add, [s[...] for s in scales])
    scale_out[...] = total[:, : scale_out.shape[1]]


def finish(own, other, scales, heads):
    tokens = own[0].shape[0]
    model = sum(o.shape[1] for o in own)
    return call(
        functools.partial(finish_body, len(own)),
        [jax.ShapeDtypeStruct((tokens, model), BF16), jax.ShapeDtypeStruct((1, heads), F32)],
        [*own, *other, *scales],
    )


def local_split(queries, key_states, value_states, head_scale, out_weight, frame_pattern, out_grad):
    frames = lax.axis_size("frame")
    group = lax.axis_size("dp")
    tokens, full = queries.shape[2:]
    model = out_grad.shape[3]
    heads = full // HDH
    place = lax.axis_index("frame").astype(jnp.int32).reshape(1)
    row = lax.axis_index("dp").astype(jnp.int32).reshape(1)

    grad_rows = out_grad[0, 0]
    other_rows = swap(grad_rows, frames)
    weights = gather_half(out_weight, frames)
    early, late = weights[: frames // 2], weights[frames // 2 :]

    sent = split_pack(place, row, [queries[0, 0], key_states[0, 0], value_states[0, 0]], frames)
    blocks = exchange(sent, 1)

    mine, theirs = context_grads(grad_rows, other_rows, early, [frame_pattern])
    other = swap(theirs, frames)
    sent = split_join(place, row, [mine], [other], frames)
    grads_early = exchange(sent, 1)
    mine, other = [], []
    for i, weight in enumerate(late):
        last = i == len(late) - 1
        own, theirs = context_grads(grad_rows, other_rows, [weight])
        mine.append(own)
        other.append(swap(theirs, frames))
    context = forward(place, row, head_scale, frame_pattern, blocks, True)
    context = exchange(context, -1)
    sent = split_join(place, row, mine, other, frames)
    grads_late = exchange(sent, 1)

    sent, scale_early = backward(
        place, row, head_scale, frame_pattern, blocks, grads_early, 0
    )
    done_early = exchange(sent, -1)
    sent, scale_part = backward(
        place, row, head_scale, frame_pattern, blocks, grads_late, 1, [scale_early]
    )
    done_late = exchange(sent, -1)

    keep, send = split_part(place, row, context)
    taken = swap(send, frames)
    cut = model // 2 // LANES * LANES
    own_first, theirs = project_pair(keep, taken, weights, 0, cut)
    first = swap(theirs, frames)
    own_last, theirs = project_pair(keep, taken, weights, cut, model)
    last = swap(theirs, frames)
    bit = group // 2
    while bit:
        scale_part = scale_part + swap(scale_part, bit)
        bit //= 2
    scale_parts = exchange([scale_part] * frames, 1)

    partly = scatter(place, row, done_early, 0, full, [])
    attended, scale_sum = finish([own_first, own_last], [first, last], scale_parts, heads)
    query_grad, key_grad, value_grad = scatter(place, row, done_late, 1, full, partly)
    shape = (1, 1, tokens, full)
    return (
        attended.reshape(1, 1, tokens, model),
        query_grad.reshape(shape),
        key_grad.reshape(shape),
        value_grad.reshape(shape),
        scale_sum[0, :heads],
    )


def local_plain(queries, key_states, value_states, head_scale, out_weight, frame_pattern, out_grad):
    frames = lax.axis_size("frame")
    group = lax.axis_size("dp")
    tokens, full = queries.shape[2:]
    model = out_grad.shape[3]
    heads = full // HDH
    count = group // 2
    size = out_weight.shape[0]
    place = lax.axis_index("frame").astype(jnp.int32).reshape(1)
    row = lax.axis_index("dp").astype(jnp.int32).reshape(1)

    grad_rows = out_grad[0, 0]
    other_rows = swap(grad_rows, count)
    weights = gather_half(out_weight, count)
    early, late = weights[: count // 2], weights[count // 2 :]
    names = (list(range(count // 2)), list(range(count // 2, count)))

    sent = pack(place, [queries[0, 0], key_states[0, 0], value_states[0, 0]], frames)
    blocks = exchange(sent, 1)
    context = exchange(forward(place, row, head_scale, frame_pattern, blocks), -1)
    mine, other = [], []
    for part_weights in (early, late):
        own, theirs = context_grads(grad_rows, other_rows, part_weights)
        mine.append(own)
        other.append(swap(theirs, count))
    sent = join(place, row, mine, other, names, size, frames, full)
    grads = exchange(sent, 1)

    keep, send = part(place, row, context, count, size)
    own, theirs = project_pair(keep, swap(send, count), weights)
    attended = (own + swap(theirs, count)).astype(BF16)

    sent, scale_part = backward(place, row, head_scale, frame_pattern, blocks, grads)
    blocks = exchange(sent, -1)
    bit = group // 2
    while bit:
        scale_part = scale_part + swap(scale_part, bit)
        bit //= 2
    scale_sum = functools.reduce(jnp.add, exchange([scale_part] * frames, 1))
    query_grad, key_grad, value_grad = unpack(place, blocks, frames)
    shape = (1, 1, tokens, full)
    return (
        attended.reshape(1, 1, tokens, model),
        query_grad.reshape(shape),
        key_grad.reshape(shape),
        value_grad.reshape(shape),
        scale_sum[0, :heads],
    )


def local(*args):
    frames = lax.axis_size("frame")
    size = args[4].shape[0]
    if lax.axis_size("dp") == 2 * frames and size % HDH == 0:
        return local_split(*args)
    return local_plain(*args)


def solution(mesh):
    spec = P("dp", "frame", None, None)
    return jax.shard_map(
        local,
        mesh=mesh,
        in_specs=(spec, spec, spec, P(), P("dp", None), P(), spec),
        out_specs=(spec, spec, spec, spec, P()),
        check_vma=False,
    )
```

```python
import functools
import math

import jax
import jax.numpy as jnp
from jax import lax
from jax.experimental import pallas as pl
from jax.experimental.pallas import tpu as pltpu
from jax.sharding import PartitionSpec as P


HDH = 128
LANES = 128
LOG2E = 1.0 / math.log(2.0)


F32 = jnp.float32
BF16 = jnp.bfloat16
NT = (((1,), (1,)), ((), ()))
NN = (((1,), (0,)), ((), ()))
TN = (((0,), (0,)), ((), ()))
SMEM = pl.BlockSpec(memory_space=pltpu.SMEM)
VMEM = pl.BlockSpec(memory_space=pltpu.VMEM)


def dot(a, b, dims):
    return lax.dot_general(a, b, dims, preferred_element_type=F32)


def lane_block(index, width):
    return pl.ds(pl.multiple_of(index * width, LANES), width)


def call(body, outs, operands, smem=0, scratch=()):
    return pl.pallas_call(
        body,
        out_shape=outs,
        in_specs=[SMEM] * smem + [VMEM] * (len(operands) - smem),
        out_specs=[VMEM] * len(outs),
        scratch_shapes=list(scratch),
    )(*operands)


def pack_body(frames, width, count, *refs):
    place = refs[0][0]
    sources = refs[1 : 1 + count]
    outs = refs[1 + count :]
    for s in range(frames):
        target = lax.rem(place + s, frames)
        for i in range(count):
            outs[s][i] = sources[i][:, lane_block(target, width)]


def pack(place, sources, frames):
    tokens, full = sources[0].shape
    width = full // frames
    shape = jax.ShapeDtypeStruct((len(sources), tokens, width), BF16)
    return call(
        functools.partial(pack_body, frames, width, len(sources)),
        [shape] * frames,
        [place, *sources],
        smem=1,
    )


def unpack_body(frames, width, count, *refs):
    place = refs[0][0]
    blocks = refs[1 : 1 + frames]
    outs = refs[1 + frames :]
    for s in range(frames):
        source = lax.rem(place + s, frames)
        for i in range(count):
            outs[i][:, lane_block(source, width)] = blocks[s][i]


def unpack(place, blocks, frames):
    count, tokens, width = blocks[0].shape
    shape = jax.ShapeDtypeStruct((tokens, width * frames), BF16)
    return call(
        functools.partial(unpack_body, frames, width, count),
        [shape] * count,
        [place, *blocks],
        smem=1,
    )


def piece_of(target, late, row, frames):
    quarter = frames // 2
    inner = lax.rem(row, frames)
    far = jnp.bitwise_xor(lax.div(inner, quarter), late)
    return lax.div(target, quarter) * frames + far * quarter + lax.rem(target, quarter)


def both(parts):
    return jnp.concatenate(parts, axis=0)


def softmax_rows(query, keys, factor):
    plain = dot(keys, query, NT)
    top = jnp.max(plain, axis=0, keepdims=True)
    raised = jnp.exp2((plain - top) * (factor * LOG2E))
    total = jnp.sum(raised, axis=0, keepdims=True)
    return plain, raised * (1.0 / total)


def head_numbers(place, row, heads, split, frames):
    if not split:
        return [place * heads + h for h in range(heads)]
    each = heads // 2
    pieces = [piece_of(place, late, row, frames) for late in range(2)]
    return [pieces[h // each] * each + h % each for h in range(heads)]


def factors_of(place, row, scale_ref, heads, split, frames):
    inv_root = 1.0 / math.sqrt(HDH)
    return [scale_ref[n] * inv_root for n in head_numbers(place, row, heads, split, frames)]


def forward_body(frames, heads, slots, split, *refs):
    place_ref, row_ref, scale_ref, pattern_ref = refs[:4]
    blocks = refs[4 : 4 + frames]
    outs = refs[4 + frames : 4 + 2 * frames]
    held = refs[-1]
    place = place_ref[0]
    factors = factors_of(place, row_ref[0], scale_ref, heads, split, frames)
    for s in range(frames):
        frame = lax.rem(place + frames - s, frames)
        held[frame] = blocks[s][1:3]
    for s in range(frames):
        frame = lax.rem(place + frames - s, frames)
        chosen = [pattern_ref[frame, j] for j in range(slots)]
        for h in range(heads):
            at = slice(h * HDH, (h + 1) * HDH)
            keys = both([held[g, 0, :, at] for g in chosen])
            values = both([held[g, 1, :, at] for g in chosen])
            _, probs = softmax_rows(blocks[s][0, :, at], keys, factors[h])
            outs[s][0, :, at] = dot(probs.astype(BF16), values, TN).astype(BF16)


def forward(place, row, scale, pattern, blocks, split=False):
    frames = len(blocks)
    _, tokens, width = blocks[0].shape
    shape = jax.ShapeDtypeStruct((1, tokens, width), BF16)
    return call(
        functools.partial(forward_body, frames, width // HDH, pattern.shape[1], split),
        [shape] * frames,
        [place, row, scale, pattern, *blocks],
        smem=4,
        scratch=[pltpu.VMEM((frames, 2, tokens, width), BF16)],
    )


def backward_body(frames, heads, slots, half, before, *refs):
    place_ref, row_ref, scale_ref, pattern_ref = refs[:4]
    earlier = refs[4 : 4 + before]
    refs = refs[4 + before :]
    blocks = refs[:frames]
    grads = refs[frames : 2 * frames]
    outs = refs[2 * frames : 3 * frames]
    scale_out = refs[3 * frames]
    held, key_sum, value_sum = refs[3 * frames + 1 :]
    place = place_ref[0]
    tokens = tokens_of(blocks)
    inv_root = 1.0 / math.sqrt(HDH)
    if half is None:
        base = 0
        numbers = head_numbers(place, row_ref[0], heads, False, frames)
    else:
        base = half * heads * HDH
        numbers = head_numbers(place, row_ref[0], 2 * heads, True, frames)
        numbers = numbers[half * heads : (half + 1) * heads]
    factors = [scale_ref[n] * inv_root for n in numbers]
    part = slice(base, base + heads * HDH)
    key_sum[...] = jnp.zeros_like(key_sum)
    value_sum[...] = jnp.zeros_like(value_sum)
    for s in range(frames):
        frame = lax.rem(place + frames - s, frames)
        held[frame] = blocks[s][1:3, :, part]
    terms = [jnp.zeros((1, tokens), F32) for _ in range(heads)]
    for s in range(frames):
        frame = lax.rem(place + frames - s, frames)
        chosen = [pattern_ref[frame, j] for j in range(slots)]
        for h in range(heads):
            at = slice(h * HDH, (h + 1) * HDH)
            query = blocks[s][0, :, base + h * HDH : base + (h + 1) * HDH]
            grad = grads[s][0, :, at]
            keys = both([held[g, 0, :, at] for g in chosen])
            values = both([held[g, 1, :, at] for g in chosen])
            plain, probs = softmax_rows(query, keys, factors[h])
            prob_grads = dot(values, grad, NT)
            weighted = jnp.sum(prob_grads * probs, axis=0, keepdims=True)
            score_grads = probs * (prob_grads - weighted)
            terms[h] = terms[h] + jnp.sum(score_grads * plain, axis=0, keepdims=True)
            low = score_grads.astype(BF16)
            outs[s][0, :, at] = (dot(low, keys, TN) * factors[h]).astype(BF16)
            key_part = dot(low, query, NN)
            value_part = dot(probs.astype(BF16), grad, NN)
            for j, g in enumerate(chosen):
                rows = slice(j * tokens, (j + 1) * tokens)
                key_sum[g, :, at] += key_part[rows]
                value_sum[g, :, at] += value_part[rows]
    for s in range(frames):
        frame = lax.rem(place + frames - s, frames)
        for h in range(heads):
            at = slice(h * HDH, (h + 1) * HDH)
            outs[s][1, :, at] = (key_sum[frame, :, at] * factors[h]).astype(BF16)
        outs[s][2] = value_sum[frame].astype(BF16)
    lanes = lax.broadcasted_iota(jnp.int32, scale_out.shape, 1)
    result = earlier[0][...] if before else jnp.zeros(scale_out.shape, F32)
    for h in range(heads):
        term = jnp.sum(terms[h], axis=1, keepdims=True) * inv_root
        result = result + jnp.where(lanes == numbers[h], term, 0.0)
    scale_out[...] = result


def tokens_of(blocks):
    return blocks[0].shape[1]


def backward(place, row, scale, pattern, blocks, grads, half=None, before=()):
    frames = len(blocks)
    _, tokens, width = grads[0].shape
    shape = jax.ShapeDtypeStruct((3, tokens, width), BF16)
    result = call(
        functools.partial(
            backward_body, frames, width // HDH, pattern.shape[1], half, len(before)
        ),
        [shape] * frames + [jax.ShapeDtypeStruct((1, LANES), F32)],
        [place, row, scale, pattern, *before, *blocks, *grads],
        smem=4,
        scratch=[
            pltpu.VMEM((frames, 2, tokens, width), BF16),
            pltpu.VMEM((frames, tokens, width), F32),
            pltpu.VMEM((frames, tokens, width), F32),
        ],
    )
    return result[:frames], result[frames]


def context_grad_body(skip, count, cut, *refs):
    refs = refs[skip:]
    mine, other = refs[:2]
    weights = refs[2 : 2 + count]
    mine_out, other_out = refs[2 + count : 4 + count]
    tokens = mine.shape[0]
    rows = both([other[...], mine[...]])
    start = 0
    for w in weights:
        at = slice(start, start + w.shape[0])
        result = dot(rows, w[...], NT).astype(BF16)
        other_out[:, at] = result[:tokens]
        mine_out[:, at] = result[tokens:]
        start += w.shape[0]
    if cut:
        refs[4 + count][...] = weights[0][:cut]
        refs[5 + count][...] = weights[0][cut:]


def context_grads(mine, other, weights, scalars=(), cut=0):
    tokens = mine.shape[0]
    features = sum(w.shape[0] for w in weights)
    shapes = [jax.ShapeDtypeStruct((tokens, features), BF16)] * 2
    if cut:
        size, model = weights[0].shape
        shapes += [jax.ShapeDtypeStruct((n, model), BF16) for n in (cut, size - cut)]
    return call(
        functools.partial(context_grad_body, len(scalars), len(weights), cut),
        shapes,
        [*scalars, mine, other, *weights],
        smem=len(scalars),
    )


def project_body(count, columns, *refs):
    mine, other = refs[:2]
    weights = refs[2 : 2 + count]
    mine_out, other_out = refs[2 + count :]
    tokens = mine.shape[0]
    rows = both([other[...], mine[...]])
    start = 0
    total = None
    for w in weights:
        part = dot(rows[:, start : start + w.shape[0]], w[:, columns], NN)
        total = part if total is None else total + part
        start += w.shape[0]
    other_out[...] = total[:tokens].astype(other_out.dtype)
    mine_out[...] = total[tokens:]


def project_pair(mine, other, weights, first=0, last=None):
    tokens, _ = mine.shape
    columns = slice(first, weights[0].shape[1] if last is None else last)
    width = columns.stop - columns.start
    return call(
        functools.partial(project_body, len(weights), columns),
        [jax.ShapeDtypeStruct((tokens, width), kind) for kind in (F32, BF16)],
        [mine, other, *weights],
    )


def place_in_half(row, group):
    half = lax.div(row, group)
    return half, row - half * group


def join_body(frames, pieces, size, *refs):
    place = refs[0][0]
    half, inner = place_in_half(refs[1][0], sum(len(p) for p in pieces))
    count = len(pieces)
    mine = refs[2 : 2 + count]
    other = refs[2 + count : 2 + 2 * count]
    outs = refs[2 + 2 * count : 2 + 2 * count + frames]
    whole = refs[-1]
    group = sum(len(p) for p in pieces)
    width = whole.shape[1] // frames
    for h, sources in ((half, mine), (1 - half, other)):
        for source, names in zip(sources, pieces):
            for k, j in enumerate(names):
                spot = h * group + jnp.bitwise_xor(inner, j)
                whole[:, lane_block(spot, size)] = source[:, k * size : (k + 1) * size]
    for s in range(frames):
        outs[s][0] = whole[:, lane_block(lax.rem(place + s, frames), width)]


def join(place, row, mine, other, pieces, size, frames, full):
    tokens = mine[0].shape[0]
    if size % LANES == 0:
        shape = jax.ShapeDtypeStruct((1, tokens, full // frames), BF16)
        return call(
            functools.partial(join_body, frames, pieces, size),
            [shape] * frames,
            [place, row, *mine, *other],
            smem=2,
            scratch=[pltpu.VMEM((tokens, full), BF16)],
        )
    group = sum(len(p) for p in pieces)
    whole = jnp.zeros((tokens, full), BF16)
    half, inner = place_in_half(row[0], group)
    for h, sources in ((half, mine), (1 - half, other)):
        for source, names in zip(sources, pieces):
            for k, j in enumerate(names):
                spot = h * group + jnp.bitwise_xor(inner, j)
                piece = source[:, k * size : (k + 1) * size]
                whole = lax.dynamic_update_slice(whole, piece, (0, spot * size))
    return pack(place, [whole], frames)


def part_body(frames, count, size, *refs):
    place = refs[0][0]
    half, inner = place_in_half(refs[1][0], count)
    blocks = refs[2 : 2 + frames]
    keep, send, whole = refs[2 + frames :]
    width = whole.shape[1] // frames
    for s in range(frames):
        whole[:, lane_block(lax.rem(place + s, frames), width)] = blocks[s][0]
    for j in range(count):
        spot = jnp.bitwise_xor(inner, j)
        at = slice(j * size, (j + 1) * size)
        keep[:, at] = whole[:, lane_block(half * count + spot, size)]
        send[:, at] = whole[:, lane_block((1 - half) * count + spot, size)]


def part(place, row, blocks, count, size):
    frames = len(blocks)
    _, tokens, width = blocks[0].shape
    if size % LANES == 0:
        shape = jax.ShapeDtypeStruct((tokens, count * size), BF16)
        return call(
            functools.partial(part_body, frames, count, size),
            [shape, shape],
            [place, row, *blocks],
            smem=2,
            scratch=[pltpu.VMEM((tokens, width * frames), BF16)],
        )
    whole = unpack(place, blocks, frames)[0]
    half, inner = place_in_half(row[0], count)

    def half_of(h):
        spots = [h * count + jnp.bitwise_xor(inner, j) for j in range(count)]
        return jnp.concatenate(
            [lax.dynamic_slice_in_dim(whole, spot * size, size, axis=1) for spot in spots], axis=1
        )

    return half_of(half), half_of(1 - half)


def split_pack_body(frames, count, *refs):
    place, row = refs[0][0], refs[1][0]
    sources = refs[2 : 2 + count]
    outs = refs[2 + count :]
    size = outs[0].shape[2] // 2
    for s in range(frames):
        target = lax.rem(place + s, frames)
        for late in range(2):
            piece = piece_of(target, late, row, frames)
            for i in range(count):
                at = slice(late * size, (late + 1) * size)
                outs[s][i, :, at] = sources[i][:, lane_block(piece, size)]


def split_pack(place, row, sources, frames):
    tokens, full = sources[0].shape
    shape = jax.ShapeDtypeStruct((len(sources), tokens, full // frames), BF16)
    return call(
        functools.partial(split_pack_body, frames, len(sources)),
        [shape] * frames,
        [place, row, *sources],
        smem=2,
    )


def split_unpack_body(frames, count, *refs):
    place, row = refs[0][0], refs[1][0]
    blocks = (refs[2 : 2 + frames], refs[2 + frames : 2 + 2 * frames])
    outs = refs[2 + 2 * frames :]
    size = blocks[0][0].shape[2]
    for late in range(2):
        for s in range(frames):
            piece = piece_of(lax.rem(place + s, frames), late, row, frames)
            for i in range(count):
                outs[i][:, lane_block(piece, size)] = blocks[late][s][i]


def split_unpack(place, row, early, late):
    frames = len(early)
    count, tokens, size = early[0].shape
    shape = jax.ShapeDtypeStruct((tokens, 2 * size * frames), BF16)
    return call(
        functools.partial(split_unpack_body, frames, count),
        [shape] * count,
        [place, row, *early, *late],
        smem=2,
    )


def split_join_body(frames, count, *refs):
    place, row = refs[0][0], refs[1][0]
    mine = refs[2 : 2 + count]
    other = refs[2 + count : 2 + 2 * count]
    outs = refs[2 + 2 * count : 2 + 2 * count + frames]
    own, theirs = refs[2 + 2 * count + frames :]
    quarter = frames // 2
    size = own.shape[1] // quarter
    half, inner = place_in_half(row, frames)
    for sources, whole in ((mine, own), (other, theirs)):
        start = 0
        for source in sources:
            whole[:, start : start + source.shape[1]] = source[...]
            start += source.shape[1]
    for s in range(frames):
        target = lax.rem(place + s, frames)
        near = jnp.bitwise_xor(lax.rem(target, quarter), lax.rem(inner, quarter))
        at = lane_block(near, size)
        outs[s][0] = jnp.where(lax.div(target, quarter) == half, own[:, at], theirs[:, at])


def split_join(place, row, mine, other, frames):
    tokens = mine[0].shape[0]
    width = sum(m.shape[1] for m in mine)
    shape = jax.ShapeDtypeStruct((1, tokens, 2 * width // frames), BF16)
    return call(
        functools.partial(split_join_body, frames, len(mine)),
        [shape] * frames,
        [place, row, *mine, *other],
        smem=2,
        scratch=[pltpu.VMEM((tokens, width), BF16)] * 2,
    )


def split_part_body(frames, *refs):
    place, row = refs[0][0], refs[1][0]
    blocks = refs[2 : 2 + frames]
    keep, send, whole = refs[2 + frames :]
    size = keep.shape[1] // frames
    half, inner = place_in_half(row, frames)
    for s in range(frames):
        for late in range(2):
            piece = piece_of(lax.rem(place + s, frames), late, row, frames)
            whole[:, lane_block(piece, size)] = blocks[s][0, :, late * size : (late + 1) * size]
    for j in range(frames):
        spot = jnp.bitwise_xor(inner, j)
        at = slice(j * size, (j + 1) * size)
        keep[:, at] = whole[:, lane_block(half * frames + spot, size)]
        send[:, at] = whole[:, lane_block((1 - half) * frames + spot, size)]


def split_part(place, row, blocks):
    frames = len(blocks)
    _, tokens, width = blocks[0].shape
    shape = jax.ShapeDtypeStruct((tokens, frames * width // 2), BF16)
    return call(
        functools.partial(split_part_body, frames),
        [shape, shape],
        [place, row, *blocks],
        smem=2,
        scratch=[pltpu.VMEM((tokens, width * frames), BF16)],
    )


def exchange(blocks, sign):
    frames = len(blocks)

    def shift(s):
        return [(i, (i + sign * s) % frames) for i in range(frames)]

    return [blocks[0]] + [lax.ppermute(blocks[s], "frame", shift(s)) for s in range(1, frames)]


def swap(x, bit):
    group = lax.axis_size("dp")
    return lax.ppermute(x, "dp", [(i, i ^ bit) for i in range(group)])


def gather_half(out_weight, count):
    weights = {0: out_weight}
    bit = count // 2
    while bit:
        for j in list(weights):
            weights[j ^ bit] = swap(weights[j], bit)
        bit //= 2
    return [weights[j] for j in range(count)]


def attend_body(counts, *refs):
    contexts = refs[: len(counts)]
    weights = list(refs[len(counts) : -1])
    total = None
    for context, pieces in zip(contexts, counts):
        start = 0
        for chunks in pieces:
            piece = both([weights.pop(0)[...] for _ in range(chunks)])
            part = dot(context[:, start : start + piece.shape[0]], piece, NN)
            total = part if total is None else total + part
            start += piece.shape[0]
    refs[-1][...] = total.astype(BF16)


def attend(contexts, weights):
    tokens, features = contexts[0].shape
    flat = [c for pieces in weights for chunks in pieces for c in chunks]
    width = flat[0].shape[1]
    tile = math.gcd(width, 1024)
    counts = [[len(chunks) for chunks in pieces] for pieces in weights]
    return pl.pallas_call(
        functools.partial(attend_body, counts),
        grid=(width // tile,),
        out_shape=jax.ShapeDtypeStruct((tokens, width), BF16),
        in_specs=[pl.BlockSpec((tokens, features), lambda i: (0, 0))] * len(contexts)
        + [pl.BlockSpec((w.shape[0], tile), lambda i: (0, i)) for w in flat],
        out_specs=pl.BlockSpec((tokens, tile), lambda i: (0, i)),
        name="attend",
    )(*contexts, *flat)


def local_split(queries, key_states, value_states, head_scale, out_weight, frame_pattern, out_grad):
    frames = lax.axis_size("frame")
    group = lax.axis_size("dp")
    tokens, full = queries.shape[2:]
    model = out_grad.shape[3]
    heads = full // HDH
    place = lax.axis_index("frame").astype(jnp.int32).reshape(1)
    row = lax.axis_index("dp").astype(jnp.int32).reshape(1)

    grad_rows = out_grad[0, 0]
    other_rows = swap(grad_rows, frames)
    weights = gather_half(out_weight, frames)
    early, late = weights[: frames // 2], weights[frames // 2 :]
    cut = out_weight.shape[0] * 11 // 16

    sent = split_pack(place, row, [queries[0, 0], key_states[0, 0], value_states[0, 0]], frames)
    blocks = exchange(sent, 1)

    mine, theirs, *chunks = context_grads(
        grad_rows, other_rows, early, [frame_pattern], cut
    )
    other = swap(theirs, frames)
    other_first = swap(chunks[0], frames)
    other_last = swap(chunks[1], frames)
    far_first = swap(other_first, frames // 2)
    far_last = swap(other_last, frames // 2)
    sent = split_join(place, row, [mine], [other], frames)
    grads_early = exchange(sent, 1)
    mine, other = [], []
    for weight in late:
        own, theirs = context_grads(grad_rows, other_rows, [weight])
        mine.append(own)
        other.append(swap(theirs, frames))
    context = forward(place, row, head_scale, frame_pattern, blocks, True)
    context = exchange(context, -1)
    sent = split_join(place, row, mine, other, frames)
    grads_late = exchange(sent, 1)

    sent, scale_early = backward(
        place, row, head_scale, frame_pattern, blocks, grads_early, 0
    )
    done_early = exchange(sent, -1)
    sent, scale_part = backward(
        place, row, head_scale, frame_pattern, blocks, grads_late, 1, [scale_early]
    )
    done_late = exchange(sent, -1)

    contexts = split_part(place, row, context)
    others = {0: [other_first, other_last], frames // 2: [far_first, far_last]}
    bit = frames // 4
    while bit:
        for j in list(others):
            others[j ^ bit] = [swap(c, bit) for c in others[j]]
        bit //= 2
    others = [others[j] for j in range(frames)]
    attended = attend(contexts, [[[w] for w in weights], others])

    bit = group // 2
    while bit:
        scale_part = scale_part + swap(scale_part, bit)
        bit //= 2
    scale_sum = functools.reduce(jnp.add, exchange([scale_part] * frames, 1))

    query_grad, key_grad, value_grad = split_unpack(place, row, done_early, done_late)
    shape = (1, 1, tokens, full)
    return (
        attended.reshape(1, 1, tokens, model),
        query_grad.reshape(shape),
        key_grad.reshape(shape),
        value_grad.reshape(shape),
        scale_sum[0, :heads],
    )


def local_plain(queries, key_states, value_states, head_scale, out_weight, frame_pattern, out_grad):
    frames = lax.axis_size("frame")
    group = lax.axis_size("dp")
    tokens, full = queries.shape[2:]
    model = out_grad.shape[3]
    heads = full // HDH
    count = group // 2
    size = out_weight.shape[0]
    place = lax.axis_index("frame").astype(jnp.int32).reshape(1)
    row = lax.axis_index("dp").astype(jnp.int32).reshape(1)

    grad_rows = out_grad[0, 0]
    other_rows = swap(grad_rows, count)
    weights = gather_half(out_weight, count)
    early, late = weights[: count // 2], weights[count // 2 :]
    names = (list(range(count // 2)), list(range(count // 2, count)))

    sent = pack(place, [queries[0, 0], key_states[0, 0], value_states[0, 0]], frames)
    blocks = exchange(sent, 1)
    context = exchange(forward(place, row, head_scale, frame_pattern, blocks), -1)
    mine, other = [], []
    for part_weights in (early, late):
        own, theirs = context_grads(grad_rows, other_rows, part_weights)
        mine.append(own)
        other.append(swap(theirs, count))
    sent = join(place, row, mine, other, names, size, frames, full)
    grads = exchange(sent, 1)

    keep, send = part(place, row, context, count, size)
    own, theirs = project_pair(keep, swap(send, count), weights)
    attended = (own + swap(theirs, count)).astype(BF16)

    sent, scale_part = backward(place, row, head_scale, frame_pattern, blocks, grads)
    blocks = exchange(sent, -1)
    bit = group // 2
    while bit:
        scale_part = scale_part + swap(scale_part, bit)
        bit //= 2
    scale_sum = functools.reduce(jnp.add, exchange([scale_part] * frames, 1))
    query_grad, key_grad, value_grad = unpack(place, blocks, frames)
    shape = (1, 1, tokens, full)
    return (
        attended.reshape(1, 1, tokens, model),
        query_grad.reshape(shape),
        key_grad.reshape(shape),
        value_grad.reshape(shape),
        scale_sum[0, :heads],
    )


def local(*args):
    frames = lax.axis_size("frame")
    size = args[4].shape[0]
    if lax.axis_size("dp") == 2 * frames and size % HDH == 0:
        return local_split(*args)
    return local_plain(*args)


def solution(mesh):
    spec = P("dp", "frame", None, None)
    return jax.shard_map(
        local,
        mesh=mesh,
        in_specs=(spec, spec, spec, P(), P("dp", None), P(), spec),
        out_specs=(spec, spec, spec, spec, P()),
        check_vma=False,
    )
```

```python
import functools
import math

import jax
import jax.numpy as jnp
from jax import lax
from jax.experimental import pallas as pl
from jax.experimental.pallas import tpu as pltpu
from jax.sharding import PartitionSpec as P


HDH = 128
LANES = 128
LOG2E = 1.0 / math.log(2.0)


F32 = jnp.float32
BF16 = jnp.bfloat16
NT = (((1,), (1,)), ((), ()))
NN = (((1,), (0,)), ((), ()))
TN = (((0,), (0,)), ((), ()))
SMEM = pl.BlockSpec(memory_space=pltpu.SMEM)
VMEM = pl.BlockSpec(memory_space=pltpu.VMEM)


def dot(a, b, dims):
    return lax.dot_general(a, b, dims, preferred_element_type=F32)


def lane_block(index, width):
    return pl.ds(pl.multiple_of(index * width, LANES), width)


def call(body, outs, operands, smem=0, scratch=()):
    return pl.pallas_call(
        body,
        out_shape=outs,
        in_specs=[SMEM] * smem + [VMEM] * (len(operands) - smem),
        out_specs=[VMEM] * len(outs),
        scratch_shapes=list(scratch),
    )(*operands)


def pack_body(frames, width, count, *refs):
    place = refs[0][0]
    sources = refs[1 : 1 + count]
    outs = refs[1 + count :]
    for s in range(frames):
        target = lax.rem(place + s, frames)
        for i in range(count):
            outs[s][i] = sources[i][:, lane_block(target, width)]


def pack(place, sources, frames):
    tokens, full = sources[0].shape
    width = full // frames
    shape = jax.ShapeDtypeStruct((len(sources), tokens, width), BF16)
    return call(
        functools.partial(pack_body, frames, width, len(sources)),
        [shape] * frames,
        [place, *sources],
        smem=1,
    )


def unpack_body(frames, width, count, *refs):
    place = refs[0][0]
    blocks = refs[1 : 1 + frames]
    outs = refs[1 + frames :]
    for s in range(frames):
        source = lax.rem(place + s, frames)
        for i in range(count):
            outs[i][:, lane_block(source, width)] = blocks[s][i]


def unpack(place, blocks, frames):
    count, tokens, width = blocks[0].shape
    shape = jax.ShapeDtypeStruct((tokens, width * frames), BF16)
    return call(
        functools.partial(unpack_body, frames, width, count),
        [shape] * count,
        [place, *blocks],
        smem=1,
    )


def piece_of(target, late, row, frames):
    quarter = frames // 2
    inner = lax.rem(row, frames)
    far = jnp.bitwise_xor(lax.div(inner, quarter), late)
    return lax.div(target, quarter) * frames + far * quarter + lax.rem(target, quarter)


def both(parts):
    return jnp.concatenate(parts, axis=0)


def softmax_rows(query, keys, factor):
    plain = dot(keys, query, NT)
    top = jnp.max(plain, axis=0, keepdims=True)
    raised = jnp.exp2((plain - top) * (factor * LOG2E))
    total = jnp.sum(raised, axis=0, keepdims=True)
    return plain, raised * (1.0 / total)


def head_numbers(place, row, heads, split, frames):
    if not split:
        return [place * heads + h for h in range(heads)]
    each = heads // 2
    pieces = [piece_of(place, late, row, frames) for late in range(2)]
    return [pieces[h // each] * each + h % each for h in range(heads)]


def factors_of(place, row, scale_ref, heads, split, frames):
    inv_root = 1.0 / math.sqrt(HDH)
    return [scale_ref[n] * inv_root for n in head_numbers(place, row, heads, split, frames)]


def forward_body(frames, heads, slots, split, *refs):
    place_ref, row_ref, scale_ref, pattern_ref = refs[:4]
    blocks = refs[4 : 4 + frames]
    outs = refs[4 + frames : 4 + 2 * frames]
    held = refs[-1]
    place = place_ref[0]
    factors = factors_of(place, row_ref[0], scale_ref, heads, split, frames)
    for s in range(frames):
        frame = lax.rem(place + frames - s, frames)
        held[frame] = blocks[s][1:3]
    for s in range(frames):
        frame = lax.rem(place + frames - s, frames)
        chosen = [pattern_ref[frame, j] for j in range(slots)]
        for h in range(heads):
            at = slice(h * HDH, (h + 1) * HDH)
            keys = both([held[g, 0, :, at] for g in chosen])
            values = both([held[g, 1, :, at] for g in chosen])
            _, probs = softmax_rows(blocks[s][0, :, at], keys, factors[h])
            outs[s][0, :, at] = dot(probs.astype(BF16), values, TN).astype(BF16)


def forward(place, row, scale, pattern, blocks, split=False):
    frames = len(blocks)
    _, tokens, width = blocks[0].shape
    shape = jax.ShapeDtypeStruct((1, tokens, width), BF16)
    return call(
        functools.partial(forward_body, frames, width // HDH, pattern.shape[1], split),
        [shape] * frames,
        [place, row, scale, pattern, *blocks],
        smem=4,
        scratch=[pltpu.VMEM((frames, 2, tokens, width), BF16)],
    )


def backward_body(frames, heads, slots, half, before, *refs):
    place_ref, row_ref, scale_ref, pattern_ref = refs[:4]
    earlier = refs[4 : 4 + before]
    refs = refs[4 + before :]
    blocks = refs[:frames]
    grads = refs[frames : 2 * frames]
    outs = refs[2 * frames : 3 * frames]
    scale_out = refs[3 * frames]
    held, key_sum, value_sum = refs[3 * frames + 1 :]
    place = place_ref[0]
    tokens = tokens_of(blocks)
    inv_root = 1.0 / math.sqrt(HDH)
    if half is None:
        base = 0
        numbers = head_numbers(place, row_ref[0], heads, False, frames)
    else:
        base = half * heads * HDH
        numbers = head_numbers(place, row_ref[0], 2 * heads, True, frames)
        numbers = numbers[half * heads : (half + 1) * heads]
    factors = [scale_ref[n] * inv_root for n in numbers]
    part = slice(base, base + heads * HDH)
    key_sum[...] = jnp.zeros_like(key_sum)
    value_sum[...] = jnp.zeros_like(value_sum)
    for s in range(frames):
        frame = lax.rem(place + frames - s, frames)
        held[frame] = blocks[s][1:3, :, part]
    terms = [jnp.zeros((1, tokens), F32) for _ in range(heads)]
    for s in range(frames):
        frame = lax.rem(place + frames - s, frames)
        chosen = [pattern_ref[frame, j] for j in range(slots)]
        for h in range(heads):
            at = slice(h * HDH, (h + 1) * HDH)
            query = blocks[s][0, :, base + h * HDH : base + (h + 1) * HDH]
            grad = grads[s][0, :, at]
            keys = both([held[g, 0, :, at] for g in chosen])
            values = both([held[g, 1, :, at] for g in chosen])
            plain, probs = softmax_rows(query, keys, factors[h])
            prob_grads = dot(values, grad, NT)
            weighted = jnp.sum(prob_grads * probs, axis=0, keepdims=True)
            score_grads = probs * (prob_grads - weighted)
            terms[h] = terms[h] + jnp.sum(score_grads * plain, axis=0, keepdims=True)
            low = score_grads.astype(BF16)
            outs[s][0, :, at] = (dot(low, keys, TN) * factors[h]).astype(BF16)
            key_part = dot(low, query, NN)
            value_part = dot(probs.astype(BF16), grad, NN)
            for j, g in enumerate(chosen):
                rows = slice(j * tokens, (j + 1) * tokens)
                key_sum[g, :, at] += key_part[rows]
                value_sum[g, :, at] += value_part[rows]
    for s in range(frames):
        frame = lax.rem(place + frames - s, frames)
        for h in range(heads):
            at = slice(h * HDH, (h + 1) * HDH)
            outs[s][1, :, at] = (key_sum[frame, :, at] * factors[h]).astype(BF16)
        outs[s][2] = value_sum[frame].astype(BF16)
    lanes = lax.broadcasted_iota(jnp.int32, scale_out.shape, 1)
    result = earlier[0][...] if before else jnp.zeros(scale_out.shape, F32)
    for h in range(heads):
        term = jnp.sum(terms[h], axis=1, keepdims=True) * inv_root
        result = result + jnp.where(lanes == numbers[h], term, 0.0)
    scale_out[...] = result


def tokens_of(blocks):
    return blocks[0].shape[1]


def backward(place, row, scale, pattern, blocks, grads, half=None, before=()):
    frames = len(blocks)
    _, tokens, width = grads[0].shape
    shape = jax.ShapeDtypeStruct((3, tokens, width), BF16)
    result = call(
        functools.partial(
            backward_body, frames, width // HDH, pattern.shape[1], half, len(before)
        ),
        [shape] * frames + [jax.ShapeDtypeStruct((1, LANES), F32)],
        [place, row, scale, pattern, *before, *blocks, *grads],
        smem=4,
        scratch=[
            pltpu.VMEM((frames, 2, tokens, width), BF16),
            pltpu.VMEM((frames, tokens, width), F32),
            pltpu.VMEM((frames, tokens, width), F32),
        ],
    )
    return result[:frames], result[frames]


def context_grad_body(skip, count, cut, *refs):
    refs = refs[skip:]
    mine, other = refs[:2]
    weights = refs[2 : 2 + count]
    mine_out, other_out = refs[2 + count : 4 + count]
    tokens = mine.shape[0]
    rows = both([other[...], mine[...]])
    start = 0
    for w in weights:
        at = slice(start, start + w.shape[0])
        result = dot(rows, w[...], NT).astype(BF16)
        other_out[:, at] = result[:tokens]
        mine_out[:, at] = result[tokens:]
        start += w.shape[0]
    if cut:
        refs[4 + count][...] = weights[0][:cut]
        refs[5 + count][...] = weights[0][cut:]


def context_grads(mine, other, weights, scalars=(), cut=0):
    tokens = mine.shape[0]
    features = sum(w.shape[0] for w in weights)
    shapes = [jax.ShapeDtypeStruct((tokens, features), BF16)] * 2
    if cut:
        size, model = weights[0].shape
        shapes += [jax.ShapeDtypeStruct((n, model), BF16) for n in (cut, size - cut)]
    return call(
        functools.partial(context_grad_body, len(scalars), len(weights), cut),
        shapes,
        [*scalars, mine, other, *weights],
        smem=len(scalars),
    )


def project_body(count, columns, *refs):
    mine, other = refs[:2]
    weights = refs[2 : 2 + count]
    mine_out, other_out = refs[2 + count :]
    tokens = mine.shape[0]
    rows = both([other[...], mine[...]])
    start = 0
    total = None
    for w in weights:
        part = dot(rows[:, start : start + w.shape[0]], w[:, columns], NN)
        total = part if total is None else total + part
        start += w.shape[0]
    other_out[...] = total[:tokens].astype(other_out.dtype)
    mine_out[...] = total[tokens:]


def project_pair(mine, other, weights, first=0, last=None):
    tokens, _ = mine.shape
    columns = slice(first, weights[0].shape[1] if last is None else last)
    width = columns.stop - columns.start
    return call(
        functools.partial(project_body, len(weights), columns),
        [jax.ShapeDtypeStruct((tokens, width), kind) for kind in (F32, BF16)],
        [mine, other, *weights],
    )


def place_in_half(row, group):
    half = lax.div(row, group)
    return half, row - half * group


def join_body(frames, pieces, size, *refs):
    place = refs[0][0]
    half, inner = place_in_half(refs[1][0], sum(len(p) for p in pieces))
    count = len(pieces)
    mine = refs[2 : 2 + count]
    other = refs[2 + count : 2 + 2 * count]
    outs = refs[2 + 2 * count : 2 + 2 * count + frames]
    whole = refs[-1]
    group = sum(len(p) for p in pieces)
    width = whole.shape[1] // frames
    for h, sources in ((half, mine), (1 - half, other)):
        for source, names in zip(sources, pieces):
            for k, j in enumerate(names):
                spot = h * group + jnp.bitwise_xor(inner, j)
                whole[:, lane_block(spot, size)] = source[:, k * size : (k + 1) * size]
    for s in range(frames):
        outs[s][0] = whole[:, lane_block(lax.rem(place + s, frames), width)]


def join(place, row, mine, other, pieces, size, frames, full):
    tokens = mine[0].shape[0]
    if size % LANES == 0:
        shape = jax.ShapeDtypeStruct((1, tokens, full // frames), BF16)
        return call(
            functools.partial(join_body, frames, pieces, size),
            [shape] * frames,
            [place, row, *mine, *other],
            smem=2,
            scratch=[pltpu.VMEM((tokens, full), BF16)],
        )
    group = sum(len(p) for p in pieces)
    whole = jnp.zeros((tokens, full), BF16)
    half, inner = place_in_half(row[0], group)
    for h, sources in ((half, mine), (1 - half, other)):
        for source, names in zip(sources, pieces):
            for k, j in enumerate(names):
                spot = h * group + jnp.bitwise_xor(inner, j)
                piece = source[:, k * size : (k + 1) * size]
                whole = lax.dynamic_update_slice(whole, piece, (0, spot * size))
    return pack(place, [whole], frames)


def part_body(frames, count, size, *refs):
    place = refs[0][0]
    half, inner = place_in_half(refs[1][0], count)
    blocks = refs[2 : 2 + frames]
    keep, send, whole = refs[2 + frames :]
    width = whole.shape[1] // frames
    for s in range(frames):
        whole[:, lane_block(lax.rem(place + s, frames), width)] = blocks[s][0]
    for j in range(count):
        spot = jnp.bitwise_xor(inner, j)
        at = slice(j * size, (j + 1) * size)
        keep[:, at] = whole[:, lane_block(half * count + spot, size)]
        send[:, at] = whole[:, lane_block((1 - half) * count + spot, size)]


def part(place, row, blocks, count, size):
    frames = len(blocks)
    _, tokens, width = blocks[0].shape
    if size % LANES == 0:
        shape = jax.ShapeDtypeStruct((tokens, count * size), BF16)
        return call(
            functools.partial(part_body, frames, count, size),
            [shape, shape],
            [place, row, *blocks],
            smem=2,
            scratch=[pltpu.VMEM((tokens, width * frames), BF16)],
        )
    whole = unpack(place, blocks, frames)[0]
    half, inner = place_in_half(row[0], count)

    def half_of(h):
        spots = [h * count + jnp.bitwise_xor(inner, j) for j in range(count)]
        return jnp.concatenate(
            [lax.dynamic_slice_in_dim(whole, spot * size, size, axis=1) for spot in spots], axis=1
        )

    return half_of(half), half_of(1 - half)


def split_pack_body(frames, count, *refs):
    place, row = refs[0][0], refs[1][0]
    sources = refs[2 : 2 + count]
    outs = refs[2 + count :]
    size = outs[0].shape[2] // 2
    for s in range(frames):
        target = lax.rem(place + s, frames)
        for late in range(2):
            piece = piece_of(target, late, row, frames)
            for i in range(count):
                at = slice(late * size, (late + 1) * size)
                outs[s][i, :, at] = sources[i][:, lane_block(piece, size)]


def split_pack(place, row, sources, frames):
    tokens, full = sources[0].shape
    shape = jax.ShapeDtypeStruct((len(sources), tokens, full // frames), BF16)
    return call(
        functools.partial(split_pack_body, frames, len(sources)),
        [shape] * frames,
        [place, row, *sources],
        smem=2,
    )


def split_unpack_body(frames, count, *refs):
    place, row = refs[0][0], refs[1][0]
    blocks = (refs[2 : 2 + frames], refs[2 + frames : 2 + 2 * frames])
    scales = refs[2 + 2 * frames : 2 + 3 * frames]
    outs = refs[2 + 3 * frames : -1]
    size = blocks[0][0].shape[2]
    for late in range(2):
        for s in range(frames):
            piece = piece_of(lax.rem(place + s, frames), late, row, frames)
            for i in range(count):
                outs[i][:, lane_block(piece, size)] = blocks[late][s][i]
    total = functools.reduce(jnp.add, [s[...] for s in scales])
    refs[-1][...] = total[:, : refs[-1].shape[1]]


def split_unpack(place, row, early, late, scales, heads):
    frames = len(early)
    count, tokens, size = early[0].shape
    shape = jax.ShapeDtypeStruct((tokens, 2 * size * frames), BF16)
    return call(
        functools.partial(split_unpack_body, frames, count),
        [shape] * count + [jax.ShapeDtypeStruct((1, heads), F32)],
        [place, row, *early, *late, *scales],
        smem=2,
    )


def split_join_body(frames, count, *refs):
    place, row = refs[0][0], refs[1][0]
    mine = refs[2 : 2 + count]
    other = refs[2 + count : 2 + 2 * count]
    outs = refs[2 + 2 * count : 2 + 2 * count + frames]
    own, theirs = refs[2 + 2 * count + frames :]
    quarter = frames // 2
    size = own.shape[1] // quarter
    half, inner = place_in_half(row, frames)
    for sources, whole in ((mine, own), (other, theirs)):
        start = 0
        for source in sources:
            whole[:, start : start + source.shape[1]] = source[...]
            start += source.shape[1]
    for s in range(frames):
        target = lax.rem(place + s, frames)
        near = jnp.bitwise_xor(lax.rem(target, quarter), lax.rem(inner, quarter))
        at = lane_block(near, size)
        outs[s][0] = jnp.where(lax.div(target, quarter) == half, own[:, at], theirs[:, at])


def split_join(place, row, mine, other, frames):
    tokens = mine[0].shape[0]
    width = sum(m.shape[1] for m in mine)
    shape = jax.ShapeDtypeStruct((1, tokens, 2 * width // frames), BF16)
    return call(
        functools.partial(split_join_body, frames, len(mine)),
        [shape] * frames,
        [place, row, *mine, *other],
        smem=2,
        scratch=[pltpu.VMEM((tokens, width), BF16)] * 2,
    )


def split_part_body(frames, *refs):
    place, row = refs[0][0], refs[1][0]
    blocks = refs[2 : 2 + frames]
    keep, send, whole = refs[2 + frames :]
    size = keep.shape[1] // frames
    half, inner = place_in_half(row, frames)
    for s in range(frames):
        for late in range(2):
            piece = piece_of(lax.rem(place + s, frames), late, row, frames)
            whole[:, lane_block(piece, size)] = blocks[s][0, :, late * size : (late + 1) * size]
    for j in range(frames):
        spot = jnp.bitwise_xor(inner, j)
        at = slice(j * size, (j + 1) * size)
        keep[:, at] = whole[:, lane_block(half * frames + spot, size)]
        send[:, at] = whole[:, lane_block((1 - half) * frames + spot, size)]


def split_part(place, row, blocks):
    frames = len(blocks)
    _, tokens, width = blocks[0].shape
    shape = jax.ShapeDtypeStruct((tokens, frames * width // 2), BF16)
    return call(
        functools.partial(split_part_body, frames),
        [shape, shape],
        [place, row, *blocks],
        smem=2,
        scratch=[pltpu.VMEM((tokens, width * frames), BF16)],
    )


def exchange(blocks, sign):
    frames = len(blocks)

    def shift(s):
        return [(i, (i + sign * s) % frames) for i in range(frames)]

    return [blocks[0]] + [lax.ppermute(blocks[s], "frame", shift(s)) for s in range(1, frames)]


def swap(x, bit):
    group = lax.axis_size("dp")
    return lax.ppermute(x, "dp", [(i, i ^ bit) for i in range(group)])


def gather_half(out_weight, count):
    weights = {0: out_weight}
    bit = count // 2
    while bit:
        for j in list(weights):
            weights[j ^ bit] = swap(weights[j], bit)
        bit //= 2
    return [weights[j] for j in range(count)]


def attend_body(counts, *refs):
    contexts = refs[: len(counts)]
    weights = list(refs[len(counts) : -1])
    total = None
    for context, pieces in zip(contexts, counts):
        start = 0
        for chunks in pieces:
            piece = both([weights.pop(0)[...] for _ in range(chunks)])
            part = dot(context[:, start : start + piece.shape[0]], piece, NN)
            total = part if total is None else total + part
            start += piece.shape[0]
    refs[-1][...] = total.astype(BF16)


def attend(contexts, weights):
    tokens, features = contexts[0].shape
    flat = [c for pieces in weights for chunks in pieces for c in chunks]
    width = flat[0].shape[1]
    tile = math.gcd(width, 1024)
    counts = [[len(chunks) for chunks in pieces] for pieces in weights]
    return pl.pallas_call(
        functools.partial(attend_body, counts),
        grid=(width // tile,),
        out_shape=jax.ShapeDtypeStruct((tokens, width), BF16),
        in_specs=[pl.BlockSpec((tokens, features), lambda i: (0, 0))] * len(contexts)
        + [pl.BlockSpec((w.shape[0], tile), lambda i: (0, i)) for w in flat],
        out_specs=pl.BlockSpec((tokens, tile), lambda i: (0, i)),
        name="attend",
    )(*contexts, *flat)


def local_split(queries, key_states, value_states, head_scale, out_weight, frame_pattern, out_grad):
    frames = lax.axis_size("frame")
    group = lax.axis_size("dp")
    tokens, full = queries.shape[2:]
    model = out_grad.shape[3]
    heads = full // HDH
    place = lax.axis_index("frame").astype(jnp.int32).reshape(1)
    row = lax.axis_index("dp").astype(jnp.int32).reshape(1)

    grad_rows = out_grad[0, 0]
    other_rows = swap(grad_rows, frames)
    weights = gather_half(out_weight, frames)
    early, late = weights[: frames // 2], weights[frames // 2 :]
    cut = out_weight.shape[0] * 11 // 16

    sent = split_pack(place, row, [queries[0, 0], key_states[0, 0], value_states[0, 0]], frames)
    blocks = exchange(sent, 1)

    mine, theirs, *chunks = context_grads(
        grad_rows, other_rows, early, [frame_pattern], cut
    )
    other = swap(theirs, frames)
    other_first = swap(chunks[0], frames)
    other_last = swap(chunks[1], frames)
    far_first = swap(other_first, frames // 2)
    far_last = swap(other_last, frames // 2)
    sent = split_join(place, row, [mine], [other], frames)
    grads_early = exchange(sent, 1)
    mine, other = [], []
    for weight in late:
        own, theirs = context_grads(grad_rows, other_rows, [weight])
        mine.append(own)
        other.append(swap(theirs, frames))
    context = forward(place, row, head_scale, frame_pattern, blocks, True)
    context = exchange(context, -1)
    sent = split_join(place, row, mine, other, frames)
    grads_late = exchange(sent, 1)

    sent, scale_early = backward(
        place, row, head_scale, frame_pattern, blocks, grads_early, 0
    )
    done_early = exchange(sent, -1)
    sent, scale_part = backward(
        place, row, head_scale, frame_pattern, blocks, grads_late, 1, [scale_early]
    )
    done_late = exchange(sent, -1)

    contexts = split_part(place, row, context)
    others = {0: [other_first, other_last], frames // 2: [far_first, far_last]}
    bit = frames // 4
    while bit:
        for j in list(others):
            others[j ^ bit] = [swap(c, bit) for c in others[j]]
        bit //= 2
    others = [others[j] for j in range(frames)]
    attended = attend(contexts, [[[w] for w in weights], others])

    bit = group // 2
    while bit:
        scale_part = scale_part + swap(scale_part, bit)
        bit //= 2
    scales = exchange([scale_part] * frames, 1)

    query_grad, key_grad, value_grad, scale_sum = split_unpack(
        place, row, done_early, done_late, scales, heads
    )
    shape = (1, 1, tokens, full)
    return (
        attended.reshape(1, 1, tokens, model),
        query_grad.reshape(shape),
        key_grad.reshape(shape),
        value_grad.reshape(shape),
        scale_sum[0, :heads],
    )


def local_plain(queries, key_states, value_states, head_scale, out_weight, frame_pattern, out_grad):
    frames = lax.axis_size("frame")
    group = lax.axis_size("dp")
    tokens, full = queries.shape[2:]
    model = out_grad.shape[3]
    heads = full // HDH
    count = group // 2
    size = out_weight.shape[0]
    place = lax.axis_index("frame").astype(jnp.int32).reshape(1)
    row = lax.axis_index("dp").astype(jnp.int32).reshape(1)

    grad_rows = out_grad[0, 0]
    other_rows = swap(grad_rows, count)
    weights = gather_half(out_weight, count)
    early, late = weights[: count // 2], weights[count // 2 :]
    names = (list(range(count // 2)), list(range(count // 2, count)))

    sent = pack(place, [queries[0, 0], key_states[0, 0], value_states[0, 0]], frames)
    blocks = exchange(sent, 1)
    context = exchange(forward(place, row, head_scale, frame_pattern, blocks), -1)
    mine, other = [], []
    for part_weights in (early, late):
        own, theirs = context_grads(grad_rows, other_rows, part_weights)
        mine.append(own)
        other.append(swap(theirs, count))
    sent = join(place, row, mine, other, names, size, frames, full)
    grads = exchange(sent, 1)

    keep, send = part(place, row, context, count, size)
    own, theirs = project_pair(keep, swap(send, count), weights)
    attended = (own + swap(theirs, count)).astype(BF16)

    sent, scale_part = backward(place, row, head_scale, frame_pattern, blocks, grads)
    blocks = exchange(sent, -1)
    bit = group // 2
    while bit:
        scale_part = scale_part + swap(scale_part, bit)
        bit //= 2
    scale_sum = functools.reduce(jnp.add, exchange([scale_part] * frames, 1))
    query_grad, key_grad, value_grad = unpack(place, blocks, frames)
    shape = (1, 1, tokens, full)
    return (
        attended.reshape(1, 1, tokens, model),
        query_grad.reshape(shape),
        key_grad.reshape(shape),
        value_grad.reshape(shape),
        scale_sum[0, :heads],
    )


def local(*args):
    frames = lax.axis_size("frame")
    size = args[4].shape[0]
    if lax.axis_size("dp") == 2 * frames and size % HDH == 0:
        return local_split(*args)
    return local_plain(*args)


def solution(mesh):
    spec = P("dp", "frame", None, None)
    return jax.shard_map(
        local,
        mesh=mesh,
        in_specs=(spec, spec, spec, P(), P("dp", None), P(), spec),
        out_specs=(spec, spec, spec, spec, P()),
        check_vma=False,
    )
```

```python
import functools
import math

import jax
import jax.numpy as jnp
from jax import lax
from jax.experimental import pallas as pl
from jax.experimental.pallas import tpu as pltpu
from jax.sharding import PartitionSpec as P


HDH = 128
LANES = 128
LOG2E = 1.0 / math.log(2.0)


F32 = jnp.float32
BF16 = jnp.bfloat16
NT = (((1,), (1,)), ((), ()))
NN = (((1,), (0,)), ((), ()))
TN = (((0,), (0,)), ((), ()))
SMEM = pl.BlockSpec(memory_space=pltpu.SMEM)
VMEM = pl.BlockSpec(memory_space=pltpu.VMEM)


def dot(a, b, dims):
    return lax.dot_general(a, b, dims, preferred_element_type=F32)


def lane_block(index, width):
    return pl.ds(pl.multiple_of(index * width, LANES), width)


def call(body, outs, operands, smem=0, scratch=()):
    return pl.pallas_call(
        body,
        out_shape=outs,
        in_specs=[SMEM] * smem + [VMEM] * (len(operands) - smem),
        out_specs=[VMEM] * len(outs),
        scratch_shapes=list(scratch),
    )(*operands)


def pack_body(frames, width, count, *refs):
    place = refs[0][0]
    sources = refs[1 : 1 + count]
    outs = refs[1 + count :]
    for s in range(frames):
        target = lax.rem(place + s, frames)
        for i in range(count):
            outs[s][i] = sources[i][:, lane_block(target, width)]


def pack(place, sources, frames):
    tokens, full = sources[0].shape
    width = full // frames
    shape = jax.ShapeDtypeStruct((len(sources), tokens, width), BF16)
    return call(
        functools.partial(pack_body, frames, width, len(sources)),
        [shape] * frames,
        [place, *sources],
        smem=1,
    )


def unpack_body(frames, width, count, *refs):
    place = refs[0][0]
    blocks = refs[1 : 1 + frames]
    outs = refs[1 + frames :]
    for s in range(frames):
        source = lax.rem(place + s, frames)
        for i in range(count):
            outs[i][:, lane_block(source, width)] = blocks[s][i]


def unpack(place, blocks, frames):
    count, tokens, width = blocks[0].shape
    shape = jax.ShapeDtypeStruct((tokens, width * frames), BF16)
    return call(
        functools.partial(unpack_body, frames, width, count),
        [shape] * count,
        [place, *blocks],
        smem=1,
    )


def piece_of(target, late, row, frames):
    quarter = frames // 2
    inner = lax.rem(row, frames)
    far = jnp.bitwise_xor(lax.div(inner, quarter), late)
    return lax.div(target, quarter) * frames + far * quarter + lax.rem(target, quarter)


def both(parts):
    return jnp.concatenate(parts, axis=0)


def softmax_rows(query, keys, factor):
    plain = dot(keys, query, NT)
    top = jnp.max(plain, axis=0, keepdims=True)
    raised = jnp.exp2((plain - top) * (factor * LOG2E))
    total = jnp.sum(raised, axis=0, keepdims=True)
    return plain, raised * (1.0 / total)


def head_numbers(place, row, heads, split, frames):
    if not split:
        return [place * heads + h for h in range(heads)]
    each = heads // 2
    pieces = [piece_of(place, late, row, frames) for late in range(2)]
    return [pieces[h // each] * each + h % each for h in range(heads)]


def factors_of(place, row, scale_ref, heads, split, frames):
    inv_root = 1.0 / math.sqrt(HDH)
    return [scale_ref[n] * inv_root for n in head_numbers(place, row, heads, split, frames)]


def forward_body(frames, heads, slots, split, *refs):
    place_ref, row_ref, scale_ref, pattern_ref = refs[:4]
    blocks = refs[4 : 4 + frames]
    outs = refs[4 + frames : 4 + 2 * frames]
    held = refs[-1]
    place = place_ref[0]
    factors = factors_of(place, row_ref[0], scale_ref, heads, split, frames)
    for s in range(frames):
        frame = lax.rem(place + frames - s, frames)
        held[frame] = blocks[s][1:3]
    for s in range(frames):
        frame = lax.rem(place + frames - s, frames)
        chosen = [pattern_ref[frame, j] for j in range(slots)]
        for h in range(heads):
            at = slice(h * HDH, (h + 1) * HDH)
            keys = both([held[g, 0, :, at] for g in chosen])
            values = both([held[g, 1, :, at] for g in chosen])
            _, probs = softmax_rows(blocks[s][0, :, at], keys, factors[h])
            outs[s][0, :, at] = dot(probs.astype(BF16), values, TN).astype(BF16)


def forward(place, row, scale, pattern, blocks, split=False):
    frames = len(blocks)
    _, tokens, width = blocks[0].shape
    shape = jax.ShapeDtypeStruct((1, tokens, width), BF16)
    return call(
        functools.partial(forward_body, frames, width // HDH, pattern.shape[1], split),
        [shape] * frames,
        [place, row, scale, pattern, *blocks],
        smem=4,
        scratch=[pltpu.VMEM((frames, 2, tokens, width), BF16)],
    )


def backward_body(frames, heads, slots, half, before, *refs):
    place_ref, row_ref, scale_ref, pattern_ref = refs[:4]
    earlier = refs[4 : 4 + before]
    refs = refs[4 + before :]
    blocks = refs[:frames]
    grads = refs[frames : 2 * frames]
    outs = refs[2 * frames : 3 * frames]
    scale_out = refs[3 * frames]
    held, key_sum, value_sum = refs[3 * frames + 1 :]
    place = place_ref[0]
    tokens = tokens_of(blocks)
    inv_root = 1.0 / math.sqrt(HDH)
    if half is None:
        base = 0
        numbers = head_numbers(place, row_ref[0], heads, False, frames)
    else:
        base = half * heads * HDH
        numbers = head_numbers(place, row_ref[0], 2 * heads, True, frames)
        numbers = numbers[half * heads : (half + 1) * heads]
    factors = [scale_ref[n] * inv_root for n in numbers]
    part = slice(base, base + heads * HDH)
    key_sum[...] = jnp.zeros_like(key_sum)
    value_sum[...] = jnp.zeros_like(value_sum)
    for s in range(frames):
        frame = lax.rem(place + frames - s, frames)
        held[frame] = blocks[s][1:3, :, part]
    terms = [jnp.zeros((1, tokens), F32) for _ in range(heads)]
    for s in range(frames):
        frame = lax.rem(place + frames - s, frames)
        chosen = [pattern_ref[frame, j] for j in range(slots)]
        for h in range(heads):
            at = slice(h * HDH, (h + 1) * HDH)
            query = blocks[s][0, :, base + h * HDH : base + (h + 1) * HDH]
            grad = grads[s][0, :, at]
            keys = both([held[g, 0, :, at] for g in chosen])
            values = both([held[g, 1, :, at] for g in chosen])
            plain, probs = softmax_rows(query, keys, factors[h])
            prob_grads = dot(values, grad, NT)
            weighted = jnp.sum(prob_grads * probs, axis=0, keepdims=True)
            score_grads = probs * (prob_grads - weighted)
            terms[h] = terms[h] + jnp.sum(score_grads * plain, axis=0, keepdims=True)
            low = score_grads.astype(BF16)
            outs[s][0, :, at] = (dot(low, keys, TN) * factors[h]).astype(BF16)
            key_part = dot(low, query, NN)
            value_part = dot(probs.astype(BF16), grad, NN)
            for j, g in enumerate(chosen):
                rows = slice(j * tokens, (j + 1) * tokens)
                key_sum[g, :, at] += key_part[rows]
                value_sum[g, :, at] += value_part[rows]
    for s in range(frames):
        frame = lax.rem(place + frames - s, frames)
        for h in range(heads):
            at = slice(h * HDH, (h + 1) * HDH)
            outs[s][1, :, at] = (key_sum[frame, :, at] * factors[h]).astype(BF16)
        outs[s][2] = value_sum[frame].astype(BF16)
    lanes = lax.broadcasted_iota(jnp.int32, scale_out.shape, 1)
    result = earlier[0][...] if before else jnp.zeros(scale_out.shape, F32)
    for h in range(heads):
        term = jnp.sum(terms[h], axis=1, keepdims=True) * inv_root
        result = result + jnp.where(lanes == numbers[h], term, 0.0)
    scale_out[...] = result


def tokens_of(blocks):
    return blocks[0].shape[1]


def backward(place, row, scale, pattern, blocks, grads, half=None, before=()):
    frames = len(blocks)
    _, tokens, width = grads[0].shape
    shape = jax.ShapeDtypeStruct((3, tokens, width), BF16)
    result = call(
        functools.partial(
            backward_body, frames, width // HDH, pattern.shape[1], half, len(before)
        ),
        [shape] * frames + [jax.ShapeDtypeStruct((1, LANES), F32)],
        [place, row, scale, pattern, *before, *blocks, *grads],
        smem=4,
        scratch=[
            pltpu.VMEM((frames, 2, tokens, width), BF16),
            pltpu.VMEM((frames, tokens, width), F32),
            pltpu.VMEM((frames, tokens, width), F32),
        ],
    )
    return result[:frames], result[frames]


def context_grad_body(skip, count, *refs):
    refs = refs[skip:]
    mine, other = refs[:2]
    weights = refs[2 : 2 + count]
    mine_out, other_out = refs[2 + count :]
    tokens = mine.shape[0]
    rows = both([other[...], mine[...]])
    start = 0
    for w in weights:
        at = slice(start, start + w.shape[0])
        result = dot(rows, w[...], NT).astype(BF16)
        other_out[:, at] = result[:tokens]
        mine_out[:, at] = result[tokens:]
        start += w.shape[0]


def context_grads(mine, other, weights, scalars=()):
    tokens = mine.shape[0]
    features = sum(w.shape[0] for w in weights)
    shape = jax.ShapeDtypeStruct((tokens, features), BF16)
    return call(
        functools.partial(context_grad_body, len(scalars), len(weights)),
        [shape, shape],
        [*scalars, mine, other, *weights],
        smem=len(scalars),
    )


def project_body(count, *refs):
    mine, other = refs[:2]
    weights = refs[2 : 2 + count]
    mine_out, other_out = refs[2 + count :]
    tokens = mine.shape[0]
    rows = both([other[...], mine[...]])
    start = 0
    total = None
    for w in weights:
        part = dot(rows[:, start : start + w.shape[0]], w[...], NN)
        total = part if total is None else total + part
        start += w.shape[0]
    other_out[...] = total[:tokens].astype(other_out.dtype)
    mine_out[...] = total[tokens:]


def project_pair(mine, other, weights, share=0, shares=1):
    tokens, features = mine.shape
    width = weights[0].shape[1] // shares
    tile = math.gcd(width, 768)
    steps = width // tile
    rows = pl.BlockSpec((tokens, features), lambda i: (0, 0))
    columns = pl.BlockSpec((tokens, tile), lambda i: (0, i))
    return pl.pallas_call(
        functools.partial(project_body, len(weights)),
        grid=(steps,),
        out_shape=[jax.ShapeDtypeStruct((tokens, width), kind) for kind in (F32, BF16)],
        in_specs=[rows, rows]
        + [
            pl.BlockSpec((w.shape[0], tile), lambda i: (0, i + share * steps)) for w in weights
        ],
        out_specs=[columns, columns],
        name="project",
    )(mine, other, *weights)


def place_in_half(row, group):
    half = lax.div(row, group)
    return half, row - half * group


def join_body(frames, pieces, size, *refs):
    place = refs[0][0]
    half, inner = place_in_half(refs[1][0], sum(len(p) for p in pieces))
    count = len(pieces)
    mine = refs[2 : 2 + count]
    other = refs[2 + count : 2 + 2 * count]
    outs = refs[2 + 2 * count : 2 + 2 * count + frames]
    whole = refs[-1]
    group = sum(len(p) for p in pieces)
    width = whole.shape[1] // frames
    for h, sources in ((half, mine), (1 - half, other)):
        for source, names in zip(sources, pieces):
            for k, j in enumerate(names):
                spot = h * group + jnp.bitwise_xor(inner, j)
                whole[:, lane_block(spot, size)] = source[:, k * size : (k + 1) * size]
    for s in range(frames):
        outs[s][0] = whole[:, lane_block(lax.rem(place + s, frames), width)]


def join(place, row, mine, other, pieces, size, frames, full):
    tokens = mine[0].shape[0]
    if size % LANES == 0:
        shape = jax.ShapeDtypeStruct((1, tokens, full // frames), BF16)
        return call(
            functools.partial(join_body, frames, pieces, size),
            [shape] * frames,
            [place, row, *mine, *other],
            smem=2,
            scratch=[pltpu.VMEM((tokens, full), BF16)],
        )
    group = sum(len(p) for p in pieces)
    whole = jnp.zeros((tokens, full), BF16)
    half, inner = place_in_half(row[0], group)
    for h, sources in ((half, mine), (1 - half, other)):
        for source, names in zip(sources, pieces):
            for k, j in enumerate(names):
                spot = h * group + jnp.bitwise_xor(inner, j)
                piece = source[:, k * size : (k + 1) * size]
                whole = lax.dynamic_update_slice(whole, piece, (0, spot * size))
    return pack(place, [whole], frames)


def part_body(frames, count, size, *refs):
    place = refs[0][0]
    half, inner = place_in_half(refs[1][0], count)
    blocks = refs[2 : 2 + frames]
    keep, send, whole = refs[2 + frames :]
    width = whole.shape[1] // frames
    for s in range(frames):
        whole[:, lane_block(lax.rem(place + s, frames), width)] = blocks[s][0]
    for j in range(count):
        spot = jnp.bitwise_xor(inner, j)
        at = slice(j * size, (j + 1) * size)
        keep[:, at] = whole[:, lane_block(half * count + spot, size)]
        send[:, at] = whole[:, lane_block((1 - half) * count + spot, size)]


def part(place, row, blocks, count, size):
    frames = len(blocks)
    _, tokens, width = blocks[0].shape
    if size % LANES == 0:
        shape = jax.ShapeDtypeStruct((tokens, count * size), BF16)
        return call(
            functools.partial(part_body, frames, count, size),
            [shape, shape],
            [place, row, *blocks],
            smem=2,
            scratch=[pltpu.VMEM((tokens, width * frames), BF16)],
        )
    whole = unpack(place, blocks, frames)[0]
    half, inner = place_in_half(row[0], count)

    def half_of(h):
        spots = [h * count + jnp.bitwise_xor(inner, j) for j in range(count)]
        return jnp.concatenate(
            [lax.dynamic_slice_in_dim(whole, spot * size, size, axis=1) for spot in spots], axis=1
        )

    return half_of(half), half_of(1 - half)


def split_pack_body(frames, count, *refs):
    place, row = refs[0][0], refs[1][0]
    sources = refs[2 : 2 + count]
    outs = refs[2 + count :]
    size = outs[0].shape[2] // 2
    for s in range(frames):
        target = lax.rem(place + s, frames)
        for late in range(2):
            piece = piece_of(target, late, row, frames)
            for i in range(count):
                at = slice(late * size, (late + 1) * size)
                outs[s][i, :, at] = sources[i][:, lane_block(piece, size)]


def split_pack(place, row, sources, frames):
    tokens, full = sources[0].shape
    shape = jax.ShapeDtypeStruct((len(sources), tokens, full // frames), BF16)
    return call(
        functools.partial(split_pack_body, frames, len(sources)),
        [shape] * frames,
        [place, row, *sources],
        smem=2,
    )


def split_unpack_body(frames, count, *refs):
    place, row = refs[0][0], refs[1][0]
    blocks = (refs[2 : 2 + frames], refs[2 + frames : 2 + 2 * frames])
    scales = refs[2 + 2 * frames : 2 + 3 * frames]
    outs = refs[2 + 3 * frames : -1]
    size = blocks[0][0].shape[2]
    for late in range(2):
        for s in range(frames):
            piece = piece_of(lax.rem(place + s, frames), late, row, frames)
            for i in range(count):
                outs[i][:, lane_block(piece, size)] = blocks[late][s][i]
    total = functools.reduce(jnp.add, [s[...] for s in scales])
    refs[-1][...] = total[:, : refs[-1].shape[1]]


def split_unpack(place, row, early, late, scales, heads):
    frames = len(early)
    count, tokens, size = early[0].shape
    shape = jax.ShapeDtypeStruct((tokens, 2 * size * frames), BF16)
    return call(
        functools.partial(split_unpack_body, frames, count),
        [shape] * count + [jax.ShapeDtypeStruct((1, heads), F32)],
        [place, row, *early, *late, *scales],
        smem=2,
    )


def split_join_body(frames, count, *refs):
    place, row = refs[0][0], refs[1][0]
    mine = refs[2 : 2 + count]
    other = refs[2 + count : 2 + 2 * count]
    outs = refs[2 + 2 * count : 2 + 2 * count + frames]
    own, theirs = refs[2 + 2 * count + frames :]
    quarter = frames // 2
    size = own.shape[1] // quarter
    half, inner = place_in_half(row, frames)
    for sources, whole in ((mine, own), (other, theirs)):
        start = 0
        for source in sources:
            whole[:, start : start + source.shape[1]] = source[...]
            start += source.shape[1]
    for s in range(frames):
        target = lax.rem(place + s, frames)
        near = jnp.bitwise_xor(lax.rem(target, quarter), lax.rem(inner, quarter))
        at = lane_block(near, size)
        outs[s][0] = jnp.where(lax.div(target, quarter) == half, own[:, at], theirs[:, at])


def split_join(place, row, mine, other, frames):
    tokens = mine[0].shape[0]
    width = sum(m.shape[1] for m in mine)
    shape = jax.ShapeDtypeStruct((1, tokens, 2 * width // frames), BF16)
    return call(
        functools.partial(split_join_body, frames, len(mine)),
        [shape] * frames,
        [place, row, *mine, *other],
        smem=2,
        scratch=[pltpu.VMEM((tokens, width), BF16)] * 2,
    )


def split_part_body(frames, *refs):
    place, row = refs[0][0], refs[1][0]
    blocks = refs[2 : 2 + frames]
    keep, send, whole = refs[2 + frames :]
    size = keep.shape[1] // frames
    half, inner = place_in_half(row, frames)
    for s in range(frames):
        for late in range(2):
            piece = piece_of(lax.rem(place + s, frames), late, row, frames)
            whole[:, lane_block(piece, size)] = blocks[s][0, :, late * size : (late + 1) * size]
    for j in range(frames):
        spot = jnp.bitwise_xor(inner, j)
        at = slice(j * size, (j + 1) * size)
        keep[:, at] = whole[:, lane_block(half * frames + spot, size)]
        send[:, at] = whole[:, lane_block((1 - half) * frames + spot, size)]


def split_part(place, row, blocks):
    frames = len(blocks)
    _, tokens, width = blocks[0].shape
    shape = jax.ShapeDtypeStruct((tokens, frames * width // 2), BF16)
    return call(
        functools.partial(split_part_body, frames),
        [shape, shape],
        [place, row, *blocks],
        smem=2,
        scratch=[pltpu.VMEM((tokens, width * frames), BF16)],
    )


def exchange(blocks, sign):
    frames = len(blocks)

    def shift(s):
        return [(i, (i + sign * s) % frames) for i in range(frames)]

    return [blocks[0]] + [lax.ppermute(blocks[s], "frame", shift(s)) for s in range(1, frames)]


def swap(x, bit):
    group = lax.axis_size("dp")
    return lax.ppermute(x, "dp", [(i, i ^ bit) for i in range(group)])


def gather_half(out_weight, count):
    weights = {0: out_weight}
    bit = count // 2
    while bit:
        for j in list(weights):
            weights[j ^ bit] = swap(weights[j], bit)
        bit //= 2
    return [weights[j] for j in range(count)]


def finish_body(pieces, *refs):
    own = refs[:pieces]
    other = refs[pieces : 2 * pieces]
    out = refs[-1]
    start = 0
    for mine, theirs in zip(own, other):
        at = slice(start, start + mine.shape[1])
        out[:, at] = (mine[...] + theirs[...].astype(F32)).astype(BF16)
        start = at.stop


def finish(own, other):
    tokens = own[0].shape[0]
    model = sum(o.shape[1] for o in own)
    return call(
        functools.partial(finish_body, len(own)),
        [jax.ShapeDtypeStruct((tokens, model), BF16)],
        [*own, *other],
    )[0]


def local_split(queries, key_states, value_states, head_scale, out_weight, frame_pattern, out_grad):
    frames = lax.axis_size("frame")
    group = lax.axis_size("dp")
    tokens, full = queries.shape[2:]
    model = out_grad.shape[3]
    heads = full // HDH
    place = lax.axis_index("frame").astype(jnp.int32).reshape(1)
    row = lax.axis_index("dp").astype(jnp.int32).reshape(1)

    grad_rows = out_grad[0, 0]
    other_rows = swap(grad_rows, frames)
    weights = gather_half(out_weight, frames)
    early, late = weights[: frames // 2], weights[frames // 2 :]

    sent = split_pack(place, row, [queries[0, 0], key_states[0, 0], value_states[0, 0]], frames)
    blocks = exchange(sent, 1)

    mine, theirs = context_grads(grad_rows, other_rows, early, [frame_pattern])
    other = swap(theirs, frames)
    sent = split_join(place, row, [mine], [other], frames)
    grads_early = exchange(sent, 1)
    mine, other = [], []
    for i, weight in enumerate(late):
        last = i == len(late) - 1
        own, theirs = context_grads(grad_rows, other_rows, [weight])
        mine.append(own)
        other.append(swap(theirs, frames))
    context = forward(place, row, head_scale, frame_pattern, blocks, True)
    context = exchange(context, -1)
    sent = split_join(place, row, mine, other, frames)
    grads_late = exchange(sent, 1)

    sent, scale_early = backward(
        place, row, head_scale, frame_pattern, blocks, grads_early, 0
    )
    done_early = exchange(sent, -1)
    sent, scale_part = backward(
        place, row, head_scale, frame_pattern, blocks, grads_late, 1, [scale_early]
    )
    done_late = exchange(sent, -1)

    keep, send = split_part(place, row, context)
    taken = swap(send, frames)
    own_first, theirs = project_pair(keep, taken, weights, 0, 2)
    first = swap(theirs, frames)
    own_last, theirs = project_pair(keep, taken, weights, 1, 2)
    last = swap(theirs, frames)

    bit = group // 2
    while bit:
        scale_part = scale_part + swap(scale_part, bit)
        bit //= 2
    scales = exchange([scale_part] * frames, 1)

    attended = finish([own_first, own_last], [first, last])
    query_grad, key_grad, value_grad, scale_sum = split_unpack(
        place, row, done_early, done_late, scales, heads
    )
    shape = (1, 1, tokens, full)
    return (
        attended.reshape(1, 1, tokens, model),
        query_grad.reshape(shape),
        key_grad.reshape(shape),
        value_grad.reshape(shape),
        scale_sum[0, :heads],
    )


def local_plain(queries, key_states, value_states, head_scale, out_weight, frame_pattern, out_grad):
    frames = lax.axis_size("frame")
    group = lax.axis_size("dp")
    tokens, full = queries.shape[2:]
    model = out_grad.shape[3]
    heads = full // HDH
    count = group // 2
    size = out_weight.shape[0]
    place = lax.axis_index("frame").astype(jnp.int32).reshape(1)
    row = lax.axis_index("dp").astype(jnp.int32).reshape(1)

    grad_rows = out_grad[0, 0]
    other_rows = swap(grad_rows, count)
    weights = gather_half(out_weight, count)
    early, late = weights[: count // 2], weights[count // 2 :]
    names = (list(range(count // 2)), list(range(count // 2, count)))

    sent = pack(place, [queries[0, 0], key_states[0, 0], value_states[0, 0]], frames)
    blocks = exchange(sent, 1)
    context = exchange(forward(place, row, head_scale, frame_pattern, blocks), -1)
    mine, other = [], []
    for part_weights in (early, late):
        own, theirs = context_grads(grad_rows, other_rows, part_weights)
        mine.append(own)
        other.append(swap(theirs, count))
    sent = join(place, row, mine, other, names, size, frames, full)
    grads = exchange(sent, 1)

    keep, send = part(place, row, context, count, size)
    own, theirs = project_pair(keep, swap(send, count), weights)
    attended = (own + swap(theirs, count)).astype(BF16)

    sent, scale_part = backward(place, row, head_scale, frame_pattern, blocks, grads)
    blocks = exchange(sent, -1)
    bit = group // 2
    while bit:
        scale_part = scale_part + swap(scale_part, bit)
        bit //= 2
    scale_sum = functools.reduce(jnp.add, exchange([scale_part] * frames, 1))
    query_grad, key_grad, value_grad = unpack(place, blocks, frames)
    shape = (1, 1, tokens, full)
    return (
        attended.reshape(1, 1, tokens, model),
        query_grad.reshape(shape),
        key_grad.reshape(shape),
        value_grad.reshape(shape),
        scale_sum[0, :heads],
    )


def local(*args):
    frames = lax.axis_size("frame")
    size = args[4].shape[0]
    if lax.axis_size("dp") == 2 * frames and size % HDH == 0:
        return local_split(*args)
    return local_plain(*args)


def solution(mesh):
    spec = P("dp", "frame", None, None)
    return jax.shard_map(
        local,
        mesh=mesh,
        in_specs=(spec, spec, spec, P(), P("dp", None), P(), spec),
        out_specs=(spec, spec, spec, spec, P()),
        check_vma=False,
    )
```

```python
import functools
import math

import jax
import jax.numpy as jnp
from jax import lax
from jax.experimental import pallas as pl
from jax.experimental.pallas import tpu as pltpu
from jax.sharding import PartitionSpec as P


HDH = 128
LANES = 128
LOG2E = 1.0 / math.log(2.0)


GRANT = 16 * 1024 * 1024
F32 = jnp.float32
BF16 = jnp.bfloat16
NT = (((1,), (1,)), ((), ()))
NN = (((1,), (0,)), ((), ()))
TN = (((0,), (0,)), ((), ()))
SMEM = pl.BlockSpec(memory_space=pltpu.SMEM)
VMEM = pl.BlockSpec(memory_space=pltpu.VMEM)


def dot(a, b, dims):
    return lax.dot_general(a, b, dims, preferred_element_type=F32)


def lane_block(index, width):
    return pl.ds(pl.multiple_of(index * width, LANES), width)


def call(body, outs, operands, smem=0, scratch=()):
    return pl.pallas_call(
        body,
        out_shape=outs,
        in_specs=[SMEM] * smem + [VMEM] * (len(operands) - smem),
        out_specs=[VMEM] * len(outs),
        scratch_shapes=list(scratch),
        compiler_params=pltpu.CompilerParams(vmem_limit_bytes=GRANT),
    )(*operands)


def pack_body(frames, width, count, *refs):
    place = refs[0][0]
    sources = refs[1 : 1 + count]
    outs = refs[1 + count :]
    for s in range(frames):
        target = lax.rem(place + s, frames)
        for i in range(count):
            outs[s][i] = sources[i][:, lane_block(target, width)]


def pack(place, sources, frames):
    tokens, full = sources[0].shape
    width = full // frames
    shape = jax.ShapeDtypeStruct((len(sources), tokens, width), BF16)
    return call(
        functools.partial(pack_body, frames, width, len(sources)),
        [shape] * frames,
        [place, *sources],
        smem=1,
    )


def unpack_body(frames, width, count, *refs):
    place = refs[0][0]
    blocks = refs[1 : 1 + frames]
    outs = refs[1 + frames :]
    for s in range(frames):
        source = lax.rem(place + s, frames)
        for i in range(count):
            outs[i][:, lane_block(source, width)] = blocks[s][i]


def unpack(place, blocks, frames):
    count, tokens, width = blocks[0].shape
    shape = jax.ShapeDtypeStruct((tokens, width * frames), BF16)
    return call(
        functools.partial(unpack_body, frames, width, count),
        [shape] * count,
        [place, *blocks],
        smem=1,
    )


def piece_of(target, late, row, frames):
    quarter = frames // 2
    inner = lax.rem(row, frames)
    far = jnp.bitwise_xor(lax.div(inner, quarter), late)
    return lax.div(target, quarter) * frames + far * quarter + lax.rem(target, quarter)


def both(parts):
    return jnp.concatenate(parts, axis=0)


def softmax_rows(query, keys, factor):
    plain = dot(keys, query, NT)
    top = jnp.max(plain, axis=0, keepdims=True)
    raised = jnp.exp2((plain - top) * (factor * LOG2E))
    total = jnp.sum(raised, axis=0, keepdims=True)
    return plain, raised * (1.0 / total)


def head_numbers(place, row, heads, split, frames):
    if not split:
        return [place * heads + h for h in range(heads)]
    each = heads // 2
    pieces = [piece_of(place, late, row, frames) for late in range(2)]
    return [pieces[h // each] * each + h % each for h in range(heads)]


def factors_of(place, row, scale_ref, heads, split, frames):
    inv_root = 1.0 / math.sqrt(HDH)
    return [scale_ref[n] * inv_root for n in head_numbers(place, row, heads, split, frames)]


def forward_body(frames, heads, slots, split, *refs):
    place_ref, row_ref, scale_ref, pattern_ref = refs[:4]
    blocks = refs[4 : 4 + frames]
    outs = refs[4 + frames : 4 + 2 * frames]
    held = refs[-1]
    place = place_ref[0]
    factors = factors_of(place, row_ref[0], scale_ref, heads, split, frames)
    for s in range(frames):
        frame = lax.rem(place + frames - s, frames)
        held[frame] = blocks[s][1:3]
    for s in range(frames):
        frame = lax.rem(place + frames - s, frames)
        chosen = [pattern_ref[frame, j] for j in range(slots)]
        for h in range(heads):
            at = slice(h * HDH, (h + 1) * HDH)
            keys = both([held[g, 0, :, at] for g in chosen])
            values = both([held[g, 1, :, at] for g in chosen])
            _, probs = softmax_rows(blocks[s][0, :, at], keys, factors[h])
            outs[s][0, :, at] = dot(probs.astype(BF16), values, TN).astype(BF16)


def forward(place, row, scale, pattern, blocks, split=False):
    frames = len(blocks)
    _, tokens, width = blocks[0].shape
    shape = jax.ShapeDtypeStruct((1, tokens, width), BF16)
    return call(
        functools.partial(forward_body, frames, width // HDH, pattern.shape[1], split),
        [shape] * frames,
        [place, row, scale, pattern, *blocks],
        smem=4,
        scratch=[pltpu.VMEM((frames, 2, tokens, width), BF16)],
    )


def backward_body(frames, heads, slots, half, before, *refs):
    place_ref, row_ref, scale_ref, pattern_ref = refs[:4]
    earlier = refs[4 : 4 + before]
    refs = refs[4 + before :]
    blocks = refs[:frames]
    grads = refs[frames : 2 * frames]
    outs = refs[2 * frames : 3 * frames]
    scale_out = refs[3 * frames]
    held, key_sum, value_sum = refs[3 * frames + 1 :]
    place = place_ref[0]
    tokens = tokens_of(blocks)
    inv_root = 1.0 / math.sqrt(HDH)
    if half is None:
        base = 0
        numbers = head_numbers(place, row_ref[0], heads, False, frames)
    else:
        base = half * heads * HDH
        numbers = head_numbers(place, row_ref[0], 2 * heads, True, frames)
        numbers = numbers[half * heads : (half + 1) * heads]
    factors = [scale_ref[n] * inv_root for n in numbers]
    part = slice(base, base + heads * HDH)
    key_sum[...] = jnp.zeros_like(key_sum)
    value_sum[...] = jnp.zeros_like(value_sum)
    for s in range(frames):
        frame = lax.rem(place + frames - s, frames)
        held[frame] = blocks[s][1:3, :, part]
    terms = [jnp.zeros((1, tokens), F32) for _ in range(heads)]
    for s in range(frames):
        frame = lax.rem(place + frames - s, frames)
        chosen = [pattern_ref[frame, j] for j in range(slots)]
        for h in range(heads):
            at = slice(h * HDH, (h + 1) * HDH)
            query = blocks[s][0, :, base + h * HDH : base + (h + 1) * HDH]
            grad = grads[s][0, :, at]
            keys = both([held[g, 0, :, at] for g in chosen])
            values = both([held[g, 1, :, at] for g in chosen])
            plain, probs = softmax_rows(query, keys, factors[h])
            prob_grads = dot(values, grad, NT)
            weighted = jnp.sum(prob_grads * probs, axis=0, keepdims=True)
            score_grads = probs * (prob_grads - weighted)
            terms[h] = terms[h] + jnp.sum(score_grads * plain, axis=0, keepdims=True)
            low = score_grads.astype(BF16)
            outs[s][0, :, at] = (dot(low, keys, TN) * factors[h]).astype(BF16)
            key_part = dot(low, query, NN)
            value_part = dot(probs.astype(BF16), grad, NN)
            for j, g in enumerate(chosen):
                rows = slice(j * tokens, (j + 1) * tokens)
                key_sum[g, :, at] += key_part[rows]
                value_sum[g, :, at] += value_part[rows]
    for s in range(frames):
        frame = lax.rem(place + frames - s, frames)
        for h in range(heads):
            at = slice(h * HDH, (h + 1) * HDH)
            outs[s][1, :, at] = (key_sum[frame, :, at] * factors[h]).astype(BF16)
        outs[s][2] = value_sum[frame].astype(BF16)
    lanes = lax.broadcasted_iota(jnp.int32, scale_out.shape, 1)
    result = earlier[0][...] if before else jnp.zeros(scale_out.shape, F32)
    for h in range(heads):
        term = jnp.sum(terms[h], axis=1, keepdims=True) * inv_root
        result = result + jnp.where(lanes == numbers[h], term, 0.0)
    scale_out[...] = result


def tokens_of(blocks):
    return blocks[0].shape[1]


def backward(place, row, scale, pattern, blocks, grads, half=None, before=()):
    frames = len(blocks)
    _, tokens, width = grads[0].shape
    shape = jax.ShapeDtypeStruct((3, tokens, width), BF16)
    result = call(
        functools.partial(
            backward_body, frames, width // HDH, pattern.shape[1], half, len(before)
        ),
        [shape] * frames + [jax.ShapeDtypeStruct((1, LANES), F32)],
        [place, row, scale, pattern, *before, *blocks, *grads],
        smem=4,
        scratch=[
            pltpu.VMEM((frames, 2, tokens, width), BF16),
            pltpu.VMEM((frames, tokens, width), F32),
            pltpu.VMEM((frames, tokens, width), F32),
        ],
    )
    return result[:frames], result[frames]


def context_grad_body(skip, count, cut, *refs):
    refs = refs[skip:]
    mine, other = refs[:2]
    weights = refs[2 : 2 + count]
    mine_out, other_out = refs[2 + count : 4 + count]
    tokens = mine.shape[0]
    rows = both([other[...], mine[...]])
    start = 0
    for w in weights:
        at = slice(start, start + w.shape[0])
        result = dot(rows, w[...], NT).astype(BF16)
        other_out[:, at] = result[:tokens]
        mine_out[:, at] = result[tokens:]
        start += w.shape[0]
    if cut:
        refs[4 + count][...] = weights[0][:cut]
        refs[5 + count][...] = weights[0][cut:]


def context_grads(mine, other, weights, scalars=(), cut=0):
    tokens = mine.shape[0]
    features = sum(w.shape[0] for w in weights)
    shapes = [jax.ShapeDtypeStruct((tokens, features), BF16)] * 2
    if cut:
        size, model = weights[0].shape
        shapes += [jax.ShapeDtypeStruct((n, model), BF16) for n in (cut, size - cut)]
    return call(
        functools.partial(context_grad_body, len(scalars), len(weights), cut),
        shapes,
        [*scalars, mine, other, *weights],
        smem=len(scalars),
    )


def project_body(count, columns, *refs):
    mine, other = refs[:2]
    weights = refs[2 : 2 + count]
    mine_out, other_out = refs[2 + count :]
    tokens = mine.shape[0]
    rows = both([other[...], mine[...]])
    start = 0
    total = None
    for w in weights:
        part = dot(rows[:, start : start + w.shape[0]], w[:, columns], NN)
        total = part if total is None else total + part
        start += w.shape[0]
    other_out[...] = total[:tokens].astype(other_out.dtype)
    mine_out[...] = total[tokens:]


def project_pair(mine, other, weights, first=0, last=None):
    tokens, _ = mine.shape
    columns = slice(first, weights[0].shape[1] if last is None else last)
    width = columns.stop - columns.start
    return call(
        functools.partial(project_body, len(weights), columns),
        [jax.ShapeDtypeStruct((tokens, width), kind) for kind in (F32, BF16)],
        [mine, other, *weights],
    )


def place_in_half(row, group):
    half = lax.div(row, group)
    return half, row - half * group


def join_body(frames, pieces, size, *refs):
    place = refs[0][0]
    half, inner = place_in_half(refs[1][0], sum(len(p) for p in pieces))
    count = len(pieces)
    mine = refs[2 : 2 + count]
    other = refs[2 + count : 2 + 2 * count]
    outs = refs[2 + 2 * count : 2 + 2 * count + frames]
    whole = refs[-1]
    group = sum(len(p) for p in pieces)
    width = whole.shape[1] // frames
    for h, sources in ((half, mine), (1 - half, other)):
        for source, names in zip(sources, pieces):
            for k, j in enumerate(names):
                spot = h * group + jnp.bitwise_xor(inner, j)
                whole[:, lane_block(spot, size)] = source[:, k * size : (k + 1) * size]
    for s in range(frames):
        outs[s][0] = whole[:, lane_block(lax.rem(place + s, frames), width)]


def join(place, row, mine, other, pieces, size, frames, full):
    tokens = mine[0].shape[0]
    if size % LANES == 0:
        shape = jax.ShapeDtypeStruct((1, tokens, full // frames), BF16)
        return call(
            functools.partial(join_body, frames, pieces, size),
            [shape] * frames,
            [place, row, *mine, *other],
            smem=2,
            scratch=[pltpu.VMEM((tokens, full), BF16)],
        )
    group = sum(len(p) for p in pieces)
    whole = jnp.zeros((tokens, full), BF16)
    half, inner = place_in_half(row[0], group)
    for h, sources in ((half, mine), (1 - half, other)):
        for source, names in zip(sources, pieces):
            for k, j in enumerate(names):
                spot = h * group + jnp.bitwise_xor(inner, j)
                piece = source[:, k * size : (k + 1) * size]
                whole = lax.dynamic_update_slice(whole, piece, (0, spot * size))
    return pack(place, [whole], frames)


def part_body(frames, count, size, *refs):
    place = refs[0][0]
    half, inner = place_in_half(refs[1][0], count)
    blocks = refs[2 : 2 + frames]
    keep, send, whole = refs[2 + frames :]
    width = whole.shape[1] // frames
    for s in range(frames):
        whole[:, lane_block(lax.rem(place + s, frames), width)] = blocks[s][0]
    for j in range(count):
        spot = jnp.bitwise_xor(inner, j)
        at = slice(j * size, (j + 1) * size)
        keep[:, at] = whole[:, lane_block(half * count + spot, size)]
        send[:, at] = whole[:, lane_block((1 - half) * count + spot, size)]


def part(place, row, blocks, count, size):
    frames = len(blocks)
    _, tokens, width = blocks[0].shape
    if size % LANES == 0:
        shape = jax.ShapeDtypeStruct((tokens, count * size), BF16)
        return call(
            functools.partial(part_body, frames, count, size),
            [shape, shape],
            [place, row, *blocks],
            smem=2,
            scratch=[pltpu.VMEM((tokens, width * frames), BF16)],
        )
    whole = unpack(place, blocks, frames)[0]
    half, inner = place_in_half(row[0], count)

    def half_of(h):
        spots = [h * count + jnp.bitwise_xor(inner, j) for j in range(count)]
        return jnp.concatenate(
            [lax.dynamic_slice_in_dim(whole, spot * size, size, axis=1) for spot in spots], axis=1
        )

    return half_of(half), half_of(1 - half)


def split_pack_body(frames, count, *refs):
    place, row = refs[0][0], refs[1][0]
    sources = refs[2 : 2 + count]
    outs = refs[2 + count :]
    size = outs[0].shape[2] // 2
    for s in range(frames):
        target = lax.rem(place + s, frames)
        for late in range(2):
            piece = piece_of(target, late, row, frames)
            for i in range(count):
                at = slice(late * size, (late + 1) * size)
                outs[s][i, :, at] = sources[i][:, lane_block(piece, size)]


def split_pack(place, row, sources, frames):
    tokens, full = sources[0].shape
    shape = jax.ShapeDtypeStruct((len(sources), tokens, full // frames), BF16)
    return call(
        functools.partial(split_pack_body, frames, len(sources)),
        [shape] * frames,
        [place, row, *sources],
        smem=2,
    )


def split_unpack_body(frames, count, *refs):
    place, row = refs[0][0], refs[1][0]
    blocks = (refs[2 : 2 + frames], refs[2 + frames : 2 + 2 * frames])
    scales = refs[2 + 2 * frames : 2 + 3 * frames]
    outs = refs[2 + 3 * frames : -1]
    size = blocks[0][0].shape[2]
    for late in range(2):
        for s in range(frames):
            piece = piece_of(lax.rem(place + s, frames), late, row, frames)
            for i in range(count):
                outs[i][:, lane_block(piece, size)] = blocks[late][s][i]
    total = functools.reduce(jnp.add, [s[...] for s in scales])
    refs[-1][...] = total[:, : refs[-1].shape[1]]


def split_unpack(place, row, early, late, scales, heads):
    frames = len(early)
    count, tokens, size = early[0].shape
    shape = jax.ShapeDtypeStruct((tokens, 2 * size * frames), BF16)
    return call(
        functools.partial(split_unpack_body, frames, count),
        [shape] * count + [jax.ShapeDtypeStruct((1, heads), F32)],
        [place, row, *early, *late, *scales],
        smem=2,
    )


def split_join_body(frames, count, *refs):
    place, row = refs[0][0], refs[1][0]
    mine = refs[2 : 2 + count]
    other = refs[2 + count : 2 + 2 * count]
    outs = refs[2 + 2 * count : 2 + 2 * count + frames]
    own, theirs = refs[2 + 2 * count + frames :]
    quarter = frames // 2
    size = own.shape[1] // quarter
    half, inner = place_in_half(row, frames)
    for sources, whole in ((mine, own), (other, theirs)):
        start = 0
        for source in sources:
            whole[:, start : start + source.shape[1]] = source[...]
            start += source.shape[1]
    for s in range(frames):
        target = lax.rem(place + s, frames)
        near = jnp.bitwise_xor(lax.rem(target, quarter), lax.rem(inner, quarter))
        at = lane_block(near, size)
        outs[s][0] = jnp.where(lax.div(target, quarter) == half, own[:, at], theirs[:, at])


def split_join(place, row, mine, other, frames):
    tokens = mine[0].shape[0]
    width = sum(m.shape[1] for m in mine)
    shape = jax.ShapeDtypeStruct((1, tokens, 2 * width // frames), BF16)
    return call(
        functools.partial(split_join_body, frames, len(mine)),
        [shape] * frames,
        [place, row, *mine, *other],
        smem=2,
        scratch=[pltpu.VMEM((tokens, width), BF16)] * 2,
    )


def split_part_body(frames, *refs):
    place, row = refs[0][0], refs[1][0]
    blocks = refs[2 : 2 + frames]
    keep, send, whole = refs[2 + frames :]
    size = keep.shape[1] // frames
    half, inner = place_in_half(row, frames)
    for s in range(frames):
        for late in range(2):
            piece = piece_of(lax.rem(place + s, frames), late, row, frames)
            whole[:, lane_block(piece, size)] = blocks[s][0, :, late * size : (late + 1) * size]
    for j in range(frames):
        spot = jnp.bitwise_xor(inner, j)
        at = slice(j * size, (j + 1) * size)
        keep[:, at] = whole[:, lane_block(half * frames + spot, size)]
        send[:, at] = whole[:, lane_block((1 - half) * frames + spot, size)]


def split_part(place, row, blocks):
    frames = len(blocks)
    _, tokens, width = blocks[0].shape
    shape = jax.ShapeDtypeStruct((tokens, frames * width // 2), BF16)
    return call(
        functools.partial(split_part_body, frames),
        [shape, shape],
        [place, row, *blocks],
        smem=2,
        scratch=[pltpu.VMEM((tokens, width * frames), BF16)],
    )


def exchange(blocks, sign):
    frames = len(blocks)

    def shift(s):
        return [(i, (i + sign * s) % frames) for i in range(frames)]

    return [blocks[0]] + [lax.ppermute(blocks[s], "frame", shift(s)) for s in range(1, frames)]


def swap(x, bit):
    group = lax.axis_size("dp")
    return lax.ppermute(x, "dp", [(i, i ^ bit) for i in range(group)])


def gather_half(out_weight, count):
    weights = {0: out_weight}
    bit = count // 2
    while bit:
        for j in list(weights):
            weights[j ^ bit] = swap(weights[j], bit)
        bit //= 2
    return [weights[j] for j in range(count)]


def attend_body(counts, *refs):
    contexts = refs[: len(counts)]
    weights = list(refs[len(counts) : -1])
    total = None
    for context, pieces in zip(contexts, counts):
        start = 0
        for chunks in pieces:
            piece = both([weights.pop(0)[...] for _ in range(chunks)])
            part = dot(context[:, start : start + piece.shape[0]], piece, NN)
            total = part if total is None else total + part
            start += piece.shape[0]
    refs[-1][...] = total.astype(BF16)


def attend(contexts, weights):
    tokens, features = contexts[0].shape
    flat = [c for pieces in weights for chunks in pieces for c in chunks]
    width = flat[0].shape[1]
    tile = math.gcd(width, 768)
    counts = [[len(chunks) for chunks in pieces] for pieces in weights]
    return pl.pallas_call(
        functools.partial(attend_body, counts),
        grid=(width // tile,),
        out_shape=jax.ShapeDtypeStruct((tokens, width), BF16),
        in_specs=[pl.BlockSpec((tokens, features), lambda i: (0, 0))] * len(contexts)
        + [pl.BlockSpec((w.shape[0], tile), lambda i: (0, i)) for w in flat],
        out_specs=pl.BlockSpec((tokens, tile), lambda i: (0, i)),
        compiler_params=pltpu.CompilerParams(vmem_limit_bytes=GRANT),
        name="attend",
    )(*contexts, *flat)


def local_split(queries, key_states, value_states, head_scale, out_weight, frame_pattern, out_grad):
    frames = lax.axis_size("frame")
    group = lax.axis_size("dp")
    tokens, full = queries.shape[2:]
    model = out_grad.shape[3]
    heads = full // HDH
    place = lax.axis_index("frame").astype(jnp.int32).reshape(1)
    row = lax.axis_index("dp").astype(jnp.int32).reshape(1)

    grad_rows = out_grad[0, 0]
    other_rows = swap(grad_rows, frames)
    weights = gather_half(out_weight, frames)
    early, late = weights[: frames // 2], weights[frames // 2 :]
    cut = out_weight.shape[0] * 11 // 16

    sent = split_pack(place, row, [queries[0, 0], key_states[0, 0], value_states[0, 0]], frames)
    blocks = exchange(sent, 1)

    mine, theirs, *chunks = context_grads(
        grad_rows, other_rows, early, [frame_pattern], cut
    )
    other = swap(theirs, frames)
    other_first = swap(chunks[0], frames)
    other_last = swap(chunks[1], frames)
    far_first = swap(other_first, frames // 2)
    far_last = swap(other_last, frames // 2)
    sent = split_join(place, row, [mine], [other], frames)
    grads_early = exchange(sent, 1)
    mine, other = [], []
    for weight in late:
        own, theirs = context_grads(grad_rows, other_rows, [weight])
        mine.append(own)
        other.append(swap(theirs, frames))
    context = forward(place, row, head_scale, frame_pattern, blocks, True)
    context = exchange(context, -1)
    sent = split_join(place, row, mine, other, frames)
    grads_late = exchange(sent, 1)

    sent, scale_early = backward(
        place, row, head_scale, frame_pattern, blocks, grads_early, 0
    )
    done_early = exchange(sent, -1)
    sent, scale_part = backward(
        place, row, head_scale, frame_pattern, blocks, grads_late, 1, [scale_early]
    )
    done_late = exchange(sent, -1)

    contexts = split_part(place, row, context)
    others = {0: [other_first, other_last], frames // 2: [far_first, far_last]}
    bit = frames // 4
    while bit:
        for j in list(others):
            others[j ^ bit] = [swap(c, bit) for c in others[j]]
        bit //= 2
    others = [others[j] for j in range(frames)]
    attended = attend(contexts, [[[w] for w in weights], others])

    bit = group // 2
    while bit:
        scale_part = scale_part + swap(scale_part, bit)
        bit //= 2
    scales = exchange([scale_part] * frames, 1)

    query_grad, key_grad, value_grad, scale_sum = split_unpack(
        place, row, done_early, done_late, scales, heads
    )
    shape = (1, 1, tokens, full)
    return (
        attended.reshape(1, 1, tokens, model),
        query_grad.reshape(shape),
        key_grad.reshape(shape),
        value_grad.reshape(shape),
        scale_sum[0, :heads],
    )


def local_plain(queries, key_states, value_states, head_scale, out_weight, frame_pattern, out_grad):
    frames = lax.axis_size("frame")
    group = lax.axis_size("dp")
    tokens, full = queries.shape[2:]
    model = out_grad.shape[3]
    heads = full // HDH
    count = group // 2
    size = out_weight.shape[0]
    place = lax.axis_index("frame").astype(jnp.int32).reshape(1)
    row = lax.axis_index("dp").astype(jnp.int32).reshape(1)

    grad_rows = out_grad[0, 0]
    other_rows = swap(grad_rows, count)
    weights = gather_half(out_weight, count)
    early, late = weights[: count // 2], weights[count // 2 :]
    names = (list(range(count // 2)), list(range(count // 2, count)))

    sent = pack(place, [queries[0, 0], key_states[0, 0], value_states[0, 0]], frames)
    blocks = exchange(sent, 1)
    context = exchange(forward(place, row, head_scale, frame_pattern, blocks), -1)
    mine, other = [], []
    for part_weights in (early, late):
        own, theirs = context_grads(grad_rows, other_rows, part_weights)
        mine.append(own)
        other.append(swap(theirs, count))
    sent = join(place, row, mine, other, names, size, frames, full)
    grads = exchange(sent, 1)

    keep, send = part(place, row, context, count, size)
    own, theirs = project_pair(keep, swap(send, count), weights)
    attended = (own + swap(theirs, count)).astype(BF16)

    sent, scale_part = backward(place, row, head_scale, frame_pattern, blocks, grads)
    blocks = exchange(sent, -1)
    bit = group // 2
    while bit:
        scale_part = scale_part + swap(scale_part, bit)
        bit //= 2
    scale_sum = functools.reduce(jnp.add, exchange([scale_part] * frames, 1))
    query_grad, key_grad, value_grad = unpack(place, blocks, frames)
    shape = (1, 1, tokens, full)
    return (
        attended.reshape(1, 1, tokens, model),
        query_grad.reshape(shape),
        key_grad.reshape(shape),
        value_grad.reshape(shape),
        scale_sum[0, :heads],
    )


def local(*args):
    frames = lax.axis_size("frame")
    size = args[4].shape[0]
    if lax.axis_size("dp") == 2 * frames and size % HDH == 0:
        return local_split(*args)
    return local_plain(*args)


def solution(mesh):
    spec = P("dp", "frame", None, None)
    return jax.shard_map(
        local,
        mesh=mesh,
        in_specs=(spec, spec, spec, P(), P("dp", None), P(), spec),
        out_specs=(spec, spec, spec, spec, P()),
        check_vma=False,
    )
```

```python
import functools
import math

import jax
import jax.numpy as jnp
from jax import lax
from jax.experimental import pallas as pl
from jax.experimental.pallas import tpu as pltpu
from jax.sharding import PartitionSpec as P


HDH = 128
LANES = 128
LOG2E = 1.0 / math.log(2.0)


GRANT = 16 * 1024 * 1024
F32 = jnp.float32
BF16 = jnp.bfloat16
NT = (((1,), (1,)), ((), ()))
NN = (((1,), (0,)), ((), ()))
TN = (((0,), (0,)), ((), ()))
SMEM = pl.BlockSpec(memory_space=pltpu.SMEM)
VMEM = pl.BlockSpec(memory_space=pltpu.VMEM)


def dot(a, b, dims):
    return lax.dot_general(a, b, dims, preferred_element_type=F32)


def lane_block(index, width):
    return pl.ds(pl.multiple_of(index * width, LANES), width)


def call(body, outs, operands, smem=0, scratch=()):
    return pl.pallas_call(
        body,
        out_shape=outs,
        in_specs=[SMEM] * smem + [VMEM] * (len(operands) - smem),
        out_specs=[VMEM] * len(outs),
        scratch_shapes=list(scratch),
        compiler_params=pltpu.CompilerParams(vmem_limit_bytes=GRANT),
    )(*operands)


def pack_body(frames, width, count, *refs):
    place = refs[0][0]
    sources = refs[1 : 1 + count]
    outs = refs[1 + count :]
    for s in range(frames):
        target = lax.rem(place + s, frames)
        for i in range(count):
            outs[s][i] = sources[i][:, lane_block(target, width)]


def pack(place, sources, frames):
    tokens, full = sources[0].shape
    width = full // frames
    shape = jax.ShapeDtypeStruct((len(sources), tokens, width), BF16)
    return call(
        functools.partial(pack_body, frames, width, len(sources)),
        [shape] * frames,
        [place, *sources],
        smem=1,
    )


def unpack_body(frames, width, count, *refs):
    place = refs[0][0]
    blocks = refs[1 : 1 + frames]
    outs = refs[1 + frames :]
    for s in range(frames):
        source = lax.rem(place + s, frames)
        for i in range(count):
            outs[i][:, lane_block(source, width)] = blocks[s][i]


def unpack(place, blocks, frames):
    count, tokens, width = blocks[0].shape
    shape = jax.ShapeDtypeStruct((tokens, width * frames), BF16)
    return call(
        functools.partial(unpack_body, frames, width, count),
        [shape] * count,
        [place, *blocks],
        smem=1,
    )


def piece_of(target, late, row, frames):
    quarter = frames // 2
    inner = lax.rem(row, frames)
    far = jnp.bitwise_xor(lax.div(inner, quarter), late)
    return lax.div(target, quarter) * frames + far * quarter + lax.rem(target, quarter)


def both(parts):
    return jnp.concatenate(parts, axis=0)


def softmax_rows(query, keys, factor):
    plain = dot(keys, query, NT)
    top = jnp.max(plain, axis=0, keepdims=True)
    raised = jnp.exp2((plain - top) * (factor * LOG2E))
    total = jnp.sum(raised, axis=0, keepdims=True)
    return plain, raised * (1.0 / total)


def head_numbers(place, row, heads, split, frames):
    if not split:
        return [place * heads + h for h in range(heads)]
    each = heads // 2
    pieces = [piece_of(place, late, row, frames) for late in range(2)]
    return [pieces[h // each] * each + h % each for h in range(heads)]


def factors_of(place, row, scale_ref, heads, split, frames):
    inv_root = 1.0 / math.sqrt(HDH)
    return [scale_ref[n] * inv_root for n in head_numbers(place, row, heads, split, frames)]


def forward_body(frames, heads, slots, split, *refs):
    place_ref, row_ref, scale_ref, pattern_ref = refs[:4]
    blocks = refs[4 : 4 + frames]
    outs = refs[4 + frames : 4 + 2 * frames]
    held = refs[-1]
    place = place_ref[0]
    factors = factors_of(place, row_ref[0], scale_ref, heads, split, frames)
    for s in range(frames):
        frame = lax.rem(place + frames - s, frames)
        held[frame] = blocks[s][1:3]
    for s in range(frames):
        frame = lax.rem(place + frames - s, frames)
        chosen = [pattern_ref[frame, j] for j in range(slots)]
        for h in range(heads):
            at = slice(h * HDH, (h + 1) * HDH)
            keys = both([held[g, 0, :, at] for g in chosen])
            values = both([held[g, 1, :, at] for g in chosen])
            _, probs = softmax_rows(blocks[s][0, :, at], keys, factors[h])
            outs[s][0, :, at] = dot(probs.astype(BF16), values, TN).astype(BF16)


def forward(place, row, scale, pattern, blocks, split=False):
    frames = len(blocks)
    _, tokens, width = blocks[0].shape
    shape = jax.ShapeDtypeStruct((1, tokens, width), BF16)
    return call(
        functools.partial(forward_body, frames, width // HDH, pattern.shape[1], split),
        [shape] * frames,
        [place, row, scale, pattern, *blocks],
        smem=4,
        scratch=[pltpu.VMEM((frames, 2, tokens, width), BF16)],
    )


def backward_body(frames, heads, slots, half, before, *refs):
    place_ref, row_ref, scale_ref, pattern_ref = refs[:4]
    earlier = refs[4 : 4 + before]
    refs = refs[4 + before :]
    blocks = refs[:frames]
    grads = refs[frames : 2 * frames]
    outs = refs[2 * frames : 3 * frames]
    scale_out = refs[3 * frames]
    held, key_sum, value_sum = refs[3 * frames + 1 :]
    place = place_ref[0]
    tokens = tokens_of(blocks)
    inv_root = 1.0 / math.sqrt(HDH)
    if half is None:
        base = 0
        numbers = head_numbers(place, row_ref[0], heads, False, frames)
    else:
        base = half * heads * HDH
        numbers = head_numbers(place, row_ref[0], 2 * heads, True, frames)
        numbers = numbers[half * heads : (half + 1) * heads]
    factors = [scale_ref[n] * inv_root for n in numbers]
    part = slice(base, base + heads * HDH)
    key_sum[...] = jnp.zeros_like(key_sum)
    value_sum[...] = jnp.zeros_like(value_sum)
    for s in range(frames):
        frame = lax.rem(place + frames - s, frames)
        held[frame] = blocks[s][1:3, :, part]
    terms = [jnp.zeros((1, tokens), F32) for _ in range(heads)]
    for s in range(frames):
        frame = lax.rem(place + frames - s, frames)
        chosen = [pattern_ref[frame, j] for j in range(slots)]
        for h in range(heads):
            at = slice(h * HDH, (h + 1) * HDH)
            query = blocks[s][0, :, base + h * HDH : base + (h + 1) * HDH]
            grad = grads[s][0, :, at]
            keys = both([held[g, 0, :, at] for g in chosen])
            values = both([held[g, 1, :, at] for g in chosen])
            plain, probs = softmax_rows(query, keys, factors[h])
            prob_grads = dot(values, grad, NT)
            weighted = jnp.sum(prob_grads * probs, axis=0, keepdims=True)
            score_grads = probs * (prob_grads - weighted)
            terms[h] = terms[h] + jnp.sum(score_grads * plain, axis=0, keepdims=True)
            low = score_grads.astype(BF16)
            outs[s][0, :, at] = (dot(low, keys, TN) * factors[h]).astype(BF16)
            key_part = dot(low, query, NN)
            value_part = dot(probs.astype(BF16), grad, NN)
            for j, g in enumerate(chosen):
                rows = slice(j * tokens, (j + 1) * tokens)
                key_sum[g, :, at] += key_part[rows]
                value_sum[g, :, at] += value_part[rows]
    for s in range(frames):
        frame = lax.rem(place + frames - s, frames)
        for h in range(heads):
            at = slice(h * HDH, (h + 1) * HDH)
            outs[s][1, :, at] = (key_sum[frame, :, at] * factors[h]).astype(BF16)
        outs[s][2] = value_sum[frame].astype(BF16)
    lanes = lax.broadcasted_iota(jnp.int32, scale_out.shape, 1)
    result = earlier[0][...] if before else jnp.zeros(scale_out.shape, F32)
    for h in range(heads):
        term = jnp.sum(terms[h], axis=1, keepdims=True) * inv_root
        result = result + jnp.where(lanes == numbers[h], term, 0.0)
    scale_out[...] = result


def tokens_of(blocks):
    return blocks[0].shape[1]


def backward(place, row, scale, pattern, blocks, grads, half=None, before=()):
    frames = len(blocks)
    _, tokens, width = grads[0].shape
    shape = jax.ShapeDtypeStruct((3, tokens, width), BF16)
    result = call(
        functools.partial(
            backward_body, frames, width // HDH, pattern.shape[1], half, len(before)
        ),
        [shape] * frames + [jax.ShapeDtypeStruct((1, LANES), F32)],
        [place, row, scale, pattern, *before, *blocks, *grads],
        smem=4,
        scratch=[
            pltpu.VMEM((frames, 2, tokens, width), BF16),
            pltpu.VMEM((frames, tokens, width), F32),
            pltpu.VMEM((frames, tokens, width), F32),
        ],
    )
    return result[:frames], result[frames]


def context_grad_body(skip, count, cut, *refs):
    refs = refs[skip:]
    mine, other = refs[:2]
    weights = refs[2 : 2 + count]
    mine_out, other_out = refs[2 + count : 4 + count]
    tokens = mine.shape[0]
    rows = both([other[...], mine[...]])
    start = 0
    for w in weights:
        at = slice(start, start + w.shape[0])
        result = dot(rows, w[...], NT).astype(BF16)
        other_out[:, at] = result[:tokens]
        mine_out[:, at] = result[tokens:]
        start += w.shape[0]
    if cut:
        refs[4 + count][...] = weights[0][:cut]
        refs[5 + count][...] = weights[0][cut:]


def context_grads(mine, other, weights, scalars=(), cut=0):
    tokens = mine.shape[0]
    features = sum(w.shape[0] for w in weights)
    shapes = [jax.ShapeDtypeStruct((tokens, features), BF16)] * 2
    if cut:
        size, model = weights[0].shape
        shapes += [jax.ShapeDtypeStruct((n, model), BF16) for n in (cut, size - cut)]
    return call(
        functools.partial(context_grad_body, len(scalars), len(weights), cut),
        shapes,
        [*scalars, mine, other, *weights],
        smem=len(scalars),
    )


def project_body(count, columns, *refs):
    mine, other = refs[:2]
    weights = refs[2 : 2 + count]
    mine_out, other_out = refs[2 + count :]
    tokens = mine.shape[0]
    rows = both([other[...], mine[...]])
    start = 0
    total = None
    for w in weights:
        part = dot(rows[:, start : start + w.shape[0]], w[:, columns], NN)
        total = part if total is None else total + part
        start += w.shape[0]
    other_out[...] = total[:tokens].astype(other_out.dtype)
    mine_out[...] = total[tokens:]


def project_pair(mine, other, weights, first=0, last=None):
    tokens, _ = mine.shape
    columns = slice(first, weights[0].shape[1] if last is None else last)
    width = columns.stop - columns.start
    return call(
        functools.partial(project_body, len(weights), columns),
        [jax.ShapeDtypeStruct((tokens, width), kind) for kind in (F32, BF16)],
        [mine, other, *weights],
    )


def place_in_half(row, group):
    half = lax.div(row, group)
    return half, row - half * group


def join_body(frames, pieces, size, *refs):
    place = refs[0][0]
    half, inner = place_in_half(refs[1][0], sum(len(p) for p in pieces))
    count = len(pieces)
    mine = refs[2 : 2 + count]
    other = refs[2 + count : 2 + 2 * count]
    outs = refs[2 + 2 * count : 2 + 2 * count + frames]
    whole = refs[-1]
    group = sum(len(p) for p in pieces)
    width = whole.shape[1] // frames
    for h, sources in ((half, mine), (1 - half, other)):
        for source, names in zip(sources, pieces):
            for k, j in enumerate(names):
                spot = h * group + jnp.bitwise_xor(inner, j)
                whole[:, lane_block(spot, size)] = source[:, k * size : (k + 1) * size]
    for s in range(frames):
        outs[s][0] = whole[:, lane_block(lax.rem(place + s, frames), width)]


def join(place, row, mine, other, pieces, size, frames, full):
    tokens = mine[0].shape[0]
    if size % LANES == 0:
        shape = jax.ShapeDtypeStruct((1, tokens, full // frames), BF16)
        return call(
            functools.partial(join_body, frames, pieces, size),
            [shape] * frames,
            [place, row, *mine, *other],
            smem=2,
            scratch=[pltpu.VMEM((tokens, full), BF16)],
        )
    group = sum(len(p) for p in pieces)
    whole = jnp.zeros((tokens, full), BF16)
    half, inner = place_in_half(row[0], group)
    for h, sources in ((half, mine), (1 - half, other)):
        for source, names in zip(sources, pieces):
            for k, j in enumerate(names):
                spot = h * group + jnp.bitwise_xor(inner, j)
                piece = source[:, k * size : (k + 1) * size]
                whole = lax.dynamic_update_slice(whole, piece, (0, spot * size))
    return pack(place, [whole], frames)


def part_body(frames, count, size, *refs):
    place = refs[0][0]
    half, inner = place_in_half(refs[1][0], count)
    blocks = refs[2 : 2 + frames]
    keep, send, whole = refs[2 + frames :]
    width = whole.shape[1] // frames
    for s in range(frames):
        whole[:, lane_block(lax.rem(place + s, frames), width)] = blocks[s][0]
    for j in range(count):
        spot = jnp.bitwise_xor(inner, j)
        at = slice(j * size, (j + 1) * size)
        keep[:, at] = whole[:, lane_block(half * count + spot, size)]
        send[:, at] = whole[:, lane_block((1 - half) * count + spot, size)]


def part(place, row, blocks, count, size):
    frames = len(blocks)
    _, tokens, width = blocks[0].shape
    if size % LANES == 0:
        shape = jax.ShapeDtypeStruct((tokens, count * size), BF16)
        return call(
            functools.partial(part_body, frames, count, size),
            [shape, shape],
            [place, row, *blocks],
            smem=2,
            scratch=[pltpu.VMEM((tokens, width * frames), BF16)],
        )
    whole = unpack(place, blocks, frames)[0]
    half, inner = place_in_half(row[0], count)

    def half_of(h):
        spots = [h * count + jnp.bitwise_xor(inner, j) for j in range(count)]
        return jnp.concatenate(
            [lax.dynamic_slice_in_dim(whole, spot * size, size, axis=1) for spot in spots], axis=1
        )

    return half_of(half), half_of(1 - half)


def split_pack_body(frames, count, *refs):
    place, row = refs[0][0], refs[1][0]
    sources = refs[2 : 2 + count]
    outs = refs[2 + count : 2 + count + frames]
    held, arrived = refs[2 + count + frames :]
    size = outs[0].shape[2] // 2
    copies = [
        pltpu.make_async_copy(sources[i], held.at[i], arrived.at[i]) for i in range(count)
    ]
    for copy in copies:
        copy.start()
    for i in range(count):
        copies[i].wait()
        for s in range(frames):
            target = lax.rem(place + s, frames)
            for late in range(2):
                piece = piece_of(target, late, row, frames)
                at = slice(late * size, (late + 1) * size)
                outs[s][i, :, at] = held[i, :, lane_block(piece, size)]


def split_pack(place, row, sources, frames):
    tokens, full = sources[0].shape
    count = len(sources)
    shape = jax.ShapeDtypeStruct((count, tokens, full // frames), BF16)
    return pl.pallas_call(
        functools.partial(split_pack_body, frames, count),
        out_shape=[shape] * frames,
        in_specs=[SMEM] * 2 + [pl.BlockSpec(memory_space=pltpu.HBM)] * count,
        out_specs=[VMEM] * frames,
        scratch_shapes=[
            pltpu.VMEM((count, tokens, full), BF16),
            pltpu.SemaphoreType.DMA((count,)),
        ],
        compiler_params=pltpu.CompilerParams(vmem_limit_bytes=GRANT),
        name="pack",
    )(place, row, *sources)


def split_unpack_body(frames, count, *refs):
    place, row = refs[0][0], refs[1][0]
    blocks = (refs[2 : 2 + frames], refs[2 + frames : 2 + 2 * frames])
    scales = refs[2 + 2 * frames : 2 + 3 * frames]
    outs = refs[2 + 3 * frames : -1]
    size = blocks[0][0].shape[2]
    for late in range(2):
        for s in range(frames):
            piece = piece_of(lax.rem(place + s, frames), late, row, frames)
            for i in range(count):
                outs[i][:, lane_block(piece, size)] = blocks[late][s][i]
    total = functools.reduce(jnp.add, [s[...] for s in scales])
    refs[-1][...] = total[:, : refs[-1].shape[1]]


def split_unpack(place, row, early, late, scales, heads):
    frames = len(early)
    count, tokens, size = early[0].shape
    shape = jax.ShapeDtypeStruct((tokens, 2 * size * frames), BF16)
    return call(
        functools.partial(split_unpack_body, frames, count),
        [shape] * count + [jax.ShapeDtypeStruct((1, heads), F32)],
        [place, row, *early, *late, *scales],
        smem=2,
    )


def split_join_body(frames, count, *refs):
    place, row = refs[0][0], refs[1][0]
    mine = refs[2 : 2 + count]
    other = refs[2 + count : 2 + 2 * count]
    outs = refs[2 + 2 * count : 2 + 2 * count + frames]
    own, theirs = refs[2 + 2 * count + frames :]
    quarter = frames // 2
    size = own.shape[1] // quarter
    half, inner = place_in_half(row, frames)
    for sources, whole in ((mine, own), (other, theirs)):
        start = 0
        for source in sources:
            whole[:, start : start + source.shape[1]] = source[...]
            start += source.shape[1]
    for s in range(frames):
        target = lax.rem(place + s, frames)
        near = jnp.bitwise_xor(lax.rem(target, quarter), lax.rem(inner, quarter))
        at = lane_block(near, size)
        outs[s][0] = jnp.where(lax.div(target, quarter) == half, own[:, at], theirs[:, at])


def split_join(place, row, mine, other, frames):
    tokens = mine[0].shape[0]
    width = sum(m.shape[1] for m in mine)
    shape = jax.ShapeDtypeStruct((1, tokens, 2 * width // frames), BF16)
    return call(
        functools.partial(split_join_body, frames, len(mine)),
        [shape] * frames,
        [place, row, *mine, *other],
        smem=2,
        scratch=[pltpu.VMEM((tokens, width), BF16)] * 2,
    )


def split_part_body(frames, *refs):
    place, row = refs[0][0], refs[1][0]
    blocks = refs[2 : 2 + frames]
    keep, send, whole = refs[2 + frames :]
    size = keep.shape[1] // frames
    half, inner = place_in_half(row, frames)
    for s in range(frames):
        for late in range(2):
            piece = piece_of(lax.rem(place + s, frames), late, row, frames)
            whole[:, lane_block(piece, size)] = blocks[s][0, :, late * size : (late + 1) * size]
    for j in range(frames):
        spot = jnp.bitwise_xor(inner, j)
        at = slice(j * size, (j + 1) * size)
        keep[:, at] = whole[:, lane_block(half * frames + spot, size)]
        send[:, at] = whole[:, lane_block((1 - half) * frames + spot, size)]


def split_part(place, row, blocks):
    frames = len(blocks)
    _, tokens, width = blocks[0].shape
    shape = jax.ShapeDtypeStruct((tokens, frames * width // 2), BF16)
    return call(
        functools.partial(split_part_body, frames),
        [shape, shape],
        [place, row, *blocks],
        smem=2,
        scratch=[pltpu.VMEM((tokens, width * frames), BF16)],
    )


def exchange(blocks, sign):
    frames = len(blocks)

    def shift(s):
        return [(i, (i + sign * s) % frames) for i in range(frames)]

    return [blocks[0]] + [lax.ppermute(blocks[s], "frame", shift(s)) for s in range(1, frames)]


def swap(x, bit):
    group = lax.axis_size("dp")
    return lax.ppermute(x, "dp", [(i, i ^ bit) for i in range(group)])


def gather_half(out_weight, count):
    weights = {0: out_weight}
    bit = count // 2
    while bit:
        for j in list(weights):
            weights[j ^ bit] = swap(weights[j], bit)
        bit //= 2
    return [weights[j] for j in range(count)]


def attend_body(counts, *refs):
    contexts = refs[: len(counts)]
    out = refs[-1]
    width = out.shape[1]
    tile = math.gcd(width, 768)
    for first in range(0, width, tile):
        columns = slice(first, first + tile)
        weights = list(refs[len(counts) : -1])
        total = None
        for context, pieces in zip(contexts, counts):
            start = 0
            for chunks in pieces:
                piece = both([weights.pop(0)[:, columns] for _ in range(chunks)])
                part = dot(context[:, start : start + piece.shape[0]], piece, NN)
                total = part if total is None else total + part
                start += piece.shape[0]
        out[:, columns] = total.astype(BF16)


def attend(contexts, weights):
    tokens, _ = contexts[0].shape
    flat = [c for pieces in weights for chunks in pieces for c in chunks]
    counts = [[len(chunks) for chunks in pieces] for pieces in weights]
    return call(
        functools.partial(attend_body, counts),
        [jax.ShapeDtypeStruct((tokens, flat[0].shape[1]), BF16)],
        [*contexts, *flat],
    )[0]


def local_split(queries, key_states, value_states, head_scale, out_weight, frame_pattern, out_grad):
    frames = lax.axis_size("frame")
    group = lax.axis_size("dp")
    tokens, full = queries.shape[2:]
    model = out_grad.shape[3]
    heads = full // HDH
    place = lax.axis_index("frame").astype(jnp.int32).reshape(1)
    row = lax.axis_index("dp").astype(jnp.int32).reshape(1)

    grad_rows = out_grad[0, 0]
    other_rows = swap(grad_rows, frames)
    weights = gather_half(out_weight, frames)
    early, late = weights[: frames // 2], weights[frames // 2 :]
    cut = out_weight.shape[0] * 7 // 16

    sent = split_pack(place, row, [queries[0, 0], key_states[0, 0], value_states[0, 0]], frames)
    blocks = exchange(sent, 1)

    mine, theirs, *chunks = context_grads(
        grad_rows, other_rows, early, [frame_pattern], cut
    )
    other = swap(theirs, frames)
    other_first = swap(chunks[0], frames)
    other_last = swap(chunks[1], frames)
    far_first = swap(other_first, frames // 2)
    far_last = swap(other_last, frames // 2)
    sent = split_join(place, row, [mine], [other], frames)
    grads_early = exchange(sent, 1)
    mine, other = [], []
    for weight in late:
        own, theirs = context_grads(grad_rows, other_rows, [weight])
        mine.append(own)
        other.append(swap(theirs, frames))
    context = forward(place, row, head_scale, frame_pattern, blocks, True)
    context = exchange(context, -1)
    sent = split_join(place, row, mine, other, frames)
    grads_late = exchange(sent, 1)

    sent, scale_early = backward(
        place, row, head_scale, frame_pattern, blocks, grads_early, 0
    )
    done_early = exchange(sent, -1)
    sent, scale_part = backward(
        place, row, head_scale, frame_pattern, blocks, grads_late, 1, [scale_early]
    )
    done_late = exchange(sent, -1)

    contexts = split_part(place, row, context)
    others = {0: [other_first, other_last], frames // 2: [far_first, far_last]}
    bit = frames // 4
    while bit:
        for j in list(others):
            others[j ^ bit] = [swap(c, bit) for c in others[j]]
        bit //= 2
    others = [others[j] for j in range(frames)]
    attended = attend(contexts, [[[w] for w in weights], others])

    bit = group // 2
    while bit:
        scale_part = scale_part + swap(scale_part, bit)
        bit //= 2
    scales = exchange([scale_part] * frames, 1)

    query_grad, key_grad, value_grad, scale_sum = split_unpack(
        place, row, done_early, done_late, scales, heads
    )
    shape = (1, 1, tokens, full)
    return (
        attended.reshape(1, 1, tokens, model),
        query_grad.reshape(shape),
        key_grad.reshape(shape),
        value_grad.reshape(shape),
        scale_sum[0, :heads],
    )


def local_plain(queries, key_states, value_states, head_scale, out_weight, frame_pattern, out_grad):
    frames = lax.axis_size("frame")
    group = lax.axis_size("dp")
    tokens, full = queries.shape[2:]
    model = out_grad.shape[3]
    heads = full // HDH
    count = group // 2
    size = out_weight.shape[0]
    place = lax.axis_index("frame").astype(jnp.int32).reshape(1)
    row = lax.axis_index("dp").astype(jnp.int32).reshape(1)

    grad_rows = out_grad[0, 0]
    other_rows = swap(grad_rows, count)
    weights = gather_half(out_weight, count)
    early, late = weights[: count // 2], weights[count // 2 :]
    names = (list(range(count // 2)), list(range(count // 2, count)))

    sent = pack(place, [queries[0, 0], key_states[0, 0], value_states[0, 0]], frames)
    blocks = exchange(sent, 1)
    context = exchange(forward(place, row, head_scale, frame_pattern, blocks), -1)
    mine, other = [], []
    for part_weights in (early, late):
        own, theirs = context_grads(grad_rows, other_rows, part_weights)
        mine.append(own)
        other.append(swap(theirs, count))
    sent = join(place, row, mine, other, names, size, frames, full)
    grads = exchange(sent, 1)

    keep, send = part(place, row, context, count, size)
    own, theirs = project_pair(keep, swap(send, count), weights)
    attended = (own + swap(theirs, count)).astype(BF16)

    sent, scale_part = backward(place, row, head_scale, frame_pattern, blocks, grads)
    blocks = exchange(sent, -1)
    bit = group // 2
    while bit:
        scale_part = scale_part + swap(scale_part, bit)
        bit //= 2
    scale_sum = functools.reduce(jnp.add, exchange([scale_part] * frames, 1))
    query_grad, key_grad, value_grad = unpack(place, blocks, frames)
    shape = (1, 1, tokens, full)
    return (
        attended.reshape(1, 1, tokens, model),
        query_grad.reshape(shape),
        key_grad.reshape(shape),
        value_grad.reshape(shape),
        scale_sum[0, :heads],
    )


def local(*args):
    frames = lax.axis_size("frame")
    size = args[4].shape[0]
    if lax.axis_size("dp") == 2 * frames and size % HDH == 0:
        return local_split(*args)
    return local_plain(*args)


def solution(mesh):
    spec = P("dp", "frame", None, None)
    return jax.shard_map(
        local,
        mesh=mesh,
        in_specs=(spec, spec, spec, P(), P("dp", None), P(), spec),
        out_specs=(spec, spec, spec, spec, P()),
        check_vma=False,
    )
```

```python
import functools
import math

import jax
import jax.numpy as jnp
from jax import lax
from jax.experimental import pallas as pl
from jax.experimental.pallas import tpu as pltpu
from jax.sharding import PartitionSpec as P


HDH = 128
LANES = 128
LOG2E = 1.0 / math.log(2.0)


GRANT = 16 * 1024 * 1024
F32 = jnp.float32
BF16 = jnp.bfloat16
NT = (((1,), (1,)), ((), ()))
NN = (((1,), (0,)), ((), ()))
TN = (((0,), (0,)), ((), ()))
SMEM = pl.BlockSpec(memory_space=pltpu.SMEM)
VMEM = pl.BlockSpec(memory_space=pltpu.VMEM)


def dot(a, b, dims):
    return lax.dot_general(a, b, dims, preferred_element_type=F32)


def lane_block(index, width):
    return pl.ds(pl.multiple_of(index * width, LANES), width)


def call(body, outs, operands, smem=0, scratch=(), grant=GRANT):
    return pl.pallas_call(
        body,
        out_shape=outs,
        in_specs=[SMEM] * smem + [VMEM] * (len(operands) - smem),
        out_specs=[VMEM] * len(outs),
        scratch_shapes=list(scratch),
        compiler_params=pltpu.CompilerParams(vmem_limit_bytes=grant),
    )(*operands)


def pack_body(frames, width, count, *refs):
    place = refs[0][0]
    sources = refs[1 : 1 + count]
    outs = refs[1 + count :]
    for s in range(frames):
        target = lax.rem(place + s, frames)
        for i in range(count):
            outs[s][i] = sources[i][:, lane_block(target, width)]


def pack(place, sources, frames):
    tokens, full = sources[0].shape
    width = full // frames
    shape = jax.ShapeDtypeStruct((len(sources), tokens, width), BF16)
    return call(
        functools.partial(pack_body, frames, width, len(sources)),
        [shape] * frames,
        [place, *sources],
        smem=1,
    )


def unpack_body(frames, width, count, *refs):
    place = refs[0][0]
    blocks = refs[1 : 1 + frames]
    outs = refs[1 + frames :]
    for s in range(frames):
        source = lax.rem(place + s, frames)
        for i in range(count):
            outs[i][:, lane_block(source, width)] = blocks[s][i]


def unpack(place, blocks, frames):
    count, tokens, width = blocks[0].shape
    shape = jax.ShapeDtypeStruct((tokens, width * frames), BF16)
    return call(
        functools.partial(unpack_body, frames, width, count),
        [shape] * count,
        [place, *blocks],
        smem=1,
    )


def piece_of(target, late, row, frames):
    quarter = frames // 2
    inner = lax.rem(row, frames)
    far = jnp.bitwise_xor(lax.div(inner, quarter), late)
    return lax.div(target, quarter) * frames + far * quarter + lax.rem(target, quarter)


def both(parts):
    return jnp.concatenate(parts, axis=0)


def softmax_rows(query, keys, factor):
    plain = dot(keys, query, NT)
    top = jnp.max(plain, axis=0, keepdims=True)
    raised = jnp.exp2((plain - top) * (factor * LOG2E))
    total = jnp.sum(raised, axis=0, keepdims=True)
    return plain, raised * (1.0 / total)


def head_numbers(place, row, heads, split, frames):
    if not split:
        return [place * heads + h for h in range(heads)]
    each = heads // 2
    pieces = [piece_of(place, late, row, frames) for late in range(2)]
    return [pieces[h // each] * each + h % each for h in range(heads)]


def factors_of(place, row, scale_ref, heads, split, frames):
    inv_root = 1.0 / math.sqrt(HDH)
    return [scale_ref[n] * inv_root for n in head_numbers(place, row, heads, split, frames)]


def forward_body(frames, heads, slots, split, *refs):
    place_ref, row_ref, scale_ref, pattern_ref = refs[:4]
    blocks = refs[4 : 4 + frames]
    outs = refs[4 + frames : 4 + 2 * frames]
    held = refs[-1]
    place = place_ref[0]
    factors = factors_of(place, row_ref[0], scale_ref, heads, split, frames)
    for s in range(frames):
        frame = lax.rem(place + frames - s, frames)
        held[frame] = blocks[s][1:3]
    for s in range(frames):
        frame = lax.rem(place + frames - s, frames)
        chosen = [pattern_ref[frame, j] for j in range(slots)]
        for h in range(heads):
            at = slice(h * HDH, (h + 1) * HDH)
            keys = both([held[g, 0, :, at] for g in chosen])
            values = both([held[g, 1, :, at] for g in chosen])
            _, probs = softmax_rows(blocks[s][0, :, at], keys, factors[h])
            outs[s][0, :, at] = dot(probs.astype(BF16), values, TN).astype(BF16)


def forward(place, row, scale, pattern, blocks, split=False):
    frames = len(blocks)
    _, tokens, width = blocks[0].shape
    shape = jax.ShapeDtypeStruct((1, tokens, width), BF16)
    return call(
        functools.partial(forward_body, frames, width // HDH, pattern.shape[1], split),
        [shape] * frames,
        [place, row, scale, pattern, *blocks],
        smem=4,
        scratch=[pltpu.VMEM((frames, 2, tokens, width), BF16)],
    )


def backward_body(frames, heads, slots, half, before, *refs):
    place_ref, row_ref, scale_ref, pattern_ref = refs[:4]
    earlier = refs[4 : 4 + before]
    refs = refs[4 + before :]
    blocks = refs[:frames]
    grads = refs[frames : 2 * frames]
    outs = refs[2 * frames : 3 * frames]
    scale_out = refs[3 * frames]
    held, key_sum, value_sum = refs[3 * frames + 1 :]
    place = place_ref[0]
    tokens = tokens_of(blocks)
    inv_root = 1.0 / math.sqrt(HDH)
    if half is None:
        base = 0
        numbers = head_numbers(place, row_ref[0], heads, False, frames)
    else:
        base = half * heads * HDH
        numbers = head_numbers(place, row_ref[0], 2 * heads, True, frames)
        numbers = numbers[half * heads : (half + 1) * heads]
    factors = [scale_ref[n] * inv_root for n in numbers]
    part = slice(base, base + heads * HDH)
    key_sum[...] = jnp.zeros_like(key_sum)
    value_sum[...] = jnp.zeros_like(value_sum)
    for s in range(frames):
        frame = lax.rem(place + frames - s, frames)
        held[frame] = blocks[s][1:3, :, part]
    terms = [jnp.zeros((1, tokens), F32) for _ in range(heads)]
    for s in range(frames):
        frame = lax.rem(place + frames - s, frames)
        chosen = [pattern_ref[frame, j] for j in range(slots)]
        for h in range(heads):
            at = slice(h * HDH, (h + 1) * HDH)
            query = blocks[s][0, :, base + h * HDH : base + (h + 1) * HDH]
            grad = grads[s][0, :, at]
            keys = both([held[g, 0, :, at] for g in chosen])
            values = both([held[g, 1, :, at] for g in chosen])
            plain, probs = softmax_rows(query, keys, factors[h])
            prob_grads = dot(values, grad, NT)
            weighted = jnp.sum(prob_grads * probs, axis=0, keepdims=True)
            score_grads = probs * (prob_grads - weighted)
            terms[h] = terms[h] + jnp.sum(score_grads * plain, axis=0, keepdims=True)
            low = score_grads.astype(BF16)
            outs[s][0, :, at] = (dot(low, keys, TN) * factors[h]).astype(BF16)
            key_part = dot(low, query, NN)
            value_part = dot(probs.astype(BF16), grad, NN)
            for j, g in enumerate(chosen):
                rows = slice(j * tokens, (j + 1) * tokens)
                key_sum[g, :, at] += key_part[rows]
                value_sum[g, :, at] += value_part[rows]
    for s in range(frames):
        frame = lax.rem(place + frames - s, frames)
        for h in range(heads):
            at = slice(h * HDH, (h + 1) * HDH)
            outs[s][1, :, at] = (key_sum[frame, :, at] * factors[h]).astype(BF16)
        outs[s][2] = value_sum[frame].astype(BF16)
    lanes = lax.broadcasted_iota(jnp.int32, scale_out.shape, 1)
    result = earlier[0][...] if before else jnp.zeros(scale_out.shape, F32)
    for h in range(heads):
        term = jnp.sum(terms[h], axis=1, keepdims=True) * inv_root
        result = result + jnp.where(lanes == numbers[h], term, 0.0)
    scale_out[...] = result


def tokens_of(blocks):
    return blocks[0].shape[1]


def backward(place, row, scale, pattern, blocks, grads, half=None, before=()):
    frames = len(blocks)
    _, tokens, width = grads[0].shape
    shape = jax.ShapeDtypeStruct((3, tokens, width), BF16)
    result = call(
        functools.partial(
            backward_body, frames, width // HDH, pattern.shape[1], half, len(before)
        ),
        [shape] * frames + [jax.ShapeDtypeStruct((1, LANES), F32)],
        [place, row, scale, pattern, *before, *blocks, *grads],
        smem=4,
        scratch=[
            pltpu.VMEM((frames, 2, tokens, width), BF16),
            pltpu.VMEM((frames, tokens, width), F32),
            pltpu.VMEM((frames, tokens, width), F32),
        ],
    )
    return result[:frames], result[frames]


def context_grad_body(skip, count, cuts, *refs):
    refs = refs[skip:]
    mine, other = refs[:2]
    weights = refs[2 : 2 + count]
    mine_out, other_out = refs[2 + count : 4 + count]
    tokens = mine.shape[0]
    rows = both([other[...], mine[...]])
    start = 0
    for w in weights:
        at = slice(start, start + w.shape[0])
        result = dot(rows, w[...], NT).astype(BF16)
        other_out[:, at] = result[:tokens]
        mine_out[:, at] = result[tokens:]
        start += w.shape[0]
    start = 0
    for chunk, size in zip(refs[4 + count :], cuts):
        chunk[...] = weights[0][start : start + size]
        start += size


def context_grads(mine, other, weights, scalars=(), cuts=()):
    tokens = mine.shape[0]
    features = sum(w.shape[0] for w in weights)
    shapes = [jax.ShapeDtypeStruct((tokens, features), BF16)] * 2
    shapes += [jax.ShapeDtypeStruct((n, weights[0].shape[1]), BF16) for n in cuts]
    return call(
        functools.partial(context_grad_body, len(scalars), len(weights), cuts),
        shapes,
        [*scalars, mine, other, *weights],
        smem=len(scalars),
    )


def project_body(count, columns, *refs):
    mine, other = refs[:2]
    weights = refs[2 : 2 + count]
    mine_out, other_out = refs[2 + count :]
    tokens = mine.shape[0]
    rows = both([other[...], mine[...]])
    start = 0
    total = None
    for w in weights:
        part = dot(rows[:, start : start + w.shape[0]], w[:, columns], NN)
        total = part if total is None else total + part
        start += w.shape[0]
    other_out[...] = total[:tokens].astype(other_out.dtype)
    mine_out[...] = total[tokens:]


def project_pair(mine, other, weights, first=0, last=None):
    tokens, _ = mine.shape
    columns = slice(first, weights[0].shape[1] if last is None else last)
    width = columns.stop - columns.start
    return call(
        functools.partial(project_body, len(weights), columns),
        [jax.ShapeDtypeStruct((tokens, width), kind) for kind in (F32, BF16)],
        [mine, other, *weights],
    )


def place_in_half(row, group):
    half = lax.div(row, group)
    return half, row - half * group


def join_body(frames, pieces, size, *refs):
    place = refs[0][0]
    half, inner = place_in_half(refs[1][0], sum(len(p) for p in pieces))
    count = len(pieces)
    mine = refs[2 : 2 + count]
    other = refs[2 + count : 2 + 2 * count]
    outs = refs[2 + 2 * count : 2 + 2 * count + frames]
    whole = refs[-1]
    group = sum(len(p) for p in pieces)
    width = whole.shape[1] // frames
    for h, sources in ((half, mine), (1 - half, other)):
        for source, names in zip(sources, pieces):
            for k, j in enumerate(names):
                spot = h * group + jnp.bitwise_xor(inner, j)
                whole[:, lane_block(spot, size)] = source[:, k * size : (k + 1) * size]
    for s in range(frames):
        outs[s][0] = whole[:, lane_block(lax.rem(place + s, frames), width)]


def join(place, row, mine, other, pieces, size, frames, full):
    tokens = mine[0].shape[0]
    if size % LANES == 0:
        shape = jax.ShapeDtypeStruct((1, tokens, full // frames), BF16)
        return call(
            functools.partial(join_body, frames, pieces, size),
            [shape] * frames,
            [place, row, *mine, *other],
            smem=2,
            scratch=[pltpu.VMEM((tokens, full), BF16)],
        )
    group = sum(len(p) for p in pieces)
    whole = jnp.zeros((tokens, full), BF16)
    half, inner = place_in_half(row[0], group)
    for h, sources in ((half, mine), (1 - half, other)):
        for source, names in zip(sources, pieces):
            for k, j in enumerate(names):
                spot = h * group + jnp.bitwise_xor(inner, j)
                piece = source[:, k * size : (k + 1) * size]
                whole = lax.dynamic_update_slice(whole, piece, (0, spot * size))
    return pack(place, [whole], frames)


def part_body(frames, count, size, *refs):
    place = refs[0][0]
    half, inner = place_in_half(refs[1][0], count)
    blocks = refs[2 : 2 + frames]
    keep, send, whole = refs[2 + frames :]
    width = whole.shape[1] // frames
    for s in range(frames):
        whole[:, lane_block(lax.rem(place + s, frames), width)] = blocks[s][0]
    for j in range(count):
        spot = jnp.bitwise_xor(inner, j)
        at = slice(j * size, (j + 1) * size)
        keep[:, at] = whole[:, lane_block(half * count + spot, size)]
        send[:, at] = whole[:, lane_block((1 - half) * count + spot, size)]


def part(place, row, blocks, count, size):
    frames = len(blocks)
    _, tokens, width = blocks[0].shape
    if size % LANES == 0:
        shape = jax.ShapeDtypeStruct((tokens, count * size), BF16)
        return call(
            functools.partial(part_body, frames, count, size),
            [shape, shape],
            [place, row, *blocks],
            smem=2,
            scratch=[pltpu.VMEM((tokens, width * frames), BF16)],
        )
    whole = unpack(place, blocks, frames)[0]
    half, inner = place_in_half(row[0], count)

    def half_of(h):
        spots = [h * count + jnp.bitwise_xor(inner, j) for j in range(count)]
        return jnp.concatenate(
            [lax.dynamic_slice_in_dim(whole, spot * size, size, axis=1) for spot in spots], axis=1
        )

    return half_of(half), half_of(1 - half)


def split_pack_body(frames, count, *refs):
    place, row = refs[0][0], refs[1][0]
    sources = refs[2 : 2 + count]
    outs = refs[2 + count :]
    size = outs[0].shape[2] // 2
    for s in range(frames):
        target = lax.rem(place + s, frames)
        for late in range(2):
            piece = piece_of(target, late, row, frames)
            for i in range(count):
                at = slice(late * size, (late + 1) * size)
                outs[s][i, :, at] = sources[i][:, lane_block(piece, size)]


def split_pack(place, row, sources, frames):
    tokens, full = sources[0].shape
    shape = jax.ShapeDtypeStruct((len(sources), tokens, full // frames), BF16)
    return call(
        functools.partial(split_pack_body, frames, len(sources)),
        [shape] * frames,
        [place, row, *sources],
        smem=2,
        grant=60 * 1024 * 1024,
    )


def split_unpack_body(frames, count, *refs):
    place, row = refs[0][0], refs[1][0]
    blocks = (refs[2 : 2 + frames], refs[2 + frames : 2 + 2 * frames])
    scales = refs[2 + 2 * frames : 2 + 3 * frames]
    outs = refs[2 + 3 * frames : -1]
    size = blocks[0][0].shape[2]
    for late in range(2):
        for s in range(frames):
            piece = piece_of(lax.rem(place + s, frames), late, row, frames)
            for i in range(count):
                outs[i][:, lane_block(piece, size)] = blocks[late][s][i]
    total = functools.reduce(jnp.add, [s[...] for s in scales])
    refs[-1][...] = total[:, : refs[-1].shape[1]]


def split_unpack(place, row, early, late, scales, heads):
    frames = len(early)
    count, tokens, size = early[0].shape
    shape = jax.ShapeDtypeStruct((tokens, 2 * size * frames), BF16)
    return call(
        functools.partial(split_unpack_body, frames, count),
        [shape] * count + [jax.ShapeDtypeStruct((1, heads), F32)],
        [place, row, *early, *late, *scales],
        smem=2,
    )


def split_join_body(frames, count, *refs):
    place, row = refs[0][0], refs[1][0]
    mine = refs[2 : 2 + count]
    other = refs[2 + count : 2 + 2 * count]
    outs = refs[2 + 2 * count : 2 + 2 * count + frames]
    own, theirs = refs[2 + 2 * count + frames :]
    quarter = frames // 2
    size = own.shape[1] // quarter
    half, inner = place_in_half(row, frames)
    for sources, whole in ((mine, own), (other, theirs)):
        start = 0
        for source in sources:
            whole[:, start : start + source.shape[1]] = source[...]
            start += source.shape[1]
    for s in range(frames):
        target = lax.rem(place + s, frames)
        near = jnp.bitwise_xor(lax.rem(target, quarter), lax.rem(inner, quarter))
        at = lane_block(near, size)
        outs[s][0] = jnp.where(lax.div(target, quarter) == half, own[:, at], theirs[:, at])


def split_join(place, row, mine, other, frames):
    tokens = mine[0].shape[0]
    width = sum(m.shape[1] for m in mine)
    shape = jax.ShapeDtypeStruct((1, tokens, 2 * width // frames), BF16)
    return call(
        functools.partial(split_join_body, frames, len(mine)),
        [shape] * frames,
        [place, row, *mine, *other],
        smem=2,
        scratch=[pltpu.VMEM((tokens, width), BF16)] * 2,
    )


def split_part_body(frames, *refs):
    place, row = refs[0][0], refs[1][0]
    blocks = refs[2 : 2 + frames]
    keep, send, whole = refs[2 + frames :]
    size = keep.shape[1] // frames
    half, inner = place_in_half(row, frames)
    for s in range(frames):
        for late in range(2):
            piece = piece_of(lax.rem(place + s, frames), late, row, frames)
            whole[:, lane_block(piece, size)] = blocks[s][0, :, late * size : (late + 1) * size]
    for j in range(frames):
        spot = jnp.bitwise_xor(inner, j)
        at = slice(j * size, (j + 1) * size)
        keep[:, at] = whole[:, lane_block(half * frames + spot, size)]
        send[:, at] = whole[:, lane_block((1 - half) * frames + spot, size)]


def split_part(place, row, blocks):
    frames = len(blocks)
    _, tokens, width = blocks[0].shape
    shape = jax.ShapeDtypeStruct((tokens, frames * width // 2), BF16)
    return call(
        functools.partial(split_part_body, frames),
        [shape, shape],
        [place, row, *blocks],
        smem=2,
        scratch=[pltpu.VMEM((tokens, width * frames), BF16)],
    )


def exchange(blocks, sign):
    frames = len(blocks)

    def shift(s):
        return [(i, (i + sign * s) % frames) for i in range(frames)]

    return [blocks[0]] + [lax.ppermute(blocks[s], "frame", shift(s)) for s in range(1, frames)]


def swap(x, bit):
    group = lax.axis_size("dp")
    return lax.ppermute(x, "dp", [(i, i ^ bit) for i in range(group)])


def gather_half(out_weight, count):
    weights = {0: out_weight}
    bit = count // 2
    while bit:
        for j in list(weights):
            weights[j ^ bit] = swap(weights[j], bit)
        bit //= 2
    return [weights[j] for j in range(count)]


def attend_body(counts, *refs):
    contexts = refs[: len(counts)]
    out = refs[-1]
    width = out.shape[1]
    tile = math.gcd(width, 768)
    for first in range(0, width, tile):
        columns = slice(first, first + tile)
        weights = list(refs[len(counts) : -1])
        total = None
        for context, pieces in zip(contexts, counts):
            start = 0
            for chunks in pieces:
                piece = both([weights.pop(0)[:, columns] for _ in range(chunks)])
                part = dot(context[:, start : start + piece.shape[0]], piece, NN)
                total = part if total is None else total + part
                start += piece.shape[0]
        out[:, columns] = total.astype(BF16)


def attend(contexts, weights):
    tokens, _ = contexts[0].shape
    flat = [c for pieces in weights for chunks in pieces for c in chunks]
    counts = [[len(chunks) for chunks in pieces] for pieces in weights]
    return call(
        functools.partial(attend_body, counts),
        [jax.ShapeDtypeStruct((tokens, flat[0].shape[1]), BF16)],
        [*contexts, *flat],
    )[0]


def local_split(queries, key_states, value_states, head_scale, out_weight, frame_pattern, out_grad):
    frames = lax.axis_size("frame")
    group = lax.axis_size("dp")
    tokens, full = queries.shape[2:]
    model = out_grad.shape[3]
    heads = full // HDH
    place = lax.axis_index("frame").astype(jnp.int32).reshape(1)
    row = lax.axis_index("dp").astype(jnp.int32).reshape(1)

    grad_rows = out_grad[0, 0]
    other_rows = swap(grad_rows, frames)
    weights = gather_half(out_weight, frames)
    early, late = weights[: frames // 2], weights[frames // 2 :]
    cuts = [out_weight.shape[0] * n // 16 for n in (6, 4, 6)]

    sent = split_pack(place, row, [queries[0, 0], key_states[0, 0], value_states[0, 0]], frames)
    blocks = exchange(sent, 1)

    mine, theirs, *chunks = context_grads(
        grad_rows, other_rows, early, [frame_pattern], cuts
    )
    other = swap(theirs, frames)
    crossed, far = [], []
    for i, chunk in enumerate(chunks):
        crossed.append(swap(chunk, frames))
        far.append(swap(crossed[i], frames // 2))
    sent = split_join(place, row, [mine], [other], frames)
    grads_early = exchange(sent, 1)
    mine, other = [], []
    for weight in late:
        own, theirs = context_grads(grad_rows, other_rows, [weight])
        mine.append(own)
        other.append(swap(theirs, frames))
    context = forward(place, row, head_scale, frame_pattern, blocks, True)
    context = exchange(context, -1)
    sent = split_join(place, row, mine, other, frames)
    grads_late = exchange(sent, 1)

    sent, scale_early = backward(
        place, row, head_scale, frame_pattern, blocks, grads_early, 0
    )
    done_early = exchange(sent, -1)
    sent, scale_part = backward(
        place, row, head_scale, frame_pattern, blocks, grads_late, 1, [scale_early]
    )
    done_late = exchange(sent, -1)

    contexts = split_part(place, row, context)
    others = {0: crossed, frames // 2: far}
    bit = frames // 4
    while bit:
        for j in list(others):
            others[j ^ bit] = [swap(c, bit) for c in others[j]]
        bit //= 2
    others = [others[j] for j in range(frames)]
    attended = attend(contexts, [[[w] for w in weights], others])

    bit = group // 2
    while bit:
        scale_part = scale_part + swap(scale_part, bit)
        bit //= 2
    scales = exchange([scale_part] * frames, 1)

    query_grad, key_grad, value_grad, scale_sum = split_unpack(
        place, row, done_early, done_late, scales, heads
    )
    shape = (1, 1, tokens, full)
    return (
        attended.reshape(1, 1, tokens, model),
        query_grad.reshape(shape),
        key_grad.reshape(shape),
        value_grad.reshape(shape),
        scale_sum[0, :heads],
    )


def local_plain(queries, key_states, value_states, head_scale, out_weight, frame_pattern, out_grad):
    frames = lax.axis_size("frame")
    group = lax.axis_size("dp")
    tokens, full = queries.shape[2:]
    model = out_grad.shape[3]
    heads = full // HDH
    count = group // 2
    size = out_weight.shape[0]
    place = lax.axis_index("frame").astype(jnp.int32).reshape(1)
    row = lax.axis_index("dp").astype(jnp.int32).reshape(1)

    grad_rows = out_grad[0, 0]
    other_rows = swap(grad_rows, count)
    weights = gather_half(out_weight, count)
    early, late = weights[: count // 2], weights[count // 2 :]
    names = (list(range(count // 2)), list(range(count // 2, count)))

    sent = pack(place, [queries[0, 0], key_states[0, 0], value_states[0, 0]], frames)
    blocks = exchange(sent, 1)
    context = exchange(forward(place, row, head_scale, frame_pattern, blocks), -1)
    mine, other = [], []
    for part_weights in (early, late):
        own, theirs = context_grads(grad_rows, other_rows, part_weights)
        mine.append(own)
        other.append(swap(theirs, count))
    sent = join(place, row, mine, other, names, size, frames, full)
    grads = exchange(sent, 1)

    keep, send = part(place, row, context, count, size)
    own, theirs = project_pair(keep, swap(send, count), weights)
    attended = (own + swap(theirs, count)).astype(BF16)

    sent, scale_part = backward(place, row, head_scale, frame_pattern, blocks, grads)
    blocks = exchange(sent, -1)
    bit = group // 2
    while bit:
        scale_part = scale_part + swap(scale_part, bit)
        bit //= 2
    scale_sum = functools.reduce(jnp.add, exchange([scale_part] * frames, 1))
    query_grad, key_grad, value_grad = unpack(place, blocks, frames)
    shape = (1, 1, tokens, full)
    return (
        attended.reshape(1, 1, tokens, model),
        query_grad.reshape(shape),
        key_grad.reshape(shape),
        value_grad.reshape(shape),
        scale_sum[0, :heads],
    )


def local(*args):
    frames = lax.axis_size("frame")
    size = args[4].shape[0]
    if lax.axis_size("dp") == 2 * frames and size % HDH == 0:
        return local_split(*args)
    return local_plain(*args)


def solution(mesh):
    spec = P("dp", "frame", None, None)
    return jax.shard_map(
        local,
        mesh=mesh,
        in_specs=(spec, spec, spec, P(), P("dp", None), P(), spec),
        out_specs=(spec, spec, spec, spec, P()),
        check_vma=False,
    )
```

```python
import functools
import math

import jax
import jax.numpy as jnp
from jax import lax
from jax.experimental import pallas as pl
from jax.experimental.pallas import tpu as pltpu
from jax.sharding import PartitionSpec as P


HDH = 128
LANES = 128
LOG2E = 1.0 / math.log(2.0)


GRANT = 16 * 1024 * 1024
F32 = jnp.float32
BF16 = jnp.bfloat16
NT = (((1,), (1,)), ((), ()))
NN = (((1,), (0,)), ((), ()))
TN = (((0,), (0,)), ((), ()))
SMEM = pl.BlockSpec(memory_space=pltpu.SMEM)
VMEM = pl.BlockSpec(memory_space=pltpu.VMEM)


def dot(a, b, dims):
    return lax.dot_general(a, b, dims, preferred_element_type=F32)


def lane_block(index, width):
    return pl.ds(pl.multiple_of(index * width, LANES), width)


def call(body, outs, operands, smem=0, scratch=(), grant=GRANT):
    return pl.pallas_call(
        body,
        out_shape=outs,
        in_specs=[SMEM] * smem + [VMEM] * (len(operands) - smem),
        out_specs=[VMEM] * len(outs),
        scratch_shapes=list(scratch),
        compiler_params=pltpu.CompilerParams(vmem_limit_bytes=grant),
    )(*operands)


def pack_body(frames, width, count, *refs):
    place = refs[0][0]
    sources = refs[1 : 1 + count]
    outs = refs[1 + count :]
    for s in range(frames):
        target = lax.rem(place + s, frames)
        for i in range(count):
            outs[s][i] = sources[i][:, lane_block(target, width)]


def pack(place, sources, frames):
    tokens, full = sources[0].shape
    width = full // frames
    shape = jax.ShapeDtypeStruct((len(sources), tokens, width), BF16)
    return call(
        functools.partial(pack_body, frames, width, len(sources)),
        [shape] * frames,
        [place, *sources],
        smem=1,
    )


def unpack_body(frames, width, count, *refs):
    place = refs[0][0]
    blocks = refs[1 : 1 + frames]
    outs = refs[1 + frames :]
    for s in range(frames):
        source = lax.rem(place + s, frames)
        for i in range(count):
            outs[i][:, lane_block(source, width)] = blocks[s][i]


def unpack(place, blocks, frames):
    count, tokens, width = blocks[0].shape
    shape = jax.ShapeDtypeStruct((tokens, width * frames), BF16)
    return call(
        functools.partial(unpack_body, frames, width, count),
        [shape] * count,
        [place, *blocks],
        smem=1,
    )


def piece_of(target, late, row, frames):
    quarter = frames // 2
    inner = lax.rem(row, frames)
    far = jnp.bitwise_xor(lax.div(inner, quarter), late)
    return lax.div(target, quarter) * frames + far * quarter + lax.rem(target, quarter)


def both(parts):
    return jnp.concatenate(parts, axis=0)


def softmax_rows(query, keys, factor):
    plain = dot(keys, query, NT)
    top = jnp.max(plain, axis=0, keepdims=True)
    raised = jnp.exp2((plain - top) * (factor * LOG2E))
    total = jnp.sum(raised, axis=0, keepdims=True)
    return plain, raised * (1.0 / total)


def head_numbers(place, row, heads, split, frames):
    if not split:
        return [place * heads + h for h in range(heads)]
    each = heads // 2
    pieces = [piece_of(place, late, row, frames) for late in range(2)]
    return [pieces[h // each] * each + h % each for h in range(heads)]


def factors_of(place, row, scale_ref, heads, split, frames):
    inv_root = 1.0 / math.sqrt(HDH)
    return [scale_ref[n] * inv_root for n in head_numbers(place, row, heads, split, frames)]


def forward_body(frames, heads, slots, split, *refs):
    place_ref, row_ref, scale_ref, pattern_ref = refs[:4]
    blocks = refs[4 : 4 + frames]
    outs = refs[4 + frames : 4 + 2 * frames]
    held = refs[-1]
    place = place_ref[0]
    factors = factors_of(place, row_ref[0], scale_ref, heads, split, frames)
    for s in range(frames):
        frame = lax.rem(place + frames - s, frames)
        held[frame] = blocks[s][1:3]
    for s in range(frames):
        frame = lax.rem(place + frames - s, frames)
        chosen = [pattern_ref[frame, j] for j in range(slots)]
        for h in range(heads):
            at = slice(h * HDH, (h + 1) * HDH)
            keys = both([held[g, 0, :, at] for g in chosen])
            values = both([held[g, 1, :, at] for g in chosen])
            _, probs = softmax_rows(blocks[s][0, :, at], keys, factors[h])
            outs[s][0, :, at] = dot(probs.astype(BF16), values, TN).astype(BF16)


def forward(place, row, scale, pattern, blocks, split=False):
    frames = len(blocks)
    _, tokens, width = blocks[0].shape
    shape = jax.ShapeDtypeStruct((1, tokens, width), BF16)
    return call(
        functools.partial(forward_body, frames, width // HDH, pattern.shape[1], split),
        [shape] * frames,
        [place, row, scale, pattern, *blocks],
        smem=4,
        scratch=[pltpu.VMEM((frames, 2, tokens, width), BF16)],
    )


def backward_body(frames, heads, slots, half, before, *refs):
    place_ref, row_ref, scale_ref, pattern_ref = refs[:4]
    earlier = refs[4 : 4 + before]
    refs = refs[4 + before :]
    blocks = refs[:frames]
    grads = refs[frames : 2 * frames]
    outs = refs[2 * frames : 3 * frames]
    scale_out = refs[3 * frames]
    held, key_sum, value_sum = refs[3 * frames + 1 :]
    place = place_ref[0]
    tokens = tokens_of(blocks)
    inv_root = 1.0 / math.sqrt(HDH)
    if half is None:
        base = 0
        numbers = head_numbers(place, row_ref[0], heads, False, frames)
    else:
        base = half * heads * HDH
        numbers = head_numbers(place, row_ref[0], 2 * heads, True, frames)
        numbers = numbers[half * heads : (half + 1) * heads]
    factors = [scale_ref[n] * inv_root for n in numbers]
    part = slice(base, base + heads * HDH)
    key_sum[...] = jnp.zeros_like(key_sum)
    value_sum[...] = jnp.zeros_like(value_sum)
    for s in range(frames):
        frame = lax.rem(place + frames - s, frames)
        held[frame] = blocks[s][1:3, :, part]
    terms = [jnp.zeros((1, tokens), F32) for _ in range(heads)]
    for s in range(frames):
        frame = lax.rem(place + frames - s, frames)
        chosen = [pattern_ref[frame, j] for j in range(slots)]
        for h in range(heads):
            at = slice(h * HDH, (h + 1) * HDH)
            query = blocks[s][0, :, base + h * HDH : base + (h + 1) * HDH]
            grad = grads[s][0, :, at]
            keys = both([held[g, 0, :, at] for g in chosen])
            values = both([held[g, 1, :, at] for g in chosen])
            plain, probs = softmax_rows(query, keys, factors[h])
            prob_grads = dot(values, grad, NT)
            weighted = jnp.sum(prob_grads * probs, axis=0, keepdims=True)
            score_grads = probs * (prob_grads - weighted)
            terms[h] = terms[h] + jnp.sum(score_grads * plain, axis=0, keepdims=True)
            low = score_grads.astype(BF16)
            outs[s][0, :, at] = (dot(low, keys, TN) * factors[h]).astype(BF16)
            key_part = dot(low, query, NN)
            value_part = dot(probs.astype(BF16), grad, NN)
            for j, g in enumerate(chosen):
                rows = slice(j * tokens, (j + 1) * tokens)
                key_sum[g, :, at] += key_part[rows]
                value_sum[g, :, at] += value_part[rows]
    for s in range(frames):
        frame = lax.rem(place + frames - s, frames)
        for h in range(heads):
            at = slice(h * HDH, (h + 1) * HDH)
            outs[s][1, :, at] = (key_sum[frame, :, at] * factors[h]).astype(BF16)
        outs[s][2] = value_sum[frame].astype(BF16)
    lanes = lax.broadcasted_iota(jnp.int32, scale_out.shape, 1)
    result = earlier[0][...] if before else jnp.zeros(scale_out.shape, F32)
    for h in range(heads):
        term = jnp.sum(terms[h], axis=1, keepdims=True) * inv_root
        result = result + jnp.where(lanes == numbers[h], term, 0.0)
    scale_out[...] = result


def tokens_of(blocks):
    return blocks[0].shape[1]


def backward(place, row, scale, pattern, blocks, grads, half=None, before=()):
    frames = len(blocks)
    _, tokens, width = grads[0].shape
    shape = jax.ShapeDtypeStruct((3, tokens, width), BF16)
    result = call(
        functools.partial(
            backward_body, frames, width // HDH, pattern.shape[1], half, len(before)
        ),
        [shape] * frames + [jax.ShapeDtypeStruct((1, LANES), F32)],
        [place, row, scale, pattern, *before, *blocks, *grads],
        smem=4,
        scratch=[
            pltpu.VMEM((frames, 2, tokens, width), BF16),
            pltpu.VMEM((frames, tokens, width), F32),
            pltpu.VMEM((frames, tokens, width), F32),
        ],
    )
    return result[:frames], result[frames]


def context_grad_body(skip, count, cuts, *refs):
    refs = refs[skip:]
    mine, other = refs[:2]
    weights = refs[2 : 2 + count]
    mine_out, other_out = refs[2 + count : 4 + count]
    tokens = mine.shape[0]
    rows = both([other[...], mine[...]])
    start = 0
    for w in weights:
        at = slice(start, start + w.shape[0])
        result = dot(rows, w[...], NT).astype(BF16)
        other_out[:, at] = result[:tokens]
        mine_out[:, at] = result[tokens:]
        start += w.shape[0]
    start = 0
    for chunk, size in zip(refs[4 + count :], cuts):
        chunk[...] = weights[0][start : start + size]
        start += size


def context_grads(mine, other, weights, scalars=(), cuts=()):
    tokens = mine.shape[0]
    features = sum(w.shape[0] for w in weights)
    shapes = [jax.ShapeDtypeStruct((tokens, features), BF16)] * 2
    shapes += [jax.ShapeDtypeStruct((n, weights[0].shape[1]), BF16) for n in cuts]
    return call(
        functools.partial(context_grad_body, len(scalars), len(weights), cuts),
        shapes,
        [*scalars, mine, other, *weights],
        smem=len(scalars),
    )


def project_body(count, columns, *refs):
    mine, other = refs[:2]
    weights = refs[2 : 2 + count]
    mine_out, other_out = refs[2 + count :]
    tokens = mine.shape[0]
    rows = both([other[...], mine[...]])
    start = 0
    total = None
    for w in weights:
        part = dot(rows[:, start : start + w.shape[0]], w[:, columns], NN)
        total = part if total is None else total + part
        start += w.shape[0]
    other_out[...] = total[:tokens].astype(other_out.dtype)
    mine_out[...] = total[tokens:]


def project_pair(mine, other, weights, first=0, last=None):
    tokens, _ = mine.shape
    columns = slice(first, weights[0].shape[1] if last is None else last)
    width = columns.stop - columns.start
    return call(
        functools.partial(project_body, len(weights), columns),
        [jax.ShapeDtypeStruct((tokens, width), kind) for kind in (F32, BF16)],
        [mine, other, *weights],
    )


def place_in_half(row, group):
    half = lax.div(row, group)
    return half, row - half * group


def join_body(frames, pieces, size, *refs):
    place = refs[0][0]
    half, inner = place_in_half(refs[1][0], sum(len(p) for p in pieces))
    count = len(pieces)
    mine = refs[2 : 2 + count]
    other = refs[2 + count : 2 + 2 * count]
    outs = refs[2 + 2 * count : 2 + 2 * count + frames]
    whole = refs[-1]
    group = sum(len(p) for p in pieces)
    width = whole.shape[1] // frames
    for h, sources in ((half, mine), (1 - half, other)):
        for source, names in zip(sources, pieces):
            for k, j in enumerate(names):
                spot = h * group + jnp.bitwise_xor(inner, j)
                whole[:, lane_block(spot, size)] = source[:, k * size : (k + 1) * size]
    for s in range(frames):
        outs[s][0] = whole[:, lane_block(lax.rem(place + s, frames), width)]


def join(place, row, mine, other, pieces, size, frames, full):
    tokens = mine[0].shape[0]
    if size % LANES == 0:
        shape = jax.ShapeDtypeStruct((1, tokens, full // frames), BF16)
        return call(
            functools.partial(join_body, frames, pieces, size),
            [shape] * frames,
            [place, row, *mine, *other],
            smem=2,
            scratch=[pltpu.VMEM((tokens, full), BF16)],
        )
    group = sum(len(p) for p in pieces)
    whole = jnp.zeros((tokens, full), BF16)
    half, inner = place_in_half(row[0], group)
    for h, sources in ((half, mine), (1 - half, other)):
        for source, names in zip(sources, pieces):
            for k, j in enumerate(names):
                spot = h * group + jnp.bitwise_xor(inner, j)
                piece = source[:, k * size : (k + 1) * size]
                whole = lax.dynamic_update_slice(whole, piece, (0, spot * size))
    return pack(place, [whole], frames)


def part_body(frames, count, size, *refs):
    place = refs[0][0]
    half, inner = place_in_half(refs[1][0], count)
    blocks = refs[2 : 2 + frames]
    keep, send, whole = refs[2 + frames :]
    width = whole.shape[1] // frames
    for s in range(frames):
        whole[:, lane_block(lax.rem(place + s, frames), width)] = blocks[s][0]
    for j in range(count):
        spot = jnp.bitwise_xor(inner, j)
        at = slice(j * size, (j + 1) * size)
        keep[:, at] = whole[:, lane_block(half * count + spot, size)]
        send[:, at] = whole[:, lane_block((1 - half) * count + spot, size)]


def part(place, row, blocks, count, size):
    frames = len(blocks)
    _, tokens, width = blocks[0].shape
    if size % LANES == 0:
        shape = jax.ShapeDtypeStruct((tokens, count * size), BF16)
        return call(
            functools.partial(part_body, frames, count, size),
            [shape, shape],
            [place, row, *blocks],
            smem=2,
            scratch=[pltpu.VMEM((tokens, width * frames), BF16)],
        )
    whole = unpack(place, blocks, frames)[0]
    half, inner = place_in_half(row[0], count)

    def half_of(h):
        spots = [h * count + jnp.bitwise_xor(inner, j) for j in range(count)]
        return jnp.concatenate(
            [lax.dynamic_slice_in_dim(whole, spot * size, size, axis=1) for spot in spots], axis=1
        )

    return half_of(half), half_of(1 - half)


def split_pack_body(frames, count, *refs):
    place, row = refs[0][0], refs[1][0]
    sources = refs[2 : 2 + count]
    outs = refs[2 + count :]
    size = outs[0].shape[2] // 2
    for s in range(frames):
        target = lax.rem(place + s, frames)
        for late in range(2):
            piece = piece_of(target, late, row, frames)
            for i in range(count):
                at = slice(late * size, (late + 1) * size)
                outs[s][i, :, at] = sources[i][:, lane_block(piece, size)]


def split_pack(place, row, sources, frames):
    tokens, full = sources[0].shape
    shape = jax.ShapeDtypeStruct((len(sources), tokens, full // frames), BF16)
    return call(
        functools.partial(split_pack_body, frames, len(sources)),
        [shape] * frames,
        [place, row, *sources],
        smem=2,
        grant=60 * 1024 * 1024,
    )


def split_unpack_body(frames, count, *refs):
    place, row = refs[0][0], refs[1][0]
    blocks = (refs[2 : 2 + frames], refs[2 + frames : 2 + 2 * frames])
    scales = refs[2 + 2 * frames : 2 + 3 * frames]
    outs = refs[2 + 3 * frames : -1]
    size = blocks[0][0].shape[2]
    for late in range(2):
        for s in range(frames):
            piece = piece_of(lax.rem(place + s, frames), late, row, frames)
            for i in range(count):
                outs[i][:, lane_block(piece, size)] = blocks[late][s][i]
    total = functools.reduce(jnp.add, [s[...] for s in scales])
    refs[-1][...] = total[:, : refs[-1].shape[1]]


def split_unpack(place, row, early, late, scales, heads):
    frames = len(early)
    count, tokens, size = early[0].shape
    shape = jax.ShapeDtypeStruct((tokens, 2 * size * frames), BF16)
    return call(
        functools.partial(split_unpack_body, frames, count),
        [shape] * count + [jax.ShapeDtypeStruct((1, heads), F32)],
        [place, row, *early, *late, *scales],
        smem=2,
    )


def split_join_body(frames, count, *refs):
    place, row = refs[0][0], refs[1][0]
    mine = refs[2 : 2 + count]
    other = refs[2 + count : 2 + 2 * count]
    outs = refs[2 + 2 * count : 2 + 2 * count + frames]
    own, theirs = refs[2 + 2 * count + frames :]
    quarter = frames // 2
    size = own.shape[1] // quarter
    half, inner = place_in_half(row, frames)
    for sources, whole in ((mine, own), (other, theirs)):
        start = 0
        for source in sources:
            whole[:, start : start + source.shape[1]] = source[...]
            start += source.shape[1]
    for s in range(frames):
        target = lax.rem(place + s, frames)
        near = jnp.bitwise_xor(lax.rem(target, quarter), lax.rem(inner, quarter))
        at = lane_block(near, size)
        outs[s][0] = jnp.where(lax.div(target, quarter) == half, own[:, at], theirs[:, at])


def split_join(place, row, mine, other, frames):
    tokens = mine[0].shape[0]
    width = sum(m.shape[1] for m in mine)
    shape = jax.ShapeDtypeStruct((1, tokens, 2 * width // frames), BF16)
    return call(
        functools.partial(split_join_body, frames, len(mine)),
        [shape] * frames,
        [place, row, *mine, *other],
        smem=2,
        scratch=[pltpu.VMEM((tokens, width), BF16)] * 2,
    )


def split_part_body(frames, *refs):
    place, row = refs[0][0], refs[1][0]
    blocks = refs[2 : 2 + frames]
    keep, send, whole = refs[2 + frames :]
    size = keep.shape[1] // frames
    half, inner = place_in_half(row, frames)
    for s in range(frames):
        for late in range(2):
            piece = piece_of(lax.rem(place + s, frames), late, row, frames)
            whole[:, lane_block(piece, size)] = blocks[s][0, :, late * size : (late + 1) * size]
    for j in range(frames):
        spot = jnp.bitwise_xor(inner, j)
        at = slice(j * size, (j + 1) * size)
        keep[:, at] = whole[:, lane_block(half * frames + spot, size)]
        send[:, at] = whole[:, lane_block((1 - half) * frames + spot, size)]


def split_part(place, row, blocks):
    frames = len(blocks)
    _, tokens, width = blocks[0].shape
    shape = jax.ShapeDtypeStruct((tokens, frames * width // 2), BF16)
    return call(
        functools.partial(split_part_body, frames),
        [shape, shape],
        [place, row, *blocks],
        smem=2,
        scratch=[pltpu.VMEM((tokens, width * frames), BF16)],
    )


def exchange(blocks, sign):
    frames = len(blocks)
    result = [blocks[0]]
    for s in range(1, frames):
        pairs = [(i, (i + sign * s) % frames) for i in range(frames)]
        result.append(lax.ppermute(blocks[s], "frame", pairs))
    return result


def swap(x, bit):
    group = lax.axis_size("dp")
    return lax.ppermute(x, "dp", [(i, i ^ bit) for i in range(group)])


def gather_half(out_weight, count):
    weights = {0: out_weight}
    bit = count // 2
    while bit:
        for j in list(weights):
            weights[j ^ bit] = swap(weights[j], bit)
        bit //= 2
    return [weights[j] for j in range(count)]


def attend_body(counts, *refs):
    contexts = refs[: len(counts)]
    out = refs[-1]
    width = out.shape[1]
    tile = math.gcd(width, 768)
    for first in range(0, width, tile):
        columns = slice(first, first + tile)
        weights = list(refs[len(counts) : -1])
        total = None
        for context, pieces in zip(contexts, counts):
            start = 0
            for chunks in pieces:
                piece = both([weights.pop(0)[:, columns] for _ in range(chunks)])
                part = dot(context[:, start : start + piece.shape[0]], piece, NN)
                total = part if total is None else total + part
                start += piece.shape[0]
        out[:, columns] = total.astype(BF16)


def attend(contexts, weights):
    tokens, _ = contexts[0].shape
    flat = [c for pieces in weights for chunks in pieces for c in chunks]
    counts = [[len(chunks) for chunks in pieces] for pieces in weights]
    return call(
        functools.partial(attend_body, counts),
        [jax.ShapeDtypeStruct((tokens, flat[0].shape[1]), BF16)],
        [*contexts, *flat],
    )[0]


def local_split(queries, key_states, value_states, head_scale, out_weight, frame_pattern, out_grad):
    frames = lax.axis_size("frame")
    group = lax.axis_size("dp")
    tokens, full = queries.shape[2:]
    model = out_grad.shape[3]
    heads = full // HDH
    place = lax.axis_index("frame").astype(jnp.int32).reshape(1)
    row = lax.axis_index("dp").astype(jnp.int32).reshape(1)

    grad_rows = out_grad[0, 0]
    other_rows = swap(grad_rows, frames)
    weights = gather_half(out_weight, frames)
    early, late = weights[: frames // 2], weights[frames // 2 :]
    cuts = [out_weight.shape[0] * n // 16 for n in (8, 4, 4)]

    sent = split_pack(place, row, [queries[0, 0], key_states[0, 0], value_states[0, 0]], frames)
    blocks = exchange(sent, 1)

    mine, theirs, *chunks = context_grads(
        grad_rows, other_rows, early, [frame_pattern], cuts
    )
    other = swap(theirs, frames)
    crossed, far = [], []
    for i, chunk in enumerate(chunks):
        crossed.append(swap(chunk, frames))
        far.append(swap(crossed[i], frames // 2))
    sent = split_join(place, row, [mine], [other], frames)
    grads_early = exchange(sent, 1)
    mine, other = [], []
    for weight in late:
        own, theirs = context_grads(grad_rows, other_rows, [weight])
        mine.append(own)
        other.append(swap(theirs, frames))
    context = forward(place, row, head_scale, frame_pattern, blocks, True)
    context = exchange(context, -1)
    sent = split_join(place, row, mine, other, frames)
    grads_late = exchange(sent, 1)

    sent, scale_early = backward(
        place, row, head_scale, frame_pattern, blocks, grads_early, 0
    )
    done_early = exchange(sent, -1)
    sent, scale_part = backward(
        place, row, head_scale, frame_pattern, blocks, grads_late, 1, [scale_early]
    )
    done_late = exchange(sent, -1)

    contexts = split_part(place, row, context)
    others = {0: crossed, frames // 2: far}
    bit = frames // 4
    while bit:
        for j in list(others):
            others[j ^ bit] = [swap(c, bit) for c in others[j]]
        bit //= 2
    others = [others[j] for j in range(frames)]
    attended = attend(contexts, [[[w] for w in weights], others])

    bit = group // 2
    while bit:
        scale_part = scale_part + swap(scale_part, bit)
        bit //= 2
    scales = exchange([scale_part] * frames, 1)

    query_grad, key_grad, value_grad, scale_sum = split_unpack(
        place, row, done_early, done_late, scales, heads
    )
    shape = (1, 1, tokens, full)
    return (
        attended.reshape(1, 1, tokens, model),
        query_grad.reshape(shape),
        key_grad.reshape(shape),
        value_grad.reshape(shape),
        scale_sum[0, :heads],
    )


def local_plain(queries, key_states, value_states, head_scale, out_weight, frame_pattern, out_grad):
    frames = lax.axis_size("frame")
    group = lax.axis_size("dp")
    tokens, full = queries.shape[2:]
    model = out_grad.shape[3]
    heads = full // HDH
    count = group // 2
    size = out_weight.shape[0]
    place = lax.axis_index("frame").astype(jnp.int32).reshape(1)
    row = lax.axis_index("dp").astype(jnp.int32).reshape(1)

    grad_rows = out_grad[0, 0]
    other_rows = swap(grad_rows, count)
    weights = gather_half(out_weight, count)
    early, late = weights[: count // 2], weights[count // 2 :]
    names = (list(range(count // 2)), list(range(count // 2, count)))

    sent = pack(place, [queries[0, 0], key_states[0, 0], value_states[0, 0]], frames)
    blocks = exchange(sent, 1)
    context = exchange(forward(place, row, head_scale, frame_pattern, blocks), -1)
    mine, other = [], []
    for part_weights in (early, late):
        own, theirs = context_grads(grad_rows, other_rows, part_weights)
        mine.append(own)
        other.append(swap(theirs, count))
    sent = join(place, row, mine, other, names, size, frames, full)
    grads = exchange(sent, 1)

    keep, send = part(place, row, context, count, size)
    own, theirs = project_pair(keep, swap(send, count), weights)
    attended = (own + swap(theirs, count)).astype(BF16)

    sent, scale_part = backward(place, row, head_scale, frame_pattern, blocks, grads)
    blocks = exchange(sent, -1)
    bit = group // 2
    while bit:
        scale_part = scale_part + swap(scale_part, bit)
        bit //= 2
    scale_sum = functools.reduce(jnp.add, exchange([scale_part] * frames, 1))
    query_grad, key_grad, value_grad = unpack(place, blocks, frames)
    shape = (1, 1, tokens, full)
    return (
        attended.reshape(1, 1, tokens, model),
        query_grad.reshape(shape),
        key_grad.reshape(shape),
        value_grad.reshape(shape),
        scale_sum[0, :heads],
    )


def local(*args):
    frames = lax.axis_size("frame")
    size = args[4].shape[0]
    if lax.axis_size("dp") == 2 * frames and size % HDH == 0:
        return local_split(*args)
    return local_plain(*args)


def solution(mesh):
    spec = P("dp", "frame", None, None)
    return jax.shard_map(
        local,
        mesh=mesh,
        in_specs=(spec, spec, spec, P(), P("dp", None), P(), spec),
        out_specs=(spec, spec, spec, spec, P()),
        check_vma=False,
    )
```

```python
import functools
import math

import jax
import jax.numpy as jnp
from jax import lax
from jax.experimental import pallas as pl
from jax.experimental.pallas import tpu as pltpu
from jax.sharding import PartitionSpec as P


HDH = 128
LANES = 128
LOG2E = 1.0 / math.log(2.0)


GRANT = 16 * 1024 * 1024
FULL_GRANT = 60 * 1024 * 1024
F32 = jnp.float32
BF16 = jnp.bfloat16
NT = (((1,), (1,)), ((), ()))
NN = (((1,), (0,)), ((), ()))
TN = (((0,), (0,)), ((), ()))
SMEM = pl.BlockSpec(memory_space=pltpu.SMEM)
VMEM = pl.BlockSpec(memory_space=pltpu.VMEM)


def dot(a, b, dims):
    return lax.dot_general(a, b, dims, preferred_element_type=F32)


def lane_block(index, width):
    return pl.ds(pl.multiple_of(index * width, LANES), width)


def call(body, outs, operands, smem=0, scratch=(), grant=GRANT):
    return pl.pallas_call(
        body,
        out_shape=outs,
        in_specs=[SMEM] * smem + [VMEM] * (len(operands) - smem),
        out_specs=[VMEM] * len(outs),
        scratch_shapes=list(scratch),
        compiler_params=pltpu.CompilerParams(vmem_limit_bytes=grant),
    )(*operands)


def pack_body(frames, width, count, *refs):
    place = refs[0][0]
    sources = refs[1 : 1 + count]
    outs = refs[1 + count :]
    for s in range(frames):
        target = lax.rem(place + s, frames)
        for i in range(count):
            outs[s][i] = sources[i][:, lane_block(target, width)]


def pack(place, sources, frames):
    tokens, full = sources[0].shape
    width = full // frames
    shape = jax.ShapeDtypeStruct((len(sources), tokens, width), BF16)
    return call(
        functools.partial(pack_body, frames, width, len(sources)),
        [shape] * frames,
        [place, *sources],
        smem=1,
    )


def unpack_body(frames, width, count, *refs):
    place = refs[0][0]
    blocks = refs[1 : 1 + frames]
    outs = refs[1 + frames :]
    for s in range(frames):
        source = lax.rem(place + s, frames)
        for i in range(count):
            outs[i][:, lane_block(source, width)] = blocks[s][i]


def unpack(place, blocks, frames):
    count, tokens, width = blocks[0].shape
    shape = jax.ShapeDtypeStruct((tokens, width * frames), BF16)
    return call(
        functools.partial(unpack_body, frames, width, count),
        [shape] * count,
        [place, *blocks],
        smem=1,
    )


def piece_of(target, late, row, frames):
    quarter = frames // 2
    inner = lax.rem(row, frames)
    far = jnp.bitwise_xor(lax.div(inner, quarter), late)
    return lax.div(target, quarter) * frames + far * quarter + lax.rem(target, quarter)


def both(parts):
    return jnp.concatenate(parts, axis=0)


def softmax_rows(query, keys, factor):
    plain = dot(keys, query, NT)
    top = jnp.max(plain, axis=0, keepdims=True)
    raised = jnp.exp2((plain - top) * (factor * LOG2E))
    total = jnp.sum(raised, axis=0, keepdims=True)
    return plain, raised * (1.0 / total)


def head_numbers(place, row, heads, split, frames):
    if not split:
        return [place * heads + h for h in range(heads)]
    each = heads // 2
    pieces = [piece_of(place, late, row, frames) for late in range(2)]
    return [pieces[h // each] * each + h % each for h in range(heads)]


def factors_of(place, row, scale_ref, heads, split, frames):
    inv_root = 1.0 / math.sqrt(HDH)
    return [scale_ref[n] * inv_root for n in head_numbers(place, row, heads, split, frames)]


def forward_body(frames, heads, slots, split, *refs):
    place_ref, row_ref, scale_ref, pattern_ref = refs[:4]
    blocks = refs[4 : 4 + frames]
    outs = refs[4 + frames : 4 + 2 * frames]
    held = refs[-1]
    place = place_ref[0]
    factors = factors_of(place, row_ref[0], scale_ref, heads, split, frames)
    for s in range(frames):
        frame = lax.rem(place + frames - s, frames)
        held[frame] = blocks[s][1:3]
    for s in range(frames):
        frame = lax.rem(place + frames - s, frames)
        chosen = [pattern_ref[frame, j] for j in range(slots)]
        for h in range(heads):
            at = slice(h * HDH, (h + 1) * HDH)
            keys = both([held[g, 0, :, at] for g in chosen])
            values = both([held[g, 1, :, at] for g in chosen])
            _, probs = softmax_rows(blocks[s][0, :, at], keys, factors[h])
            outs[s][0, :, at] = dot(probs.astype(BF16), values, TN).astype(BF16)


def forward(place, row, scale, pattern, blocks, split=False):
    frames = len(blocks)
    _, tokens, width = blocks[0].shape
    shape = jax.ShapeDtypeStruct((1, tokens, width), BF16)
    return call(
        functools.partial(forward_body, frames, width // HDH, pattern.shape[1], split),
        [shape] * frames,
        [place, row, scale, pattern, *blocks],
        smem=4,
        scratch=[pltpu.VMEM((frames, 2, tokens, width), BF16)],
    )


def backward_body(frames, heads, slots, half, before, *refs):
    place_ref, row_ref, scale_ref, pattern_ref = refs[:4]
    earlier = refs[4 : 4 + before]
    refs = refs[4 + before :]
    blocks = refs[:frames]
    grads = refs[frames : 2 * frames]
    outs = refs[2 * frames : 3 * frames]
    scale_out = refs[3 * frames]
    held, key_sum, value_sum = refs[3 * frames + 1 :]
    place = place_ref[0]
    tokens = tokens_of(blocks)
    inv_root = 1.0 / math.sqrt(HDH)
    if half is None:
        base = 0
        numbers = head_numbers(place, row_ref[0], heads, False, frames)
    else:
        base = half * heads * HDH
        numbers = head_numbers(place, row_ref[0], 2 * heads, True, frames)
        numbers = numbers[half * heads : (half + 1) * heads]
    factors = [scale_ref[n] * inv_root for n in numbers]
    part = slice(base, base + heads * HDH)
    key_sum[...] = jnp.zeros_like(key_sum)
    value_sum[...] = jnp.zeros_like(value_sum)
    for s in range(frames):
        frame = lax.rem(place + frames - s, frames)
        held[frame] = blocks[s][1:3, :, part]
    terms = [jnp.zeros((1, tokens), F32) for _ in range(heads)]
    for s in range(frames):
        frame = lax.rem(place + frames - s, frames)
        chosen = [pattern_ref[frame, j] for j in range(slots)]
        for h in range(heads):
            at = slice(h * HDH, (h + 1) * HDH)
            query = blocks[s][0, :, base + h * HDH : base + (h + 1) * HDH]
            grad = grads[s][0, :, at]
            keys = both([held[g, 0, :, at] for g in chosen])
            values = both([held[g, 1, :, at] for g in chosen])
            plain, probs = softmax_rows(query, keys, factors[h])
            prob_grads = dot(values, grad, NT)
            weighted = jnp.sum(prob_grads * probs, axis=0, keepdims=True)
            score_grads = probs * (prob_grads - weighted)
            terms[h] = terms[h] + jnp.sum(score_grads * plain, axis=0, keepdims=True)
            low = score_grads.astype(BF16)
            outs[s][0, :, at] = (dot(low, keys, TN) * factors[h]).astype(BF16)
            key_part = dot(low, query, NN)
            value_part = dot(probs.astype(BF16), grad, NN)
            for j, g in enumerate(chosen):
                rows = slice(j * tokens, (j + 1) * tokens)
                key_sum[g, :, at] += key_part[rows]
                value_sum[g, :, at] += value_part[rows]
    for s in range(frames):
        frame = lax.rem(place + frames - s, frames)
        for h in range(heads):
            at = slice(h * HDH, (h + 1) * HDH)
            outs[s][1, :, at] = (key_sum[frame, :, at] * factors[h]).astype(BF16)
        outs[s][2] = value_sum[frame].astype(BF16)
    lanes = lax.broadcasted_iota(jnp.int32, scale_out.shape, 1)
    result = earlier[0][...] if before else jnp.zeros(scale_out.shape, F32)
    for h in range(heads):
        term = jnp.sum(terms[h], axis=1, keepdims=True) * inv_root
        result = result + jnp.where(lanes == numbers[h], term, 0.0)
    scale_out[...] = result


def tokens_of(blocks):
    return blocks[0].shape[1]


def backward(place, row, scale, pattern, blocks, grads, half=None, before=()):
    frames = len(blocks)
    _, tokens, width = grads[0].shape
    shape = jax.ShapeDtypeStruct((3, tokens, width), BF16)
    result = call(
        functools.partial(
            backward_body, frames, width // HDH, pattern.shape[1], half, len(before)
        ),
        [shape] * frames + [jax.ShapeDtypeStruct((1, LANES), F32)],
        [place, row, scale, pattern, *before, *blocks, *grads],
        smem=4,
        scratch=[
            pltpu.VMEM((frames, 2, tokens, width), BF16),
            pltpu.VMEM((frames, tokens, width), F32),
            pltpu.VMEM((frames, tokens, width), F32),
        ],
    )
    return result[:frames], result[frames]


def context_grad_body(skip, count, cuts, *refs):
    refs = refs[skip:]
    mine, other = refs[:2]
    weights = refs[2 : 2 + count]
    mine_out, other_out = refs[2 + count : 4 + count]
    tokens = mine.shape[0]
    rows = both([other[...], mine[...]])
    start = 0
    for w in weights:
        at = slice(start, start + w.shape[0])
        result = dot(rows, w[...], NT).astype(BF16)
        other_out[:, at] = result[:tokens]
        mine_out[:, at] = result[tokens:]
        start += w.shape[0]
    start = 0
    for chunk, size in zip(refs[4 + count :], cuts):
        chunk[...] = weights[0][start : start + size]
        start += size


def context_grads(mine, other, weights, scalars=(), cuts=()):
    tokens = mine.shape[0]
    features = sum(w.shape[0] for w in weights)
    shapes = [jax.ShapeDtypeStruct((tokens, features), BF16)] * 2
    shapes += [jax.ShapeDtypeStruct((n, weights[0].shape[1]), BF16) for n in cuts]
    return call(
        functools.partial(context_grad_body, len(scalars), len(weights), cuts),
        shapes,
        [*scalars, mine, other, *weights],
        smem=len(scalars),
    )


def project_body(count, columns, *refs):
    mine, other = refs[:2]
    weights = refs[2 : 2 + count]
    mine_out, other_out = refs[2 + count :]
    tokens = mine.shape[0]
    rows = both([other[...], mine[...]])
    start = 0
    total = None
    for w in weights:
        part = dot(rows[:, start : start + w.shape[0]], w[:, columns], NN)
        total = part if total is None else total + part
        start += w.shape[0]
    other_out[...] = total[:tokens].astype(other_out.dtype)
    mine_out[...] = total[tokens:]


def project_pair(mine, other, weights, first=0, last=None):
    tokens, _ = mine.shape
    columns = slice(first, weights[0].shape[1] if last is None else last)
    width = columns.stop - columns.start
    return call(
        functools.partial(project_body, len(weights), columns),
        [jax.ShapeDtypeStruct((tokens, width), kind) for kind in (F32, BF16)],
        [mine, other, *weights],
    )


def place_in_half(row, group):
    half = lax.div(row, group)
    return half, row - half * group


def join_body(frames, pieces, size, *refs):
    place = refs[0][0]
    half, inner = place_in_half(refs[1][0], sum(len(p) for p in pieces))
    count = len(pieces)
    mine = refs[2 : 2 + count]
    other = refs[2 + count : 2 + 2 * count]
    outs = refs[2 + 2 * count : 2 + 2 * count + frames]
    whole = refs[-1]
    group = sum(len(p) for p in pieces)
    width = whole.shape[1] // frames
    for h, sources in ((half, mine), (1 - half, other)):
        for source, names in zip(sources, pieces):
            for k, j in enumerate(names):
                spot = h * group + jnp.bitwise_xor(inner, j)
                whole[:, lane_block(spot, size)] = source[:, k * size : (k + 1) * size]
    for s in range(frames):
        outs[s][0] = whole[:, lane_block(lax.rem(place + s, frames), width)]


def join(place, row, mine, other, pieces, size, frames, full):
    tokens = mine[0].shape[0]
    if size % LANES == 0:
        shape = jax.ShapeDtypeStruct((1, tokens, full // frames), BF16)
        return call(
            functools.partial(join_body, frames, pieces, size),
            [shape] * frames,
            [place, row, *mine, *other],
            smem=2,
            scratch=[pltpu.VMEM((tokens, full), BF16)],
        )
    group = sum(len(p) for p in pieces)
    whole = jnp.zeros((tokens, full), BF16)
    half, inner = place_in_half(row[0], group)
    for h, sources in ((half, mine), (1 - half, other)):
        for source, names in zip(sources, pieces):
            for k, j in enumerate(names):
                spot = h * group + jnp.bitwise_xor(inner, j)
                piece = source[:, k * size : (k + 1) * size]
                whole = lax.dynamic_update_slice(whole, piece, (0, spot * size))
    return pack(place, [whole], frames)


def part_body(frames, count, size, *refs):
    place = refs[0][0]
    half, inner = place_in_half(refs[1][0], count)
    blocks = refs[2 : 2 + frames]
    keep, send, whole = refs[2 + frames :]
    width = whole.shape[1] // frames
    for s in range(frames):
        whole[:, lane_block(lax.rem(place + s, frames), width)] = blocks[s][0]
    for j in range(count):
        spot = jnp.bitwise_xor(inner, j)
        at = slice(j * size, (j + 1) * size)
        keep[:, at] = whole[:, lane_block(half * count + spot, size)]
        send[:, at] = whole[:, lane_block((1 - half) * count + spot, size)]


def part(place, row, blocks, count, size):
    frames = len(blocks)
    _, tokens, width = blocks[0].shape
    if size % LANES == 0:
        shape = jax.ShapeDtypeStruct((tokens, count * size), BF16)
        return call(
            functools.partial(part_body, frames, count, size),
            [shape, shape],
            [place, row, *blocks],
            smem=2,
            scratch=[pltpu.VMEM((tokens, width * frames), BF16)],
        )
    whole = unpack(place, blocks, frames)[0]
    half, inner = place_in_half(row[0], count)

    def half_of(h):
        spots = [h * count + jnp.bitwise_xor(inner, j) for j in range(count)]
        return jnp.concatenate(
            [lax.dynamic_slice_in_dim(whole, spot * size, size, axis=1) for spot in spots], axis=1
        )

    return half_of(half), half_of(1 - half)


def split_pack_body(frames, shifts, count, *refs):
    place, row = refs[0][0], refs[1][0]
    sources = refs[2 : 2 + count]
    outs = refs[2 + count :]
    size = outs[0].shape[2] // 2
    for out, s in zip(outs, shifts):
        target = lax.rem(place + s, frames)
        for late in range(2):
            piece = piece_of(target, late, row, frames)
            for i in range(count):
                at = slice(late * size, (late + 1) * size)
                out[i, :, at] = sources[i][:, lane_block(piece, size)]


def split_pack(place, row, sources, frames, shifts):
    tokens, full = sources[0].shape
    shape = jax.ShapeDtypeStruct((len(sources), tokens, full // frames), BF16)
    return call(
        functools.partial(split_pack_body, frames, shifts, len(sources)),
        [shape] * len(shifts),
        [place, row, *sources],
        smem=2,
        grant=FULL_GRANT,
    )


def pack_one_body(count, *refs):
    out = refs[-1]
    for i in range(count):
        out[i] = refs[2 + i][...]


def pack_one(place, row, sources, frames, shift):
    tokens, full = sources[0].shape
    count = len(sources)
    size = full // frames // 2

    def columns(late, place_ref, row_ref):
        target = lax.rem(place_ref[0] + shift, frames)
        return 0, piece_of(target, late, row_ref[0], frames)

    return pl.pallas_call(
        functools.partial(pack_one_body, count),
        out_shape=jax.ShapeDtypeStruct((count, tokens, 2 * size), BF16),
        grid_spec=pltpu.PrefetchScalarGridSpec(
            num_scalar_prefetch=2,
            grid=(2,),
            in_specs=[pl.BlockSpec((tokens, size), columns)] * count,
            out_specs=pl.BlockSpec((count, tokens, size), lambda late, p, r: (0, 0, late)),
        ),
        compiler_params=pltpu.CompilerParams(vmem_limit_bytes=FULL_GRANT),
        name="pack_one",
    )(place, row, *sources)


def split_unpack_body(frames, count, *refs):
    place, row = refs[0][0], refs[1][0]
    blocks = (refs[2 : 2 + frames], refs[2 + frames : 2 + 2 * frames])
    scales = refs[2 + 2 * frames : 2 + 3 * frames]
    outs = refs[2 + 3 * frames : -1]
    size = blocks[0][0].shape[2]
    for late in range(2):
        for s in range(frames):
            piece = piece_of(lax.rem(place + s, frames), late, row, frames)
            for i in range(count):
                outs[i][:, lane_block(piece, size)] = blocks[late][s][i]
    total = functools.reduce(jnp.add, [s[...] for s in scales])
    refs[-1][...] = total[:, : refs[-1].shape[1]]


def split_unpack(place, row, early, late, scales, heads):
    frames = len(early)
    count, tokens, size = early[0].shape
    shape = jax.ShapeDtypeStruct((tokens, 2 * size * frames), BF16)
    return call(
        functools.partial(split_unpack_body, frames, count),
        [shape] * count + [jax.ShapeDtypeStruct((1, heads), F32)],
        [place, row, *early, *late, *scales],
        smem=2,
    )


def split_join_body(frames, count, *refs):
    place, row = refs[0][0], refs[1][0]
    mine = refs[2 : 2 + count]
    other = refs[2 + count : 2 + 2 * count]
    outs = refs[2 + 2 * count : 2 + 2 * count + frames]
    own, theirs = refs[2 + 2 * count + frames :]
    quarter = frames // 2
    size = own.shape[1] // quarter
    half, inner = place_in_half(row, frames)
    for sources, whole in ((mine, own), (other, theirs)):
        start = 0
        for source in sources:
            whole[:, start : start + source.shape[1]] = source[...]
            start += source.shape[1]
    for s in range(frames):
        target = lax.rem(place + s, frames)
        near = jnp.bitwise_xor(lax.rem(target, quarter), lax.rem(inner, quarter))
        at = lane_block(near, size)
        outs[s][0] = jnp.where(lax.div(target, quarter) == half, own[:, at], theirs[:, at])


def split_join(place, row, mine, other, frames):
    tokens = mine[0].shape[0]
    width = sum(m.shape[1] for m in mine)
    shape = jax.ShapeDtypeStruct((1, tokens, 2 * width // frames), BF16)
    return call(
        functools.partial(split_join_body, frames, len(mine)),
        [shape] * frames,
        [place, row, *mine, *other],
        smem=2,
        scratch=[pltpu.VMEM((tokens, width), BF16)] * 2,
    )


def split_part_body(frames, *refs):
    place, row = refs[0][0], refs[1][0]
    blocks = refs[2 : 2 + frames]
    keep, send, whole = refs[2 + frames :]
    size = keep.shape[1] // frames
    half, inner = place_in_half(row, frames)
    for s in range(frames):
        for late in range(2):
            piece = piece_of(lax.rem(place + s, frames), late, row, frames)
            whole[:, lane_block(piece, size)] = blocks[s][0, :, late * size : (late + 1) * size]
    for j in range(frames):
        spot = jnp.bitwise_xor(inner, j)
        at = slice(j * size, (j + 1) * size)
        keep[:, at] = whole[:, lane_block(half * frames + spot, size)]
        send[:, at] = whole[:, lane_block((1 - half) * frames + spot, size)]


def split_part(place, row, blocks):
    frames = len(blocks)
    _, tokens, width = blocks[0].shape
    shape = jax.ShapeDtypeStruct((tokens, frames * width // 2), BF16)
    return call(
        functools.partial(split_part_body, frames),
        [shape, shape],
        [place, row, *blocks],
        smem=2,
        scratch=[pltpu.VMEM((tokens, width * frames), BF16)],
    )


def exchange(blocks, sign):
    frames = len(blocks)
    result = [blocks[0]]
    for s in range(1, frames):
        pairs = [(i, (i + sign * s) % frames) for i in range(frames)]
        result.append(lax.ppermute(blocks[s], "frame", pairs))
    return result


def swap(x, bit):
    group = lax.axis_size("dp")
    return lax.ppermute(x, "dp", [(i, i ^ bit) for i in range(group)])


def gather_half(out_weight, count):
    weights = {0: out_weight}
    bit = count // 2
    while bit:
        for j in list(weights):
            weights[j ^ bit] = swap(weights[j], bit)
        bit //= 2
    return [weights[j] for j in range(count)]


def attend_body(counts, *refs):
    contexts = refs[: len(counts)]
    out = refs[-1]
    width = out.shape[1]
    tile = math.gcd(width, 768)
    for first in range(0, width, tile):
        columns = slice(first, first + tile)
        weights = list(refs[len(counts) : -1])
        total = None
        for context, pieces in zip(contexts, counts):
            start = 0
            for chunks in pieces:
                piece = both([weights.pop(0)[:, columns] for _ in range(chunks)])
                part = dot(context[:, start : start + piece.shape[0]], piece, NN)
                total = part if total is None else total + part
                start += piece.shape[0]
        out[:, columns] = total.astype(BF16)


def attend(contexts, weights):
    tokens, _ = contexts[0].shape
    flat = [c for pieces in weights for chunks in pieces for c in chunks]
    counts = [[len(chunks) for chunks in pieces] for pieces in weights]
    return call(
        functools.partial(attend_body, counts),
        [jax.ShapeDtypeStruct((tokens, flat[0].shape[1]), BF16)],
        [*contexts, *flat],
    )[0]


def local_split(queries, key_states, value_states, head_scale, out_weight, frame_pattern, out_grad):
    frames = lax.axis_size("frame")
    tokens, full = queries.shape[2:]
    model = out_grad.shape[3]
    heads = full // HDH
    place = lax.axis_index("frame").astype(jnp.int32).reshape(1)
    row = lax.axis_index("dp").astype(jnp.int32).reshape(1)

    grad_rows = out_grad[0, 0]
    other_rows = swap(grad_rows, frames)
    weights = gather_half(out_weight, frames)
    early, late = weights[: frames // 2], weights[frames // 2 :]
    cuts = [out_weight.shape[0] * n // 16 for n in (8, 5, 3)]

    states = [queries[0, 0], key_states[0, 0], value_states[0, 0]]
    wide = frames // 2
    others = [n for n in range(frames) if n != wide]
    sent = {wide: pack_one(place, row, states, frames, wide)}
    sent.update(zip(others, split_pack(place, row, states, frames, others)))
    blocks = exchange(sent, 1)

    mine, theirs, *chunks = context_grads(
        grad_rows, other_rows, early, [frame_pattern], cuts
    )
    other = swap(theirs, frames)
    crossed, far = [], []
    for i, chunk in enumerate(chunks):
        crossed.append(swap(chunk, frames))
        far.append(swap(crossed[i], frames // 2))
    sent = split_join(place, row, [mine], [other], frames)
    grads_early = exchange(sent, 1)
    mine, other = [], []
    for weight in late:
        own, theirs = context_grads(grad_rows, other_rows, [weight])
        mine.append(own)
        other.append(swap(theirs, frames))
    context = forward(place, row, head_scale, frame_pattern, blocks, True)
    context = exchange(context, -1)
    sent = split_join(place, row, mine, other, frames)
    grads_late = exchange(sent, 1)

    sent, scale_early = backward(
        place, row, head_scale, frame_pattern, blocks, grads_early, 0
    )
    done_early = exchange(sent, -1)
    sent, scale_part = backward(
        place, row, head_scale, frame_pattern, blocks, grads_late, 1, [scale_early]
    )
    done_late = exchange(sent, -1)

    contexts = split_part(place, row, context)
    others = {0: crossed, frames // 2: far}
    bit = frames // 4
    while bit:
        for j in list(others):
            others[j ^ bit] = [swap(c, bit) for c in others[j]]
        bit //= 2
    others = [others[j] for j in range(frames)]
    attended = attend(contexts, [[[w] for w in weights], others])

    bits = [frames // 2, frames]
    while bits[0] > 1 and bits[-1] != 1:
        bits.append(min(bits) // 2)
    for bit in bits:
        scale_part = scale_part + swap(scale_part, bit)
    scales = exchange([scale_part] * frames, 1)

    query_grad, key_grad, value_grad, scale_sum = split_unpack(
        place, row, done_early, done_late, scales, heads
    )
    shape = (1, 1, tokens, full)
    return (
        attended.reshape(1, 1, tokens, model),
        query_grad.reshape(shape),
        key_grad.reshape(shape),
        value_grad.reshape(shape),
        scale_sum[0, :heads],
    )


def local_plain(queries, key_states, value_states, head_scale, out_weight, frame_pattern, out_grad):
    frames = lax.axis_size("frame")
    group = lax.axis_size("dp")
    tokens, full = queries.shape[2:]
    model = out_grad.shape[3]
    heads = full // HDH
    count = group // 2
    size = out_weight.shape[0]
    place = lax.axis_index("frame").astype(jnp.int32).reshape(1)
    row = lax.axis_index("dp").astype(jnp.int32).reshape(1)

    grad_rows = out_grad[0, 0]
    other_rows = swap(grad_rows, count)
    weights = gather_half(out_weight, count)
    early, late = weights[: count // 2], weights[count // 2 :]
    names = (list(range(count // 2)), list(range(count // 2, count)))

    sent = pack(place, [queries[0, 0], key_states[0, 0], value_states[0, 0]], frames)
    blocks = exchange(sent, 1)
    context = exchange(forward(place, row, head_scale, frame_pattern, blocks), -1)
    mine, other = [], []
    for part_weights in (early, late):
        own, theirs = context_grads(grad_rows, other_rows, part_weights)
        mine.append(own)
        other.append(swap(theirs, count))
    sent = join(place, row, mine, other, names, size, frames, full)
    grads = exchange(sent, 1)

    keep, send = part(place, row, context, count, size)
    own, theirs = project_pair(keep, swap(send, count), weights)
    attended = (own + swap(theirs, count)).astype(BF16)

    sent, scale_part = backward(place, row, head_scale, frame_pattern, blocks, grads)
    blocks = exchange(sent, -1)
    bit = group // 2
    while bit:
        scale_part = scale_part + swap(scale_part, bit)
        bit //= 2
    scale_sum = functools.reduce(jnp.add, exchange([scale_part] * frames, 1))
    query_grad, key_grad, value_grad = unpack(place, blocks, frames)
    shape = (1, 1, tokens, full)
    return (
        attended.reshape(1, 1, tokens, model),
        query_grad.reshape(shape),
        key_grad.reshape(shape),
        value_grad.reshape(shape),
        scale_sum[0, :heads],
    )


def local(*args):
    frames = lax.axis_size("frame")
    size = args[4].shape[0]
    if lax.axis_size("dp") == 2 * frames and size % HDH == 0:
        return local_split(*args)
    return local_plain(*args)


def solution(mesh):
    spec = P("dp", "frame", None, None)
    return jax.shard_map(
        local,
        mesh=mesh,
        in_specs=(spec, spec, spec, P(), P("dp", None), P(), spec),
        out_specs=(spec, spec, spec, spec, P()),
        check_vma=False,
    )
```
